128 devices in a mesh: tm: 4 (over z_lo, core), rows: 32 (over y, z_hi, x).
Axes of the slice: x: 4, y: 4, z: 4 (z_hi: 2, z_lo: 2; z = z_hi * 2 + z_lo), core: 2. Of those that a mesh axis runs over, the one named last changes fastest.
Arguments:
- latent_feat: bfloat16 [16, 64, 128, 384], P('tm', 'rows'), may hold values from -6 to 6
- norm_gain: float32 [384], replicated, may hold values from 0.25 to 1.75
- conv_weight: bfloat16 [27, 384, 384], replicated, may hold values from -0.0625 to 0.0625
- rgb_weight: bfloat16 [384, 3], replicated, may hold values from -0.3125 to 0.3125
- real_frames: bfloat16 [3, 16, 64, 128], P(None, 'tm', 'rows'), may hold values from -6 to 6
- disc_first: bfloat16 [27, 64, 3], replicated, may hold values from -0.625 to 0.625
- disc_second: bfloat16 [27, 128, 64], replicated, may hold values from -0.15625 to 0.15625
Outputs:
- decoded: bfloat16 [16, 64, 128, 384], P('tm', 'rows')
- match_map: float32 [16, 64, 128], P('tm', 'rows')
The draws below stay inside these ranges and needn't reach their ends.
All inputs are finite; a program needn't handle non-finite values.
Results may differ from the reference program's by a relative error of at most 0.0033.
Values may be sent and summed in bfloat16 or wider, within the bound.
No kernel may reach another device: no remote copies, remote signals or barrier semaphores. Data moves between devices by JAX's collectives and lax.ppermute only.
A program may use at most 128 MiB of HBM per device.

```python
import jax
import jax.numpy as jnp
from jax import lax

C = 384
D1 = 64
D2 = 128
WC = 128
FR = 16
H = 64


def shard_levels(own_key, shape, cuts, least, largest):
    gain = 1.0
    for position, parts in cuts:
        heights = jax.random.uniform(jax.random.fold_in(jax.random.fold_in(own_key, 6), position), (parts,), jnp.float32, least / len(cuts), largest / len(cuts))
        gain = gain * jnp.repeat(jnp.exp(heights), shape[position] // parts).reshape((-1,) + (1,) * (len(shape) - 1 - position))
    return gain


def bell_draw(own_key, extent, spread, reach, cuts=(), kind=jnp.bfloat16):
    entries = spread * jax.random.normal(own_key, extent, jnp.float32)
    if cuts:
        entries = entries * shard_levels(own_key, extent, cuts, -0.22, 0.18)
    return jnp.clip(entries, -reach, reach).astype(kind)


def setup_inputs(seed: int = 0) -> dict:
    arg_keys = jax.random.split(jax.random.key(seed), 8)
    latent_feat = bell_draw(arg_keys[0], (FR, H, WC, C), 1.0, 6.0, ((0, 4), (1, 32)))
    norm_gain = jnp.clip(1.0 + 0.15 * jax.random.normal(arg_keys[1], (C,), jnp.float32), 0.25, 1.75)
    conv_weight = bell_draw(arg_keys[2], (27, C, C), (27 * C) ** -0.5, 0.0625)
    rgb_weight = bell_draw(arg_keys[3], (C, 3), C ** -0.5, 0.3125)
    real_frames = bell_draw(arg_keys[4], (3, FR, H, WC), 1.0, 6.0, ((1, 4), (2, 32)))
    disc_first = bell_draw(arg_keys[5], (27, D1, 3), 81 ** -0.5, 0.625)
    disc_second = bell_draw(arg_keys[6], (27, D2, D1), (27 * D1) ** -0.5, 0.15625)
    return {"latent_feat": latent_feat, "norm_gain": norm_gain, "conv_weight": conv_weight, "rgb_weight": rgb_weight, "real_frames": real_frames, "disc_first": disc_first, "disc_second": disc_second}


def leaky(value):
    return jnp.maximum(value, 0.2 * value)

def disc_layer(inputs, weights):
    padded = jnp.pad(inputs, ((0, 0), (1, 1), (1, 1), (1, 1)))
    frames, height, width = (inputs.shape[1], inputs.shape[2], inputs.shape[3])
    total = jnp.zeros((weights.shape[1], frames, height, width), jnp.float32)
    for tap in range(27):
        dt, dh, dw = (tap // 9, tap // 3 % 3, tap % 3)
        piece = padded[:, dt:dt + frames, dh:dh + height, dw:dw + width]
        total = total + jnp.einsum('oc,cthw->othw', weights[tap].astype(jnp.float32), piece.astype(jnp.float32))
    return leaky(total).astype(jnp.bfloat16)

def reference(latent_feat, norm_gain, conv_weight, rgb_weight, real_frames, disc_first, disc_second):
    feats = latent_feat.astype(jnp.float32)
    normed = feats * lax.rsqrt(lax.optimization_barrier(jnp.mean(feats * feats, axis=-1, keepdims=True)) + 1e-06) * norm_gain
    act = jax.nn.silu(normed).astype(jnp.bfloat16)
    frames, height, width, chans = act.shape
    padded = jnp.pad(act, ((2, 0), (1, 1), (1, 1), (0, 0)))
    total = jnp.zeros((frames * height * width, chans), jnp.float32)
    for tap in range(27):
        dt, dh, dw = (tap // 9, tap // 3 % 3, tap % 3)
        piece = padded[dt:dt + frames, dh:dh + height, dw:dw + width].reshape(-1, chans)
        total = total + jnp.dot(piece, conv_weight[tap], preferred_element_type=jnp.float32)
    decoded = (feats + total.reshape(frames, height, width, chans)).astype(jnp.bfloat16)
    colour = jnp.dot(decoded.reshape(-1, chans), rgb_weight, preferred_element_type=jnp.float32).astype(jnp.bfloat16)
    fake = jnp.transpose(colour.reshape(frames, height, width, 3), (3, 0, 1, 2))
    first_fake = disc_layer(fake, disc_first)
    first_real = disc_layer(real_frames, disc_first)
    second_fake = disc_layer(first_fake, disc_second)
    second_real = disc_layer(first_real, disc_second)
    match_map = lax.optimization_barrier(jnp.mean(jnp.abs(first_fake.astype(jnp.float32) - first_real.astype(jnp.float32)), axis=0))
    match_map = match_map + lax.optimization_barrier(jnp.mean(jnp.abs(second_fake.astype(jnp.float32) - second_real.astype(jnp.float32)), axis=0))
    return (decoded, match_map)
```

```python
import jax
import jax.numpy as jnp
from jax import lax
from jax.experimental import pallas as pl
from jax.experimental.pallas import tpu as pltpu
from jax.sharding import PartitionSpec as P

F32 = jnp.float32
BF16 = jnp.bfloat16
VMEM = pl.BlockSpec(memory_space=pltpu.VMEM)
SMEM = pl.BlockSpec(memory_space=pltpu.SMEM)


def pairs(count, first):
    route = []
    for i in range(first, count - 1, 2):
        route += [(i, i + 1), (i + 1, i)]
    return route


def swap(block, axis, first):
    return lax.ppermute(block, axis, pairs(lax.axis_size(axis), first))


def leaky(value):
    return jnp.maximum(value, 0.2 * value)


def act_kernel(pos_ref, feat_ref, gain_ref, to_a_ref, to_b_ref, tail_ref):
    odd = lax.rem(pos_ref[1], 2)
    gain = gain_ref[...]
    frames = feat_ref.shape[0]
    for row_sel, out_ref in ((1 - odd, to_a_ref), (odd, to_b_ref)):
        for t in range(frames):
            feats = feat_ref[t, row_sel].astype(F32)
            mean = jnp.mean(feats * feats, axis=-1, keepdims=True)
            normed = feats * lax.rsqrt(mean + 1e-06) * gain
            act = (normed * jax.nn.sigmoid(normed)).astype(BF16)
            out_ref[t] = act
            if t >= frames - 2:
                tail_ref[0 if out_ref is to_a_ref else 1, t - frames + 2] = act


def stack_frames(lines, frames, width):
    return [lines[dt : dt + frames].reshape(frames * width, lines.shape[-1]) for dt in range(3)]


def rhs_tile(w_ref, columns):
    halves = []
    for dhs, dw, off in columns:
        halves.append(
            jnp.concatenate(
                [w_ref[9 * dt + 3 * dh + dw, :, off : off + 128] for dh in dhs for dt in range(3)],
                axis=0,
            )
        )
    return halves[0] if len(halves) == 1 else jnp.concatenate(halves, axis=1)


def merge_columns(y0, y1, y2):
    width = y0.shape[0]
    col = lax.broadcasted_iota(jnp.int32, y0.shape, 0)
    left = jnp.where(col == 0, 0.0, pltpu.roll(y0, 1, 0))
    right = jnp.where(col == width - 1, 0.0, pltpu.roll(y2, width - 1, 0))
    return y1 + left + right


def own_kernel(pos_ref, a_ref, b_ref, past_ref, w_ref, part_ref, lines_ref, y_ref):
    odd = lax.rem(pos_ref[1], 2)
    frames, width, chans = a_ref.shape
    for row, own_ref, k in ((1 - odd, a_ref, 0), (odd, b_ref, 1)):
        lines_ref[row, pl.ds(0, 2)] = past_ref[k]
        lines_ref[row, pl.ds(2, frames)] = own_ref[...]
    lhs = jnp.concatenate(
        stack_frames(lines_ref[0], frames, width) + stack_frames(lines_ref[1], frames, width), axis=1
    )
    columns = [
        (dhs, dw, off)
        for dhs in ((1, 2), (0, 1))
        for dw in range(3)
        for off in range(0, chans, 128)
    ]
    for j in range(0, len(columns), 2):
        y_ref[:, j * 128 : (j + 2) * 128] = jnp.dot(
            lhs, rhs_tile(w_ref, columns[j : j + 2]), preferred_element_type=F32
        )
    for row in range(2):
        for t in range(frames):
            ys = [
                y_ref[t * width : (t + 1) * width, (row * 3 + dw) * chans : (row * 3 + dw + 1) * chans]
                for dw in range(3)
            ]
            part_ref[t, row] = merge_columns(*ys)


def halo_kernel(
    pos_ref, a_ref, b_ref, past_a_ref, past_b_ref, w_ref, part_ref, feat_ref, rgb_ref, real_ref,
    decoded_ref, colour_ref, lines_ref, y_ref,
):
    odd = lax.rem(pos_ref[1], 2)
    frames, width, chans = a_ref.shape
    for side, own_ref, past in ((1 - odd, a_ref, past_a_ref), (odd, b_ref, past_b_ref)):
        lines_ref[side, pl.ds(0, 2)] = past[...]
        lines_ref[side, pl.ds(2, frames)] = own_ref[...]
    for row in range(2):
        lhs = jnp.concatenate(stack_frames(lines_ref[row], frames, width), axis=1)
        columns = [((2 * row,), dw, off) for dw in range(3) for off in range(0, chans, 128)]
        for j in range(0, len(columns), 2):
            some = columns[j : j + 2]
            y_ref[row, :, j * 128 : (j + len(some)) * 128] = jnp.dot(
                lhs, rhs_tile(w_ref, some), preferred_element_type=F32
            )
        for t in range(frames):
            ys = [
                y_ref[row, t * width : (t + 1) * width, dw * chans : (dw + 1) * chans]
                for dw in range(3)
            ]
            total = merge_columns(*ys) + part_ref[t, row]
            decoded = (feat_ref[t, row].astype(F32) + total).astype(BF16)
            decoded_ref[t, row] = decoded
            colour = lax.dot_general(
                rgb_ref[...], decoded, (((1,), (1,)), ((), ())), preferred_element_type=F32
            )
            colour_ref[t, row] = (
                colour.astype(BF16).astype(F32) + real_ref[t, row].astype(F32)
            ).astype(BF16)


def disc_kernel(
    pos_ref, mid_ref, ta_ref, tb_ref, w1_ref, w2_ref, out_ref, x_ref, f_ref, *, tm_count, row_count
):
    tm, band = pos_ref[0], pos_ref[1]
    odd_t, odd_r = lax.rem(tm, 2), lax.rem(band, 2)
    width = out_ref.shape[-1]
    frames = out_ref.shape[0]
    col = lax.broadcasted_iota(jnp.int32, (8, width), 1)

    def put(t, h, line):
        x = line.astype(F32)
        x_ref[t, h, 0:8] = jnp.where(col == 0, 0.0, pltpu.roll(x, 1, 1))
        x_ref[t, h, 8:16] = x
        x_ref[t, h, 16:24] = jnp.where(col == width - 1, 0.0, pltpu.roll(x, width - 1, 1))

    row_at = [4 * (1 - odd_r), 4 * (1 - odd_r) + 1, 2, 3, 4 * odd_r, 4 * odd_r + 1]
    a_at = (frames + 2) * (1 - odd_t)
    b_at = (frames + 2) * odd_t
    for k in range(6):
        for t in range(frames):
            put(t + 2, row_at[k], mid_ref[t, k])
        for t in range(2):
            put(a_at + t, row_at[k], ta_ref[t, k])
            put(b_at + t, row_at[k], tb_ref[t, k])

    w1 = w1_ref[...]
    near = {}
    for t in range(frames + 2):
        for h in range(0, 4, 2):
            cols = []
            for hh in (h, h + 1):
                cols.append(
                    jnp.concatenate(
                        [x_ref[t + dt, hh + dh] for dt in range(3) for dh in range(3)], axis=0
                    ).astype(BF16)
                )
            first = leaky(jnp.dot(w1, jnp.concatenate(cols, axis=1), preferred_element_type=F32))
            for i, hh in enumerate((h, h + 1)):
                part = first[:, i * width : (i + 1) * width]
                keep = None
                if t == 0:
                    keep = tm > 0
                if t == frames + 1:
                    keep = tm < tm_count - 1
                edge = None
                if hh == 0:
                    edge = band > 0
                if hh == 3:
                    edge = band < row_count - 1
                if keep is not None and edge is not None:
                    keep = jnp.logical_and(keep, edge)
                elif keep is None:
                    keep = edge
                if keep is not None:
                    part = jnp.where(keep, part, 0.0)
                part = part.astype(BF16)
                f_ref[t, hh] = part
                if 1 <= t <= frames and 1 <= hh <= 2:
                    wide = part.astype(F32)
                    half = wide.shape[0] // 2
                    near[t - 1, hh - 1] = jnp.mean(
                        jnp.abs(wide[:half] - wide[half:]), axis=0, keepdims=True
                    )

    w2 = w2_ref[...]
    depth2 = w2.shape[0] // 3
    half = f_ref.shape[2] // 2
    colw = lax.broadcasted_iota(jnp.int32, (depth2, width), 1)
    for t in range(frames):
        for h in range(2):
            sides = []
            for s in range(2):
                sides.append(
                    jnp.concatenate(
                        [
                            f_ref[t + dt, h + dh, s * half : (s + 1) * half]
                            for dt in range(3)
                            for dh in range(3)
                        ],
                        axis=0,
                    )
                )
            y = jnp.dot(w2, jnp.concatenate(sides, axis=1), preferred_element_type=F32)
            outs = []
            for s in range(2):
                y0, y1, y2 = (
                    y[d * depth2 : (d + 1) * depth2, s * width : (s + 1) * width] for d in range(3)
                )
                total = (
                    y1
                    + jnp.where(colw == 0, 0.0, pltpu.roll(y0, 1, 1))
                    + jnp.where(colw == width - 1, 0.0, pltpu.roll(y2, width - 1, 1))
                )
                outs.append(leaky(total).astype(BF16).astype(F32))
            far = jnp.mean(jnp.abs(outs[0] - outs[1]), axis=0, keepdims=True)
            out_ref[t, h : h + 1] = near[t, h] + far


def shape(dims, dtype):
    return jax.ShapeDtypeStruct(dims, dtype)


def per_device(
    latent_feat, norm_gain, conv_weight, rgb_weight, real_frames, disc_first, disc_second
):
    frames, height, width, chans = latent_feat.shape
    pos = jnp.stack([lax.axis_index("tm"), lax.axis_index("rows")]).astype(jnp.int32)
    depth1, depth2 = disc_first.shape[1], disc_second.shape[1]

    rgb = jnp.pad(rgb_weight.T, ((0, 5), (0, 0)))
    real = jnp.pad(jnp.transpose(real_frames, (1, 2, 0, 3)), ((0, 0), (0, 0), (3, 2), (0, 0)))
    w1 = jnp.transpose(disc_first, (1, 0, 2))
    w1 = jnp.concatenate(
        [jnp.pad(w1, ((0, 0), (0, 0), (0, 5))), jnp.pad(w1, ((0, 0), (0, 0), (3, 2)))], axis=0
    ).reshape(2 * depth1, 27 * 8)
    w2 = disc_second.reshape(9, 3, depth2, depth1)
    w2 = jnp.transpose(w2, (1, 2, 0, 3)).reshape(3 * depth2, 9 * depth1)

    to_a, to_b, tail = pl.pallas_call(
        act_kernel,
        out_shape=(
            shape((frames, width, chans), BF16),
            shape((frames, width, chans), BF16),
            shape((2, 2, width, chans), BF16),
        ),
        in_specs=[SMEM, VMEM, VMEM],
        out_specs=(VMEM,) * 3,
        name="act",
    )(pos, latent_feat, norm_gain.reshape(1, chans))

    from_b = swap(to_b, "rows", 1)
    from_a = swap(to_a, "rows", 0)
    count = lax.axis_size("tm")
    past = lax.ppermute(tail, "tm", [(i, i + 1) for i in range(count - 1)])
    past_b = swap(past[1], "rows", 1)
    past_a = swap(past[0], "rows", 0)

    flops = 2 * frames * width * 9 * chans * chans
    part = pl.pallas_call(
        own_kernel,
        out_shape=shape((frames, height, width, chans), F32),
        in_specs=[SMEM] + [VMEM] * 4,
        out_specs=VMEM,
        scratch_shapes=[
            pltpu.VMEM((2, frames + 2, width, chans), BF16),
            pltpu.VMEM((frames * width, 6 * chans), F32),
        ],
        cost_estimate=pl.CostEstimate(flops=4 * flops, bytes_accessed=10**7, transcendentals=0),
        name="own",
    )(pos, to_a, to_b, past, conv_weight)

    decoded, colour = pl.pallas_call(
        halo_kernel,
        out_shape=(
            shape((frames, height, width, chans), BF16),
            shape((frames, height, 8, width), BF16),
        ),
        in_specs=[SMEM] + [VMEM] * 9,
        out_specs=(VMEM,) * 2,
        scratch_shapes=[
            pltpu.VMEM((2, frames + 2, width, chans), BF16),
            pltpu.VMEM((2, frames * width, 3 * chans), F32),
        ],
        cost_estimate=pl.CostEstimate(flops=2 * flops, bytes_accessed=10**7, transcendentals=0),
        name="halo",
    )(pos, from_a, from_b, past_a, past_b, conv_weight, part, latent_feat, rgb, real)

    side_b = swap(colour, "rows", 1)
    side_a = swap(colour, "rows", 0)
    mid = jnp.concatenate([side_a, colour, side_b], axis=1)
    odd_t = lax.rem(pos[0], 2)
    for_a = lax.dynamic_slice_in_dim(mid, (frames - 2) * (1 - odd_t), 2, axis=0)
    for_b = lax.dynamic_slice_in_dim(mid, (frames - 2) * odd_t, 2, axis=0)
    time_b = swap(for_b, "tm", 1)
    time_a = swap(for_a, "tm", 0)

    match_map = pl.pallas_call(
        lambda *refs: disc_kernel(
            *refs, tm_count=lax.axis_size("tm"), row_count=lax.axis_size("rows")
        ),
        out_shape=shape((frames, height, width), F32),
        in_specs=[SMEM] + [VMEM] * 5,
        out_specs=VMEM,
        scratch_shapes=[
            pltpu.VMEM((frames + 4, height + 4, 24, width), F32),
            pltpu.VMEM((frames + 2, height + 2, 2 * depth1, width), BF16),
        ],
        name="disc",
    )(pos, mid, time_a, time_b, w1, w2)
    return (decoded, match_map)


def solution(mesh):
    placed = (P("tm", "rows", None, None), P(), P(), P(), P(None, "tm", "rows", None), P(), P())
    return jax.shard_map(
        per_device,
        mesh=mesh,
        in_specs=placed,
        out_specs=(P("tm", "rows", None, None), P("tm", "rows", None)),
        check_vma=False,
    )
```

```python
import jax
import jax.numpy as jnp
from jax import lax
from jax.experimental import pallas as pl
from jax.experimental.pallas import tpu as pltpu
from jax.sharding import PartitionSpec as P


F32 = jnp.float32
BF16 = jnp.bfloat16
VMEM = pl.BlockSpec(memory_space=pltpu.VMEM)
HBM = pl.BlockSpec(memory_space=pltpu.HBM)
NT = (((1,), (1,)), ((), ()))


def pairs(count, first):
    route = []
    for i in range(first, count - 1, 2):
        route += [(i, i + 1), (i + 1, i)]
    return route


def swap(block, axis, first):
    return lax.ppermute(block, axis, pairs(lax.axis_size(axis), first))


def onward(block, axis):
    return lax.ppermute(block, axis, [(i, i + 1) for i in range(lax.axis_size(axis) - 1)])


def local(kernel, outs, args, scratch=(), aliases=None, flops=0, hbm=(), limit=24):
    args = [
        pltpu.with_memory_space_constraint(a, pltpu.HBM if i in hbm else pltpu.VMEM)
        for i, a in enumerate(args)
    ]
    return pl.pallas_call(
        kernel,
        out_shape=outs,
        in_specs=[HBM if i in hbm else VMEM for i in range(len(args))],
        out_specs=jax.tree.map(lambda _: VMEM, outs),
        scratch_shapes=scratch,
        input_output_aliases=aliases or {},
        compiler_params=pltpu.CompilerParams(vmem_limit_bytes=limit << 20),
        cost_estimate=pl.CostEstimate(flops=flops, bytes_accessed=10**6, transcendentals=0),
    )(*args)


def kept(*dims, dtype=BF16):
    return pltpu.VMEM(dims, dtype)


def leaky(value):
    return jnp.maximum(value, 0.2 * value)


def act_kernel(feat_ref, gain_ref, to_a_ref, to_b_ref, tail_ref):
    odd = lax.rem(lax.axis_index("rows"), 2)
    gain = gain_ref[...]
    frames = feat_ref.shape[0]
    for k, (row, out_ref) in enumerate(((odd, to_b_ref), (1 - odd, to_a_ref))):
        for t in range(frames):
            feats = feat_ref[t, row].astype(F32)
            mean = jnp.mean(feats * feats, axis=-1, keepdims=True)
            normed = feats * lax.rsqrt(mean + 1e-06) * gain
            act = (normed * jax.nn.sigmoid(normed)).astype(BF16)
            out_ref[t] = act
            if t >= frames - 2:
                tail_ref[1 - k, t - frames + 2] = act


def column_blocks(rows, chans):
    return [(o, dw, off) for o in rows for dw in range(3) for off in range(0, chans, 128)]


def rhs_tile(w_ref, blocks, inputs):
    halves = [
        jnp.concatenate(
            [w_ref[9 * dt + 3 * (i - o + 1) + dw, :, off : off + 128] for dt, i in inputs], axis=0
        )
        for o, dw, off in blocks
    ]
    return halves[0] if len(halves) == 1 else jnp.concatenate(halves, axis=1)


def tiles(blocks):
    return [(j, blocks[j : j + 2]) for j in range(0, len(blocks), 2)]


def own_kernel(
    a_ref, b_ref, weight_ref, d2_ref, d1_ref, y_ref, w2_ref, w1_ref, w_ref, lines_ref, sems
):
    odd = lax.rem(lax.axis_index("rows"), 2)
    frames, width, chans = a_ref.shape
    order = [9 * dt + k for dt in (2, 1, 0) for k in range(9)]
    loads = {
        tap: pltpu.make_async_copy(weight_ref.at[tap], w_ref.at[tap], sems.at[tap]) for tap in order
    }
    for tap in order:
        loads[tap].start()
    lines_ref[1 - odd] = a_ref[...]
    lines_ref[odd] = b_ref[...]
    lhs = jnp.concatenate(
        [lines_ref[i].reshape(frames * width, chans) for i in range(2)], axis=1
    )
    for dt in (2, 1, 0):
        for tap in range(9 * dt, 9 * dt + 9):
            loads[tap].wait()
        used = frames - 2 + dt
        for j, some in tiles(column_blocks((0, 1), chans)):
            cols = slice(j * 128, (j + len(some)) * 128)
            got = jnp.dot(
                lhs[: used * width],
                rhs_tile(w_ref, some, [(dt, 0), (dt, 1)]),
                preferred_element_type=F32,
            )
            if dt == 2:
                y_ref[:, cols] = got
            else:
                y_ref[(frames - used) * width :, cols] += got
    depth2, depth1 = d2_ref.shape[2], d2_ref.shape[1]
    for tap in range(27):
        dw, rest = tap % 3, tap // 3
        if rest % 2 == 0:
            parts = [d2_ref[tap].astype(F32)]
            if rest < 8:
                parts.append(d2_ref[tap + 3].astype(F32))
            wide = jnp.concatenate(parts, axis=0)
            w2_ref[dw * depth2 : (dw + 1) * depth2, rest * depth1 : rest * depth1 + wide.shape[0]] = (
                wide.T.astype(BF16)
            )
    w1_ref[...] = d1_ref[...].astype(F32).T.astype(BF16)


def past_lhs(lines, zeros):
    first = [line[0] for line in lines] + [line[1] for line in lines]
    second = [line[1] for line in lines] + [zeros for _ in lines]
    return jnp.concatenate(
        [jnp.concatenate(first, axis=1), jnp.concatenate(second, axis=1)], axis=0
    )


def past_kernel(past_ref, w_ref, sum_ref, y_ref, lines_ref):
    odd = lax.rem(lax.axis_index("rows"), 2)
    width, chans = past_ref.shape[2:]
    lines_ref[1 - odd] = past_ref[0]
    lines_ref[odd] = past_ref[1]
    zeros = jnp.zeros((width, chans), BF16)
    lhs = past_lhs([lines_ref[i] for i in range(2)], zeros)
    inputs = [(dt, i) for dt in range(2) for i in range(2)]
    for j, some in tiles(column_blocks((0, 1), chans)):
        y_ref[: 2 * width, j * 128 : (j + len(some)) * 128] += jnp.dot(
            lhs, rhs_tile(w_ref, some, inputs), preferred_element_type=F32
        )


def rows_kernel(a_ref, b_ref, w_ref, sum_ref, y_ref, lines_ref):
    odd = lax.rem(lax.axis_index("rows"), 2)
    frames, width, chans = a_ref.shape
    lines_ref[1 - odd] = a_ref[...]
    lines_ref[odd] = b_ref[...]
    zeros = jnp.zeros((width, chans), BF16)
    for o in range(2):
        line = [zeros, zeros] + [lines_ref[o, t] for t in range(frames)]
        lhs = jnp.concatenate(
            [jnp.concatenate(line[dt : dt + frames], axis=0) for dt in range(3)], axis=1
        )
        inputs = [(dt, 3 * o - 1) for dt in range(3)]
        base = o * 3 * chans
        for j, some in tiles(column_blocks((o,), chans)):
            y_ref[:, base + j * 128 : base + (j + len(some)) * 128] += jnp.dot(
                lhs, rhs_tile(w_ref, some, inputs), preferred_element_type=F32
            )


def corner_kernel(
    past_ref, w_ref, sum_ref, feat_ref, rgb_ref, real_ref, decoded_ref, colour_ref, y_ref, lines_ref
):
    odd = lax.rem(lax.axis_index("rows"), 2)
    width, chans = past_ref.shape[2:]
    frames = feat_ref.shape[0]
    lines_ref[1 - odd] = past_ref[0]
    lines_ref[odd] = past_ref[1]
    zeros = jnp.zeros((width, chans), BF16)
    col = lax.broadcasted_iota(jnp.int32, (width, chans), 0)
    for o in range(2):
        lhs = past_lhs([lines_ref[o]], zeros)
        inputs = [(dt, 3 * o - 1) for dt in range(2)]
        for j, some in tiles(column_blocks((o,), chans)):
            y_ref[o, :, j * 128 : (j + len(some)) * 128] = jnp.dot(
                lhs, rhs_tile(w_ref, some, inputs), preferred_element_type=F32
            )
    for t in reversed(range(frames)):
        for o in range(2):
            ys = []
            for dw in range(3):
                at = (o * 3 + dw) * chans
                y = sum_ref[t * width : (t + 1) * width, at : at + chans]
                if t < 2:
                    y = y + y_ref[o, t * width : (t + 1) * width, dw * chans : (dw + 1) * chans]
                ys.append(y)
            total = (
                ys[1]
                + jnp.where(col == 0, 0.0, pltpu.roll(ys[0], 1, 0))
                + jnp.where(col == width - 1, 0.0, pltpu.roll(ys[2], width - 1, 0))
            )
            decoded = (feat_ref[t, o].astype(F32) + total).astype(BF16)
            decoded_ref[t, o] = decoded
            colour = lax.dot_general(rgb_ref[...], decoded, NT, preferred_element_type=F32)
            real = [real_ref[c, t, o : o + 1].astype(F32) for c in range(3)]
            colour_ref[t, o] = jnp.concatenate(
                [colour.astype(BF16).astype(F32)] + real + [jnp.zeros((2, width), F32)], axis=0
            ).astype(BF16)


def pack_kernel(a_ref, own_ref, b_ref, for_a_ref, for_b_ref):
    odd = lax.rem(lax.axis_index("tm"), 2)
    frames = own_ref.shape[0]
    for start, out_ref in (((frames - 2) * (1 - odd), for_a_ref), ((frames - 2) * odd, for_b_ref)):
        for k, ref in enumerate((a_ref, own_ref, b_ref)):
            out_ref[:, 2 * k : 2 * k + 2] = ref[pl.ds(start, 2)]


def disc_kernel(a_ref, own_ref, b_ref, ta_ref, tb_ref, w1_ref, w2_ref, out_ref, x_ref, f_ref):
    tm, band = lax.axis_index("tm"), lax.axis_index("rows")
    tm_count, row_count = lax.axis_size("tm"), lax.axis_size("rows")
    odd_t, odd_r = lax.rem(tm, 2), lax.rem(band, 2)
    width = out_ref.shape[-1]
    frames = out_ref.shape[0]
    col = lax.broadcasted_iota(jnp.int32, (8, width), 1)

    def put(t, h, line):
        x = line.astype(F32)
        x_ref[t, h, 0:8] = jnp.where(col == 0, 0.0, pltpu.roll(x, 1, 1))
        x_ref[t, h, 8:16] = x
        x_ref[t, h, 16:24] = jnp.where(col == width - 1, 0.0, pltpu.roll(x, width - 1, 1))

    row_at = [4 * (1 - odd_r), 4 * (1 - odd_r) + 1, 2, 3, 4 * odd_r, 4 * odd_r + 1]
    a_at = (frames + 2) * (1 - odd_t)
    b_at = (frames + 2) * odd_t
    for k in range(6):
        for t in range(frames):
            put(t + 2, row_at[k], (a_ref, own_ref, b_ref)[k // 2][t, k % 2])
        for t in range(2):
            put(a_at + t, row_at[k], ta_ref[t, k])
            put(b_at + t, row_at[k], tb_ref[t, k])

    w1 = w1_ref[...]
    near = {}
    for t in range(frames + 2):
        for h in range(0, 4, 2):
            cols = []
            for hh in (h, h + 1):
                cols.append(
                    jnp.concatenate(
                        [x_ref[t + dt, hh + dh] for dt in range(3) for dh in range(3)], axis=0
                    ).astype(BF16)
                )
            first = leaky(jnp.dot(w1, jnp.concatenate(cols, axis=1), preferred_element_type=F32))
            for i, hh in enumerate((h, h + 1)):
                part = first[:, i * width : (i + 1) * width]
                inside = []
                if t == 0:
                    inside.append(tm > 0)
                if t == frames + 1:
                    inside.append(tm < tm_count - 1)
                if hh == 0:
                    inside.append(band > 0)
                if hh == 3:
                    inside.append(band < row_count - 1)
                if inside:
                    keep = inside[0] if len(inside) == 1 else jnp.logical_and(*inside)
                    part = jnp.where(keep, part, 0.0)
                part = part.astype(BF16)
                f_ref[t, hh] = part
                if 1 <= t <= frames and 1 <= hh <= 2:
                    wide = part.astype(F32)
                    half = wide.shape[0] // 2
                    near[t - 1, hh - 1] = jnp.mean(
                        jnp.abs(wide[:half] - wide[half:]), axis=0, keepdims=True
                    )

    w2 = w2_ref[...]
    depth2 = w2.shape[0] // 3
    half = f_ref.shape[2] // 2
    colw = lax.broadcasted_iota(jnp.int32, (depth2, width), 1)
    for t in range(frames):
        for h in range(2):
            sides = []
            for s in range(2):
                sides.append(
                    jnp.concatenate(
                        [
                            f_ref[t + dt, h + dh, s * half : (s + 1) * half]
                            for dt in range(3)
                            for dh in range(3)
                        ],
                        axis=0,
                    )
                )
            y = jnp.dot(w2, jnp.concatenate(sides, axis=1), preferred_element_type=F32)
            outs = []
            for s in range(2):
                y0, y1, y2 = (
                    y[d * depth2 : (d + 1) * depth2, s * width : (s + 1) * width] for d in range(3)
                )
                total = (
                    y1
                    + jnp.where(colw == 0, 0.0, pltpu.roll(y0, 1, 1))
                    + jnp.where(colw == width - 1, 0.0, pltpu.roll(y2, width - 1, 1))
                )
                outs.append(leaky(total).astype(BF16).astype(F32))
            far = jnp.mean(jnp.abs(outs[0] - outs[1]), axis=0, keepdims=True)
            out_ref[t, h : h + 1] = near[t, h] + far


def per_device(
    latent_feat, norm_gain, conv_weight, rgb_weight, real_frames, disc_first, disc_second
):
    frames, height, width, chans = latent_feat.shape
    depth1, depth2 = disc_first.shape[1], disc_second.shape[1]
    cells = frames * width

    d1 = jnp.transpose(disc_first, (0, 2, 1))
    d1 = (
        jnp.pad(d1, ((0, 0), (0, 5), (0, depth1))) + jnp.pad(d1, ((0, 0), (3, 2), (depth1, 0)))
    ).reshape(27 * 8, 2 * depth1)
    d2 = jnp.transpose(disc_second, (0, 2, 1))

    to_a, to_b, tail = local(
        act_kernel,
        (kept(frames, width, chans), kept(frames, width, chans), kept(2, 2, width, chans)),
        (latent_feat, norm_gain),
    )
    from_b = swap(to_b, "rows", 1)
    from_a = swap(to_a, "rows", 0)
    past = onward(tail, "tm")

    line = 2 * width * chans * chans
    sums = kept(cells, 6 * chans, dtype=F32)
    y, w2, w1, weight = local(
        own_kernel,
        (sums, kept(3 * depth2, 9 * depth1), kept(2 * depth1, 27 * 8), kept(*conv_weight.shape)),
        (to_a, to_b, conv_weight, d2, d1),
        hbm=(2,),
        scratch=[pltpu.VMEM((2, frames, width, chans), BF16), pltpu.SemaphoreType.DMA((27,))],
        flops=36 * 3 * line,
    )
    y = local(
        past_kernel,
        sums,
        (past, weight, y),
        scratch=[pltpu.VMEM((2, 2, width, chans), BF16)],
        aliases={2: 0},
        flops=12 * 3 * line,
    )
    corner = onward(jnp.stack([from_a[frames - 2 :], from_b[frames - 2 :]]), "tm")
    y = local(
        rows_kernel,
        sums,
        (from_a, from_b, weight, y),
        scratch=[pltpu.VMEM((2, frames, width, chans), BF16)],
        aliases={3: 0},
        flops=18 * 3 * line,
    )
    decoded, colour = local(
        corner_kernel,
        (jax.ShapeDtypeStruct((frames, height, width, chans), BF16), kept(frames, height, 8, width)),
        (corner, weight, y, latent_feat, rgb_weight.T, real_frames),
        scratch=[
            pltpu.VMEM((2, 2 * width, 3 * chans), F32),
            pltpu.VMEM((2, 2, width, chans), BF16),
        ],
        flops=6 * 3 * line,
    )

    side_b = swap(colour, "rows", 1)
    side_a = swap(colour, "rows", 0)
    ends = kept(2, height + 4, 8, width)
    for_a, for_b = local(pack_kernel, (ends, ends), (side_a, colour, side_b))
    time_b = swap(for_b, "tm", 1)
    time_a = swap(for_a, "tm", 0)

    match_map = local(
        disc_kernel,
        jax.ShapeDtypeStruct((frames, height, width), F32),
        (side_a, colour, side_b, time_a, time_b, w1, w2),
        scratch=[
            pltpu.VMEM((frames + 4, height + 4, 24, width), F32),
            pltpu.VMEM((frames + 2, height + 2, 2 * depth1, width), BF16),
        ],
    )
    return (decoded, match_map)


def solution(mesh):
    placed = (P("tm", "rows", None, None), P(), P(), P(), P(None, "tm", "rows", None), P(), P())
    return jax.shard_map(
        per_device,
        mesh=mesh,
        in_specs=placed,
        out_specs=(P("tm", "rows", None, None), P("tm", "rows", None)),
        check_vma=False,
    )
```

```python
import jax
import jax.numpy as jnp
from jax import lax
from jax.experimental import pallas as pl
from jax.experimental.pallas import tpu as pltpu
from jax.sharding import PartitionSpec as P


F32 = jnp.float32
BF16 = jnp.bfloat16
VMEM = pl.BlockSpec(memory_space=pltpu.VMEM)
HBM = pl.BlockSpec(memory_space=pltpu.HBM)
NT = (((1,), (1,)), ((), ()))


def pairs(count, first):
    route = []
    for i in range(first, count - 1, 2):
        route += [(i, i + 1), (i + 1, i)]
    return route


def swap(block, axis, first):
    return lax.ppermute(block, axis, pairs(lax.axis_size(axis), first))


def onward(block, axis):
    return lax.ppermute(block, axis, [(i, i + 1) for i in range(lax.axis_size(axis) - 1)])


def local(kernel, outs, args, scratch=(), aliases=None, flops=0, hbm=(), limit=24):
    args = [
        pltpu.with_memory_space_constraint(a, pltpu.HBM if i in hbm else pltpu.VMEM)
        for i, a in enumerate(args)
    ]
    return pl.pallas_call(
        kernel,
        out_shape=outs,
        in_specs=[HBM if i in hbm else VMEM for i in range(len(args))],
        out_specs=jax.tree.map(lambda _: VMEM, outs),
        scratch_shapes=scratch,
        input_output_aliases=aliases or {},
        compiler_params=pltpu.CompilerParams(vmem_limit_bytes=limit << 20),
        cost_estimate=pl.CostEstimate(flops=flops, bytes_accessed=10**6, transcendentals=0),
    )(*args)


def kept(*dims, dtype=BF16):
    return pltpu.VMEM(dims, dtype)


def leaky(value):
    return jnp.maximum(value, 0.2 * value)


def act_kernel(feat_ref, gain_ref, to_a_ref, to_b_ref, tail_ref, feats_ref, scale_ref, sems):
    odd = lax.rem(lax.axis_index("rows"), 2)
    frames = feat_ref.shape[0]
    order = [frames - 2, frames - 1] + list(range(frames - 2))
    fetch_gain = pltpu.make_async_copy(gain_ref, scale_ref, sems.at[frames])
    fetch = [pltpu.make_async_copy(feat_ref.at[t], feats_ref.at[t], sems.at[t]) for t in range(frames)]
    fetch_gain.start()
    for t in order:
        fetch[t].start()
    fetch_gain.wait()
    gain = scale_ref[...]
    for t in order:
        fetch[t].wait()
        for k, (row, out_ref) in enumerate(((1 - odd, to_a_ref), (odd, to_b_ref))):
            feats = feats_ref[t, row].astype(F32)
            mean = jnp.mean(feats * feats, axis=-1, keepdims=True)
            normed = feats * lax.rsqrt(mean + 1e-06) * gain
            act = (normed * jax.nn.sigmoid(normed)).astype(BF16)
            out_ref[t] = act
            if t >= frames - 2:
                tail_ref[k, t - frames + 2] = act


def column_blocks(rows, chans):
    return [(o, dw, off) for o in rows for dw in range(3) for off in range(0, chans, 128)]


def rhs_tile(w_ref, blocks, inputs):
    halves = [
        jnp.concatenate(
            [w_ref[9 * dt + 3 * (i - o + 1) + dw, :, off : off + 128] for dt, i in inputs], axis=0
        )
        for o, dw, off in blocks
    ]
    return halves[0] if len(halves) == 1 else jnp.concatenate(halves, axis=1)


def tiles(blocks):
    return [(j, blocks[j : j + 2]) for j in range(0, len(blocks), 2)]


def own_kernel(a_ref, b_ref, past_ref, weight_ref, y_ref, w_ref, lines_ref, sems):
    odd = lax.rem(lax.axis_index("rows"), 2)
    frames, width, chans = a_ref.shape
    order = [9 * dt + k for dt in (2, 1, 0) for k in range(9)]
    loads = {
        tap: pltpu.make_async_copy(weight_ref.at[tap], w_ref.at[tap], sems.at[tap]) for tap in order
    }
    for tap in order:
        loads[tap].start()
    for k, (row, line_ref) in enumerate(((1 - odd, a_ref), (odd, b_ref))):
        lines_ref[row, pl.ds(0, 2)] = past_ref[k]
        lines_ref[row, pl.ds(2, frames)] = line_ref[...]
    for dt in (2, 1, 0):
        for tap in range(9 * dt, 9 * dt + 9):
            loads[tap].wait()
        lhs = jnp.concatenate(
            [lines_ref[i, dt : dt + frames].reshape(frames * width, chans) for i in range(2)], axis=1
        )
        for j, some in tiles(column_blocks((0, 1), chans)):
            cols = slice(j * 128, (j + len(some)) * 128)
            got = jnp.dot(
                lhs, rhs_tile(w_ref, some, [(dt, 0), (dt, 1)]), preferred_element_type=F32
            )
            if dt == 2:
                y_ref[:, cols] = got
            else:
                y_ref[:, cols] += got


def prep_kernel(d2_ref, d1_ref, w2_ref, w1_ref):
    depth1, depth2 = d2_ref.shape[1:]
    for tap in range(27):
        dw, rest = tap % 3, tap // 3
        if rest % 2 == 0:
            parts = [d2_ref[tap].astype(F32)]
            if rest < 8:
                parts.append(d2_ref[tap + 3].astype(F32))
            wide = jnp.concatenate(parts, axis=0)
            w2_ref[dw * depth2 : (dw + 1) * depth2, rest * depth1 : rest * depth1 + wide.shape[0]] = (
                wide.T.astype(BF16)
            )
    tap = lax.broadcasted_iota(jnp.int32, (27, 27 * 8), 0)
    place = lax.broadcasted_iota(jnp.int32, (27, 27 * 8), 1)
    for side in range(2):
        total = jnp.zeros((depth1, 27 * 8), F32)
        for c in range(3):
            pick = jnp.where(place == 8 * tap + 3 * side + c, 1.0, 0.0).astype(BF16)
            total = total + lax.dot_general(
                d1_ref[c], pick, (((0,), (0,)), ((), ())), preferred_element_type=F32
            )
        w1_ref[side * depth1 : (side + 1) * depth1] = total.astype(BF16)


def past_lhs(lines, zeros):
    first = [line[0] for line in lines] + [line[1] for line in lines]
    second = [line[1] for line in lines] + [zeros for _ in lines]
    return jnp.concatenate(
        [jnp.concatenate(first, axis=1), jnp.concatenate(second, axis=1)], axis=0
    )


def finish(ys, feats, rgb, reals):
    width, chans = ys[1].shape
    col = lax.broadcasted_iota(jnp.int32, (width, chans), 0)
    total = (
        ys[1]
        + jnp.where(col == 0, 0.0, pltpu.roll(ys[0], 1, 0))
        + jnp.where(col == width - 1, 0.0, pltpu.roll(ys[2], width - 1, 0))
    )
    decoded = (feats.astype(F32) + total).astype(BF16)
    colour = lax.dot_general(rgb, decoded, NT, preferred_element_type=F32)
    both = jnp.concatenate(
        [colour.astype(BF16).astype(F32)]
        + [real.astype(F32) for real in reals]
        + [jnp.zeros((2, width), F32)],
        axis=0,
    )
    return decoded, both.astype(BF16)


def rows_kernel(
    a_ref, b_ref, w_ref, sum_ref, feat_ref, rgb_ref, real_ref, y_ref, decoded_ref, colour_ref,
    lines_ref, late_ref,
):
    odd = lax.rem(lax.axis_index("rows"), 2)
    frames, width, chans = a_ref.shape
    lines_ref[1 - odd] = a_ref[...]
    lines_ref[odd] = b_ref[...]
    zeros = jnp.zeros((width, chans), BF16)
    for o in range(2):
        line = [zeros, zeros] + [lines_ref[o, t] for t in range(frames)]
        lhs = jnp.concatenate(
            [jnp.concatenate(line[dt : dt + frames], axis=0) for dt in range(3)], axis=1
        )
        inputs = [(dt, 3 * o - 1) for dt in range(3)]
        base = o * 3 * chans
        for j, some in tiles(column_blocks((o,), chans)):
            cols = slice(base + j * 128, base + (j + len(some)) * 128)
            got = jnp.dot(lhs, rhs_tile(w_ref, some, inputs), preferred_element_type=F32)
            got = got + sum_ref[:, cols]
            y_ref[:, cols] = got[: 2 * width]
            late_ref[:, cols] = got[2 * width :]
        for t in range(frames - 2):
            ys = [
                late_ref[t * width : (t + 1) * width, base + dw * chans : base + (dw + 1) * chans]
                for dw in range(3)
            ]
            decoded_ref[t, o], colour_ref[t, o] = finish(
                ys,
                feat_ref[t + 2, o],
                rgb_ref[...],
                [real_ref[c, t + 2, o : o + 1] for c in range(3)],
            )


def corner_kernel(
    past_ref, w_ref, sum_ref, feat_ref, rgb_ref, real_ref, done_ref, shown_ref,
    decoded_ref, colour_ref, y_ref, lines_ref,
):
    odd = lax.rem(lax.axis_index("rows"), 2)
    width, chans = past_ref.shape[2:]
    decoded_ref[2:] = done_ref[...]
    colour_ref[2:] = shown_ref[...]
    lines_ref[1 - odd] = past_ref[0]
    lines_ref[odd] = past_ref[1]
    zeros = jnp.zeros((width, chans), BF16)
    for o in range(2):
        lhs = past_lhs([lines_ref[o]], zeros)
        inputs = [(dt, 3 * o - 1) for dt in range(2)]
        base = o * 3 * chans
        for j, some in tiles(column_blocks((o,), chans)):
            cols = slice(base + j * 128, base + (j + len(some)) * 128)
            y_ref[:, cols] = sum_ref[:, cols] + jnp.dot(
                lhs, rhs_tile(w_ref, some, inputs), preferred_element_type=F32
            )
        for t in range(2):
            ys = [
                y_ref[t * width : (t + 1) * width, base + dw * chans : base + (dw + 1) * chans]
                for dw in range(3)
            ]
            decoded_ref[t, o], colour_ref[t, o] = finish(
                ys,
                feat_ref[t, o],
                rgb_ref[...],
                [real_ref[c, t, o : o + 1] for c in range(3)],
            )


def pack_kernel(a_ref, own_ref, b_ref, for_a_ref, for_b_ref):
    odd = lax.rem(lax.axis_index("tm"), 2)
    frames = own_ref.shape[0]
    for start, out_ref in (((frames - 2) * (1 - odd), for_a_ref), ((frames - 2) * odd, for_b_ref)):
        for k, ref in enumerate((a_ref, own_ref, b_ref)):
            out_ref[:, 2 * k : 2 * k + 2] = ref[pl.ds(start, 2)]


def disc_kernel(a_ref, own_ref, b_ref, ta_ref, tb_ref, w1_ref, w2_ref, out_ref, x_ref, f_ref):
    tm, band = lax.axis_index("tm"), lax.axis_index("rows")
    tm_count, row_count = lax.axis_size("tm"), lax.axis_size("rows")
    odd_t, odd_r = lax.rem(tm, 2), lax.rem(band, 2)
    width = out_ref.shape[-1]
    frames = out_ref.shape[0]
    col = lax.broadcasted_iota(jnp.int32, (8, width), 1)

    def put(t, h, line):
        x = line.astype(F32)
        x_ref[t, h, 0:8] = jnp.where(col == 0, 0.0, pltpu.roll(x, 1, 1))
        x_ref[t, h, 8:16] = x
        x_ref[t, h, 16:24] = jnp.where(col == width - 1, 0.0, pltpu.roll(x, width - 1, 1))

    row_at = [4 * (1 - odd_r), 4 * (1 - odd_r) + 1, 2, 3, 4 * odd_r, 4 * odd_r + 1]
    a_at = (frames + 2) * (1 - odd_t)
    b_at = (frames + 2) * odd_t
    for k in range(6):
        for t in range(frames):
            put(t + 2, row_at[k], (a_ref, own_ref, b_ref)[k // 2][t, k % 2])
        for t in range(2):
            put(a_at + t, row_at[k], ta_ref[t, k])
            put(b_at + t, row_at[k], tb_ref[t, k])

    w1 = w1_ref[...]
    near = {}
    for t in range(frames + 2):
        for h in range(0, 4, 2):
            cols = []
            for hh in (h, h + 1):
                cols.append(
                    jnp.concatenate(
                        [x_ref[t + dt, hh + dh] for dt in range(3) for dh in range(3)], axis=0
                    ).astype(BF16)
                )
            first = leaky(jnp.dot(w1, jnp.concatenate(cols, axis=1), preferred_element_type=F32))
            for i, hh in enumerate((h, h + 1)):
                part = first[:, i * width : (i + 1) * width]
                inside = []
                if t == 0:
                    inside.append(tm > 0)
                if t == frames + 1:
                    inside.append(tm < tm_count - 1)
                if hh == 0:
                    inside.append(band > 0)
                if hh == 3:
                    inside.append(band < row_count - 1)
                if inside:
                    keep = inside[0] if len(inside) == 1 else jnp.logical_and(*inside)
                    part = jnp.where(keep, part, 0.0)
                part = part.astype(BF16)
                f_ref[t, hh] = part
                if 1 <= t <= frames and 1 <= hh <= 2:
                    wide = part.astype(F32)
                    half = wide.shape[0] // 2
                    near[t - 1, hh - 1] = jnp.mean(
                        jnp.abs(wide[:half] - wide[half:]), axis=0, keepdims=True
                    )

    w2 = w2_ref[...]
    depth2 = w2.shape[0] // 3
    half = f_ref.shape[2] // 2
    colw = lax.broadcasted_iota(jnp.int32, (depth2, width), 1)
    for t in range(frames):
        for h in range(2):
            sides = []
            for s in range(2):
                sides.append(
                    jnp.concatenate(
                        [
                            f_ref[t + dt, h + dh, s * half : (s + 1) * half]
                            for dt in range(3)
                            for dh in range(3)
                        ],
                        axis=0,
                    )
                )
            y = jnp.dot(w2, jnp.concatenate(sides, axis=1), preferred_element_type=F32)
            outs = []
            for s in range(2):
                y0, y1, y2 = (
                    y[d * depth2 : (d + 1) * depth2, s * width : (s + 1) * width] for d in range(3)
                )
                total = (
                    y1
                    + jnp.where(colw == 0, 0.0, pltpu.roll(y0, 1, 1))
                    + jnp.where(colw == width - 1, 0.0, pltpu.roll(y2, width - 1, 1))
                )
                outs.append(leaky(total).astype(BF16).astype(F32))
            far = jnp.mean(jnp.abs(outs[0] - outs[1]), axis=0, keepdims=True)
            out_ref[t, h : h + 1] = near[t, h] + far


def per_device(
    latent_feat, norm_gain, conv_weight, rgb_weight, real_frames, disc_first, disc_second
):
    frames, height, width, chans = latent_feat.shape
    depth1, depth2 = disc_first.shape[1], disc_second.shape[1]
    cells = frames * width

    to_a, to_b, tail = local(
        act_kernel,
        (kept(frames, width, chans), kept(frames, width, chans), kept(2, 2, width, chans)),
        (latent_feat, norm_gain),
        hbm=(0, 1),
        scratch=[
            pltpu.VMEM(latent_feat.shape, BF16),
            pltpu.VMEM(norm_gain.shape, F32),
            pltpu.SemaphoreType.DMA((frames + 1,)),
        ],
    )
    past = onward(tail, "tm")
    from_b = swap(to_b, "rows", 1)
    from_a = swap(to_a, "rows", 0)

    line = 2 * width * chans * chans
    y, weight = local(
        own_kernel,
        (kept(cells, 6 * chans, dtype=F32), kept(*conv_weight.shape)),
        (to_a, to_b, past, conv_weight),
        hbm=(3,),
        scratch=[
            pltpu.VMEM((2, frames + 2, width, chans), BF16),
            pltpu.SemaphoreType.DMA((27,)),
        ],
        flops=48 * 3 * line,
    )
    corner = onward(jnp.stack([from_a[frames - 2 :], from_b[frames - 2 :]]), "tm")
    rgb = rgb_weight.T
    y, done, shown = local(
        rows_kernel,
        (
            kept(2 * width, 6 * chans, dtype=F32),
            kept(frames - 2, height, width, chans),
            kept(frames - 2, height, 8, width),
        ),
        (from_a, from_b, weight, y, latent_feat, rgb, real_frames),
        scratch=[
            pltpu.VMEM((2, frames, width, chans), BF16),
            pltpu.VMEM((cells - 2 * width, 6 * chans), F32),
        ],
        flops=18 * 3 * line,
    )
    decoded, colour = local(
        corner_kernel,
        (jax.ShapeDtypeStruct((frames, height, width, chans), BF16), kept(frames, height, 8, width)),
        (corner, weight, y, latent_feat, rgb, real_frames, done, shown),
        scratch=[
            pltpu.VMEM((2 * width, 6 * chans), F32),
            pltpu.VMEM((2, 2, width, chans), BF16),
        ],
        flops=6 * 3 * line,
    )
    w2, w1 = local(
        prep_kernel,
        (kept(3 * depth2, 9 * depth1), kept(2 * depth1, 27 * 8)),
        (jnp.transpose(disc_second, (0, 2, 1)), jnp.transpose(disc_first, (2, 0, 1))),
    )

    side_b = swap(colour, "rows", 1)
    side_a = swap(colour, "rows", 0)
    ends = kept(2, height + 4, 8, width)
    for_a, for_b = local(pack_kernel, (ends, ends), (side_a, colour, side_b))
    time_b = swap(for_b, "tm", 1)
    time_a = swap(for_a, "tm", 0)

    match_map = local(
        disc_kernel,
        jax.ShapeDtypeStruct((frames, height, width), F32),
        (side_a, colour, side_b, time_a, time_b, w1, w2),
        scratch=[
            pltpu.VMEM((frames + 4, height + 4, 24, width), F32),
            pltpu.VMEM((frames + 2, height + 2, 2 * depth1, width), BF16),
        ],
    )
    return (decoded, match_map)


def solution(mesh):
    placed = (P("tm", "rows", None, None), P(), P(), P(), P(None, "tm", "rows", None), P(), P())
    return jax.shard_map(
        per_device,
        mesh=mesh,
        in_specs=placed,
        out_specs=(P("tm", "rows", None, None), P("tm", "rows", None)),
        check_vma=False,
    )
```

```python
import jax
import jax.numpy as jnp
from jax import lax
from jax.experimental import pallas as pl
from jax.experimental.pallas import tpu as pltpu
from jax.sharding import PartitionSpec as P


F32 = jnp.float32
BF16 = jnp.bfloat16
VMEM = pl.BlockSpec(memory_space=pltpu.VMEM)
HBM = pl.BlockSpec(memory_space=pltpu.HBM)
NT = (((1,), (1,)), ((), ()))


def pairs(count, first):
    route = []
    for i in range(first, count - 1, 2):
        route += [(i, i + 1), (i + 1, i)]
    return route


def swap(block, axis, first):
    return lax.ppermute(block, axis, pairs(lax.axis_size(axis), first))


def onward(block, axis):
    return lax.ppermute(block, axis, [(i, i + 1) for i in range(lax.axis_size(axis) - 1)])


def local(kernel, outs, args, scratch=(), aliases=None, flops=0, hbm=(), limit=24):
    args = [
        pltpu.with_memory_space_constraint(a, pltpu.HBM if i in hbm else pltpu.VMEM)
        for i, a in enumerate(args)
    ]
    return pl.pallas_call(
        kernel,
        out_shape=outs,
        in_specs=[HBM if i in hbm else VMEM for i in range(len(args))],
        out_specs=jax.tree.map(lambda _: VMEM, outs),
        scratch_shapes=scratch,
        input_output_aliases=aliases or {},
        compiler_params=pltpu.CompilerParams(vmem_limit_bytes=limit << 20),
        cost_estimate=pl.CostEstimate(flops=flops, bytes_accessed=10**6, transcendentals=0),
    )(*args)


def kept(*dims, dtype=BF16):
    return pltpu.VMEM(dims, dtype)


def leaky(value):
    return jnp.maximum(value, 0.2 * value)


def act_kernel(feat_ref, gain_ref, to_a_ref, to_b_ref, tail_ref, feats_ref, scale_ref, sems):
    odd = lax.rem(lax.axis_index("rows"), 2)
    frames = feat_ref.shape[0]
    order = [frames - 2, frames - 1] + list(range(frames - 2))
    fetch_gain = pltpu.make_async_copy(gain_ref, scale_ref, sems.at[frames])
    fetch = [pltpu.make_async_copy(feat_ref.at[t], feats_ref.at[t], sems.at[t]) for t in range(frames)]
    fetch_gain.start()
    for t in order:
        fetch[t].start()
    fetch_gain.wait()
    gain = scale_ref[...]
    for t in order:
        fetch[t].wait()
        for k, (row, out_ref) in enumerate(((1 - odd, to_a_ref), (odd, to_b_ref))):
            feats = feats_ref[t, row].astype(F32)
            mean = jnp.mean(feats * feats, axis=-1, keepdims=True)
            normed = feats * lax.rsqrt(mean + 1e-06) * gain
            act = (normed * jax.nn.sigmoid(normed)).astype(BF16)
            out_ref[t] = act
            if t >= frames - 2:
                tail_ref[k, t - frames + 2] = act


def column_blocks(rows, chans):
    return [(o, dw, off) for o in rows for dw in range(3) for off in range(0, chans, 128)]


def rhs_tile(w_ref, blocks, inputs):
    halves = [
        jnp.concatenate(
            [w_ref[9 * dt + 3 * (i - o + 1) + dw, :, off : off + 128] for dt, i in inputs], axis=0
        )
        for o, dw, off in blocks
    ]
    return halves[0] if len(halves) == 1 else jnp.concatenate(halves, axis=1)


def tiles(blocks):
    return [(j, blocks[j : j + 2]) for j in range(0, len(blocks), 2)]


def own_kernel(a_ref, b_ref, past_ref, weight_ref, y_ref, w_ref, lines_ref, sems):
    odd = lax.rem(lax.axis_index("rows"), 2)
    frames, width, chans = a_ref.shape
    order = [9 * dt + k for dt in (2, 1, 0) for k in range(9)]
    loads = {
        tap: pltpu.make_async_copy(weight_ref.at[tap], w_ref.at[tap], sems.at[tap]) for tap in order
    }
    for tap in order:
        loads[tap].start()
    for k, (row, line_ref) in enumerate(((1 - odd, a_ref), (odd, b_ref))):
        lines_ref[row, pl.ds(0, 2)] = past_ref[k]
        lines_ref[row, pl.ds(2, frames)] = line_ref[...]
    for dts in ((2,), (1, 0)):
        for dt in dts:
            for tap in range(9 * dt, 9 * dt + 9):
                loads[tap].wait()
        lhs = jnp.concatenate(
            [
                lines_ref[i, dt : dt + frames].reshape(frames * width, chans)
                for dt in dts
                for i in range(2)
            ],
            axis=1,
        )
        inputs = [(dt, i) for dt in dts for i in range(2)]
        for j, some in tiles(column_blocks((0, 1), chans)):
            cols = slice(j * 128, (j + len(some)) * 128)
            got = jnp.dot(lhs, rhs_tile(w_ref, some, inputs), preferred_element_type=F32)
            if 2 in dts:
                y_ref[:, cols] = got
            else:
                y_ref[:, cols] += got


def prep_kernel(d2_ref, d1_ref, w2_ref, w1_ref):
    depth1, depth2 = d2_ref.shape[1:]
    for tap in range(27):
        dw, rest = tap % 3, tap // 3
        if rest % 2 == 0:
            parts = [d2_ref[tap].astype(F32)]
            if rest < 8:
                parts.append(d2_ref[tap + 3].astype(F32))
            wide = jnp.concatenate(parts, axis=0)
            w2_ref[dw * depth2 : (dw + 1) * depth2, rest * depth1 : rest * depth1 + wide.shape[0]] = (
                wide.T.astype(BF16)
            )
    tap = lax.broadcasted_iota(jnp.int32, (27, 27 * 8), 0)
    place = lax.broadcasted_iota(jnp.int32, (27, 27 * 8), 1)
    for side in range(2):
        total = jnp.zeros((depth1, 27 * 8), F32)
        for c in range(3):
            pick = jnp.where(place == 8 * tap + 3 * side + c, 1.0, 0.0).astype(BF16)
            total = total + lax.dot_general(
                d1_ref[c], pick, (((0,), (0,)), ((), ())), preferred_element_type=F32
            )
        w1_ref[side * depth1 : (side + 1) * depth1] = total.astype(BF16)


def past_lhs(lines, zeros):
    first = [line[0] for line in lines] + [line[1] for line in lines]
    second = [line[1] for line in lines] + [zeros for _ in lines]
    return jnp.concatenate(
        [jnp.concatenate(first, axis=1), jnp.concatenate(second, axis=1)], axis=0
    )


def finish(ys, feats, rgb, reals):
    width, chans = ys[1].shape
    col = lax.broadcasted_iota(jnp.int32, (width, chans), 0)
    total = (
        ys[1]
        + jnp.where(col == 0, 0.0, pltpu.roll(ys[0], 1, 0))
        + jnp.where(col == width - 1, 0.0, pltpu.roll(ys[2], width - 1, 0))
    )
    decoded = (feats.astype(F32) + total).astype(BF16)
    colour = lax.dot_general(rgb, decoded, NT, preferred_element_type=F32)
    both = jnp.concatenate(
        [colour.astype(BF16).astype(F32)]
        + [real.astype(F32) for real in reals]
        + [jnp.zeros((2, width), F32)],
        axis=0,
    )
    return decoded, both.astype(BF16)


def rows_kernel(
    a_ref, b_ref, w_ref, sum_ref, feat_ref, rgb_ref, real_ref, y_ref, decoded_ref, colour_ref,
    lines_ref, late_ref,
):
    odd = lax.rem(lax.axis_index("rows"), 2)
    frames, width, chans = a_ref.shape
    lines_ref[1 - odd] = a_ref[...]
    lines_ref[odd] = b_ref[...]
    zeros = jnp.zeros((width, chans), BF16)
    for o in range(2):
        line = [zeros, zeros] + [lines_ref[o, t] for t in range(frames)]
        lhs = jnp.concatenate(
            [jnp.concatenate(line[dt : dt + frames], axis=0) for dt in range(3)], axis=1
        )
        inputs = [(dt, 3 * o - 1) for dt in range(3)]
        base = o * 3 * chans
        for j, some in tiles(column_blocks((o,), chans)):
            cols = slice(base + j * 128, base + (j + len(some)) * 128)
            got = jnp.dot(lhs, rhs_tile(w_ref, some, inputs), preferred_element_type=F32)
            got = got + sum_ref[:, cols]
            y_ref[:, cols] = got[: 2 * width]
            late_ref[:, cols] = got[2 * width :]
        for t in range(frames - 2):
            ys = [
                late_ref[t * width : (t + 1) * width, base + dw * chans : base + (dw + 1) * chans]
                for dw in range(3)
            ]
            decoded_ref[t + 2, o], colour_ref[t + 2, o] = finish(
                ys,
                feat_ref[t + 2, o],
                rgb_ref[...],
                [real_ref[c, t + 2, o : o + 1] for c in range(3)],
            )


def corner_kernel(
    past_ref, w_ref, sum_ref, feat_ref, rgb_ref, real_ref, done_ref, shown_ref,
    decoded_ref, colour_ref, y_ref, lines_ref,
):
    odd = lax.rem(lax.axis_index("rows"), 2)
    width, chans = past_ref.shape[2:]
    lines_ref[1 - odd] = past_ref[0]
    lines_ref[odd] = past_ref[1]
    zeros = jnp.zeros((width, chans), BF16)
    for o in range(2):
        lhs = past_lhs([lines_ref[o]], zeros)
        inputs = [(dt, 3 * o - 1) for dt in range(2)]
        base = o * 3 * chans
        for j, some in tiles(column_blocks((o,), chans)):
            cols = slice(base + j * 128, base + (j + len(some)) * 128)
            y_ref[:, cols] = sum_ref[:, cols] + jnp.dot(
                lhs, rhs_tile(w_ref, some, inputs), preferred_element_type=F32
            )
        for t in range(2):
            ys = [
                y_ref[t * width : (t + 1) * width, base + dw * chans : base + (dw + 1) * chans]
                for dw in range(3)
            ]
            decoded_ref[t, o], colour_ref[t, o] = finish(
                ys,
                feat_ref[t, o],
                rgb_ref[...],
                [real_ref[c, t, o : o + 1] for c in range(3)],
            )


def pack_kernel(a_ref, own_ref, b_ref, for_a_ref, for_b_ref):
    odd = lax.rem(lax.axis_index("tm"), 2)
    frames = own_ref.shape[0]
    for start, out_ref in (((frames - 2) * (1 - odd), for_a_ref), ((frames - 2) * odd, for_b_ref)):
        for k, ref in enumerate((a_ref, own_ref, b_ref)):
            out_ref[:, 2 * k : 2 * k + 2] = ref[pl.ds(start, 2)]


def disc_kernel(a_ref, own_ref, b_ref, ta_ref, tb_ref, w1_ref, w2_ref, out_ref, x_ref, f_ref):
    tm, band = lax.axis_index("tm"), lax.axis_index("rows")
    tm_count, row_count = lax.axis_size("tm"), lax.axis_size("rows")
    odd_t, odd_r = lax.rem(tm, 2), lax.rem(band, 2)
    width = out_ref.shape[-1]
    frames = out_ref.shape[0]
    col = lax.broadcasted_iota(jnp.int32, (8, width), 1)

    def put(t, h, line):
        x = line.astype(F32)
        x_ref[t, h, 0:8] = jnp.where(col == 0, 0.0, pltpu.roll(x, 1, 1))
        x_ref[t, h, 8:16] = x
        x_ref[t, h, 16:24] = jnp.where(col == width - 1, 0.0, pltpu.roll(x, width - 1, 1))

    row_at = [4 * (1 - odd_r), 4 * (1 - odd_r) + 1, 2, 3, 4 * odd_r, 4 * odd_r + 1]
    a_at = (frames + 2) * (1 - odd_t)
    b_at = (frames + 2) * odd_t
    for k in range(6):
        for t in range(frames):
            put(t + 2, row_at[k], (a_ref, own_ref, b_ref)[k // 2][t, k % 2])
        for t in range(2):
            put(a_at + t, row_at[k], ta_ref[t, k])
            put(b_at + t, row_at[k], tb_ref[t, k])

    w1 = w1_ref[...]
    near = {}
    for t in range(frames + 2):
        for h in range(0, 4, 2):
            cols = []
            for hh in (h, h + 1):
                cols.append(
                    jnp.concatenate(
                        [x_ref[t + dt, hh + dh] for dt in range(3) for dh in range(3)], axis=0
                    ).astype(BF16)
                )
            first = leaky(jnp.dot(w1, jnp.concatenate(cols, axis=1), preferred_element_type=F32))
            for i, hh in enumerate((h, h + 1)):
                part = first[:, i * width : (i + 1) * width]
                inside = []
                if t == 0:
                    inside.append(tm > 0)
                if t == frames + 1:
                    inside.append(tm < tm_count - 1)
                if hh == 0:
                    inside.append(band > 0)
                if hh == 3:
                    inside.append(band < row_count - 1)
                if inside:
                    keep = inside[0] if len(inside) == 1 else jnp.logical_and(*inside)
                    part = jnp.where(keep, part, 0.0)
                part = part.astype(BF16)
                f_ref[t, hh] = part
                if 1 <= t <= frames and 1 <= hh <= 2:
                    wide = part.astype(F32)
                    half = wide.shape[0] // 2
                    near[t - 1, hh - 1] = jnp.mean(
                        jnp.abs(wide[:half] - wide[half:]), axis=0, keepdims=True
                    )

    w2 = w2_ref[...]
    depth2 = w2.shape[0] // 3
    half = f_ref.shape[2] // 2
    colw = lax.broadcasted_iota(jnp.int32, (depth2, width), 1)
    for t in range(frames):
        for h in range(2):
            sides = []
            for s in range(2):
                sides.append(
                    jnp.concatenate(
                        [
                            f_ref[t + dt, h + dh, s * half : (s + 1) * half]
                            for dt in range(3)
                            for dh in range(3)
                        ],
                        axis=0,
                    )
                )
            y = jnp.dot(w2, jnp.concatenate(sides, axis=1), preferred_element_type=F32)
            outs = []
            for s in range(2):
                y0, y1, y2 = (
                    y[d * depth2 : (d + 1) * depth2, s * width : (s + 1) * width] for d in range(3)
                )
                total = (
                    y1
                    + jnp.where(colw == 0, 0.0, pltpu.roll(y0, 1, 1))
                    + jnp.where(colw == width - 1, 0.0, pltpu.roll(y2, width - 1, 1))
                )
                outs.append(leaky(total).astype(BF16).astype(F32))
            far = jnp.mean(jnp.abs(outs[0] - outs[1]), axis=0, keepdims=True)
            out_ref[t, h : h + 1] = near[t, h] + far


def per_device(
    latent_feat, norm_gain, conv_weight, rgb_weight, real_frames, disc_first, disc_second
):
    frames, height, width, chans = latent_feat.shape
    depth1, depth2 = disc_first.shape[1], disc_second.shape[1]
    cells = frames * width

    to_a, to_b, tail = local(
        act_kernel,
        (kept(frames, width, chans), kept(frames, width, chans), kept(2, 2, width, chans)),
        (latent_feat, norm_gain),
        hbm=(0, 1),
        scratch=[
            pltpu.VMEM(latent_feat.shape, BF16),
            pltpu.VMEM(norm_gain.shape, F32),
            pltpu.SemaphoreType.DMA((frames + 1,)),
        ],
    )
    past = onward(tail, "tm")
    from_b = swap(to_b, "rows", 1)
    from_a = swap(to_a, "rows", 0)

    line = 2 * width * chans * chans
    y, weight = local(
        own_kernel,
        (kept(cells, 6 * chans, dtype=F32), kept(*conv_weight.shape)),
        (to_a, to_b, past, conv_weight),
        hbm=(3,),
        scratch=[
            pltpu.VMEM((2, frames + 2, width, chans), BF16),
            pltpu.SemaphoreType.DMA((27,)),
        ],
        flops=48 * 3 * line,
    )
    corner = onward(jnp.stack([from_a[frames - 2 :], from_b[frames - 2 :]]), "tm")
    rgb = rgb_weight.T
    y, done, shown = local(
        rows_kernel,
        (
            kept(2 * width, 6 * chans, dtype=F32),
            kept(frames, height, width, chans),
            kept(frames, height, 8, width),
        ),
        (from_a, from_b, weight, y, latent_feat, rgb, real_frames),
        scratch=[
            pltpu.VMEM((2, frames, width, chans), BF16),
            pltpu.VMEM((cells - 2 * width, 6 * chans), F32),
        ],
        flops=18 * 3 * line,
    )
    decoded, colour = local(
        corner_kernel,
        (kept(frames, height, width, chans), kept(frames, height, 8, width)),
        (corner, weight, y, latent_feat, rgb, real_frames, done, shown),
        scratch=[
            pltpu.VMEM((2 * width, 6 * chans), F32),
            pltpu.VMEM((2, 2, width, chans), BF16),
        ],
        aliases={6: 0, 7: 1},
        flops=6 * 3 * line,
    )
    w2, w1 = local(
        prep_kernel,
        (kept(3 * depth2, 9 * depth1), kept(2 * depth1, 27 * 8)),
        (jnp.transpose(disc_second, (0, 2, 1)), jnp.transpose(disc_first, (2, 0, 1))),
    )

    side_b = swap(colour, "rows", 1)
    side_a = swap(colour, "rows", 0)
    ends = kept(2, height + 4, 8, width)
    for_a, for_b = local(pack_kernel, (ends, ends), (side_a, colour, side_b))
    time_b = swap(for_b, "tm", 1)
    time_a = swap(for_a, "tm", 0)

    match_map = local(
        disc_kernel,
        jax.ShapeDtypeStruct((frames, height, width), F32),
        (side_a, colour, side_b, time_a, time_b, w1, w2),
        scratch=[
            pltpu.VMEM((frames + 4, height + 4, 24, width), F32),
            pltpu.VMEM((frames + 2, height + 2, 2 * depth1, width), BF16),
        ],
    )
    return (decoded, match_map)


def solution(mesh):
    placed = (P("tm", "rows", None, None), P(), P(), P(), P(None, "tm", "rows", None), P(), P())
    return jax.shard_map(
        per_device,
        mesh=mesh,
        in_specs=placed,
        out_specs=(P("tm", "rows", None, None), P("tm", "rows", None)),
        check_vma=False,
    )
```

```python
import jax
import jax.numpy as jnp
from jax import lax
from jax.experimental import pallas as pl
from jax.experimental.pallas import tpu as pltpu
from jax.sharding import PartitionSpec as P


F32 = jnp.float32
BF16 = jnp.bfloat16
VMEM = pl.BlockSpec(memory_space=pltpu.VMEM)
HBM = pl.BlockSpec(memory_space=pltpu.HBM)
NT = (((1,), (1,)), ((), ()))


def pairs(count, first):
    route = []
    for i in range(first, count - 1, 2):
        route += [(i, i + 1), (i + 1, i)]
    return route


def swap(block, axis, first):
    return lax.ppermute(block, axis, pairs(lax.axis_size(axis), first))


def onward(block, axis):
    return lax.ppermute(block, axis, [(i, i + 1) for i in range(lax.axis_size(axis) - 1)])


def local(kernel, outs, args, scratch=(), aliases=None, flops=0, hbm=(), limit=24):
    args = [
        pltpu.with_memory_space_constraint(a, pltpu.HBM if i in hbm else pltpu.VMEM)
        for i, a in enumerate(args)
    ]
    return pl.pallas_call(
        kernel,
        out_shape=outs,
        in_specs=[HBM if i in hbm else VMEM for i in range(len(args))],
        out_specs=jax.tree.map(lambda _: VMEM, outs),
        scratch_shapes=scratch,
        input_output_aliases=aliases or {},
        compiler_params=pltpu.CompilerParams(vmem_limit_bytes=limit << 20),
        cost_estimate=pl.CostEstimate(flops=flops, bytes_accessed=10**6, transcendentals=0),
    )(*args)


def kept(*dims, dtype=BF16):
    return pltpu.VMEM(dims, dtype)


def leaky(value):
    return jnp.maximum(value, 0.2 * value)


def act_kernel(feat_ref, gain_ref, to_a_ref, to_b_ref, tail_ref, feats_ref, scale_ref, sems):
    odd = lax.rem(lax.axis_index("rows"), 2)
    frames = feat_ref.shape[0]
    order = [frames - 2, frames - 1] + list(range(frames - 2))
    fetch_gain = pltpu.make_async_copy(gain_ref, scale_ref, sems.at[frames])
    fetch = [pltpu.make_async_copy(feat_ref.at[t], feats_ref.at[t], sems.at[t]) for t in range(frames)]
    fetch_gain.start()
    for t in order:
        fetch[t].start()
    fetch_gain.wait()
    gain = scale_ref[...]
    for t in order:
        fetch[t].wait()
        for k, (row, out_ref) in enumerate(((1 - odd, to_a_ref), (odd, to_b_ref))):
            feats = feats_ref[t, row].astype(F32)
            mean = jnp.mean(feats * feats, axis=-1, keepdims=True)
            normed = feats * lax.rsqrt(mean + 1e-06) * gain
            act = (normed * jax.nn.sigmoid(normed)).astype(BF16)
            out_ref[t] = act
            if t >= frames - 2:
                tail_ref[k, t - frames + 2] = act


def column_blocks(rows, chans):
    return [(o, dw, off) for o in rows for dw in range(3) for off in range(0, chans, 128)]


def rhs_tile(w_ref, blocks, inputs):
    halves = [
        jnp.concatenate(
            [w_ref[9 * dt + 3 * (i - o + 1) + dw, :, off : off + 128] for dt, i in inputs], axis=0
        )
        for o, dw, off in blocks
    ]
    return halves[0] if len(halves) == 1 else jnp.concatenate(halves, axis=1)


def tiles(blocks):
    return [(j, blocks[j : j + 2]) for j in range(0, len(blocks), 2)]


def fetch_kernel(weight_ref, w_ref, sems):
    loads = [
        pltpu.make_async_copy(weight_ref.at[tap], w_ref.at[tap], sems.at[tap]) for tap in range(27)
    ]
    for load in loads:
        load.start()
    for load in loads:
        load.wait()


def own_kernel(a_ref, b_ref, past_ref, w_ref, y_ref, lines_ref):
    odd = lax.rem(lax.axis_index("rows"), 2)
    frames, width, chans = a_ref.shape
    for k, (row, line_ref) in enumerate(((1 - odd, a_ref), (odd, b_ref))):
        lines_ref[row, pl.ds(0, 2)] = past_ref[k]
        lines_ref[row, pl.ds(2, frames)] = line_ref[...]
    inputs = [(dt, i) for dt in range(3) for i in range(2)]
    lhs = jnp.concatenate(
        [lines_ref[i, dt : dt + frames].reshape(frames * width, chans) for dt, i in inputs], axis=1
    )
    for j, some in tiles(column_blocks((0, 1), chans)):
        y_ref[:, j * 128 : (j + len(some)) * 128] = jnp.dot(
            lhs, rhs_tile(w_ref, some, inputs), preferred_element_type=F32
        )


def prep_kernel(d2_ref, d1_ref, w2_ref, w1_ref):
    depth1, depth2 = d2_ref.shape[1:]
    for tap in range(27):
        dw, rest = tap % 3, tap // 3
        if rest % 2 == 0:
            parts = [d2_ref[tap].astype(F32)]
            if rest < 8:
                parts.append(d2_ref[tap + 3].astype(F32))
            wide = jnp.concatenate(parts, axis=0)
            w2_ref[dw * depth2 : (dw + 1) * depth2, rest * depth1 : rest * depth1 + wide.shape[0]] = (
                wide.T.astype(BF16)
            )
    tap = lax.broadcasted_iota(jnp.int32, (27, 27 * 8), 0)
    place = lax.broadcasted_iota(jnp.int32, (27, 27 * 8), 1)
    for side in range(2):
        total = jnp.zeros((depth1, 27 * 8), F32)
        for c in range(3):
            pick = jnp.where(place == 8 * tap + 3 * side + c, 1.0, 0.0).astype(BF16)
            total = total + lax.dot_general(
                d1_ref[c], pick, (((0,), (0,)), ((), ())), preferred_element_type=F32
            )
        w1_ref[side * depth1 : (side + 1) * depth1] = total.astype(BF16)


def past_lhs(lines, zeros):
    first = [line[0] for line in lines] + [line[1] for line in lines]
    second = [line[1] for line in lines] + [zeros for _ in lines]
    return jnp.concatenate(
        [jnp.concatenate(first, axis=1), jnp.concatenate(second, axis=1)], axis=0
    )


def finish(ys, feats, rgb, reals):
    width, chans = ys[1].shape
    col = lax.broadcasted_iota(jnp.int32, (width, chans), 0)
    total = (
        ys[1]
        + jnp.where(col == 0, 0.0, pltpu.roll(ys[0], 1, 0))
        + jnp.where(col == width - 1, 0.0, pltpu.roll(ys[2], width - 1, 0))
    )
    decoded = (feats.astype(F32) + total).astype(BF16)
    colour = lax.dot_general(rgb, decoded, NT, preferred_element_type=F32)
    both = jnp.concatenate(
        [colour.astype(BF16).astype(F32)]
        + [real.astype(F32) for real in reals]
        + [jnp.zeros((2, width), F32)],
        axis=0,
    )
    return decoded, both.astype(BF16)


def rows_kernel(
    a_ref, b_ref, w_ref, sum_ref, feat_ref, rgb_ref, real_ref, y_ref, decoded_ref, colour_ref,
    lines_ref, late_ref,
):
    odd = lax.rem(lax.axis_index("rows"), 2)
    frames, width, chans = a_ref.shape
    lines_ref[1 - odd] = a_ref[...]
    lines_ref[odd] = b_ref[...]
    zeros = jnp.zeros((width, chans), BF16)
    for o in range(2):
        line = [zeros, zeros] + [lines_ref[o, t] for t in range(frames)]
        lhs = jnp.concatenate(
            [jnp.concatenate(line[dt : dt + frames], axis=0) for dt in range(3)], axis=1
        )
        inputs = [(dt, 3 * o - 1) for dt in range(3)]
        base = o * 3 * chans
        for j, some in tiles(column_blocks((o,), chans)):
            cols = slice(base + j * 128, base + (j + len(some)) * 128)
            got = jnp.dot(lhs, rhs_tile(w_ref, some, inputs), preferred_element_type=F32)
            got = got + sum_ref[:, cols]
            y_ref[:, cols] = got[: 2 * width]
            late_ref[:, cols] = got[2 * width :]
        for t in range(frames - 2):
            ys = [
                late_ref[t * width : (t + 1) * width, base + dw * chans : base + (dw + 1) * chans]
                for dw in range(3)
            ]
            decoded_ref[t + 2, o], colour_ref[t + 2, o] = finish(
                ys,
                feat_ref[t + 2, o],
                rgb_ref[...],
                [real_ref[c, t + 2, o : o + 1] for c in range(3)],
            )


def corner_kernel(
    past_ref, w_ref, sum_ref, feat_ref, rgb_ref, real_ref, done_ref, shown_ref,
    decoded_ref, colour_ref, y_ref, lines_ref,
):
    odd = lax.rem(lax.axis_index("rows"), 2)
    width, chans = past_ref.shape[2:]
    lines_ref[1 - odd] = past_ref[0]
    lines_ref[odd] = past_ref[1]
    zeros = jnp.zeros((width, chans), BF16)
    for o in range(2):
        lhs = past_lhs([lines_ref[o]], zeros)
        inputs = [(dt, 3 * o - 1) for dt in range(2)]
        base = o * 3 * chans
        for j, some in tiles(column_blocks((o,), chans)):
            cols = slice(base + j * 128, base + (j + len(some)) * 128)
            y_ref[:, cols] = sum_ref[:, cols] + jnp.dot(
                lhs, rhs_tile(w_ref, some, inputs), preferred_element_type=F32
            )
        for t in range(2):
            ys = [
                y_ref[t * width : (t + 1) * width, base + dw * chans : base + (dw + 1) * chans]
                for dw in range(3)
            ]
            decoded_ref[t, o], colour_ref[t, o] = finish(
                ys,
                feat_ref[t, o],
                rgb_ref[...],
                [real_ref[c, t, o : o + 1] for c in range(3)],
            )


def pack_kernel(a_ref, own_ref, b_ref, for_a_ref, for_b_ref):
    odd = lax.rem(lax.axis_index("tm"), 2)
    frames = own_ref.shape[0]
    for start, out_ref in (((frames - 2) * (1 - odd), for_a_ref), ((frames - 2) * odd, for_b_ref)):
        for k, ref in enumerate((a_ref, own_ref, b_ref)):
            out_ref[:, 2 * k : 2 * k + 2] = ref[pl.ds(start, 2)]


def disc_kernel(a_ref, own_ref, b_ref, ta_ref, tb_ref, w1_ref, w2_ref, out_ref, x_ref, f_ref):
    tm, band = lax.axis_index("tm"), lax.axis_index("rows")
    tm_count, row_count = lax.axis_size("tm"), lax.axis_size("rows")
    odd_t, odd_r = lax.rem(tm, 2), lax.rem(band, 2)
    width = out_ref.shape[-1]
    frames = out_ref.shape[0]
    col = lax.broadcasted_iota(jnp.int32, (8, width), 1)

    def put(t, h, line):
        x = line.astype(F32)
        x_ref[t, h, 0:8] = jnp.where(col == 0, 0.0, pltpu.roll(x, 1, 1))
        x_ref[t, h, 8:16] = x
        x_ref[t, h, 16:24] = jnp.where(col == width - 1, 0.0, pltpu.roll(x, width - 1, 1))

    row_at = [4 * (1 - odd_r), 4 * (1 - odd_r) + 1, 2, 3, 4 * odd_r, 4 * odd_r + 1]
    a_at = (frames + 2) * (1 - odd_t)
    b_at = (frames + 2) * odd_t
    for k in range(6):
        for t in range(frames):
            put(t + 2, row_at[k], (a_ref, own_ref, b_ref)[k // 2][t, k % 2])
        for t in range(2):
            put(a_at + t, row_at[k], ta_ref[t, k])
            put(b_at + t, row_at[k], tb_ref[t, k])

    w1 = w1_ref[...]
    near = {}
    for t in range(frames + 2):
        for h in range(0, 4, 2):
            cols = []
            for hh in (h, h + 1):
                cols.append(
                    jnp.concatenate(
                        [x_ref[t + dt, hh + dh] for dt in range(3) for dh in range(3)], axis=0
                    ).astype(BF16)
                )
            first = leaky(jnp.dot(w1, jnp.concatenate(cols, axis=1), preferred_element_type=F32))
            for i, hh in enumerate((h, h + 1)):
                part = first[:, i * width : (i + 1) * width]
                inside = []
                if t == 0:
                    inside.append(tm > 0)
                if t == frames + 1:
                    inside.append(tm < tm_count - 1)
                if hh == 0:
                    inside.append(band > 0)
                if hh == 3:
                    inside.append(band < row_count - 1)
                if inside:
                    keep = inside[0] if len(inside) == 1 else jnp.logical_and(*inside)
                    part = jnp.where(keep, part, 0.0)
                part = part.astype(BF16)
                f_ref[t, hh] = part
                if 1 <= t <= frames and 1 <= hh <= 2:
                    wide = part.astype(F32)
                    half = wide.shape[0] // 2
                    near[t - 1, hh - 1] = jnp.mean(
                        jnp.abs(wide[:half] - wide[half:]), axis=0, keepdims=True
                    )

    w2 = w2_ref[...]
    depth2 = w2.shape[0] // 3
    half = f_ref.shape[2] // 2
    colw = lax.broadcasted_iota(jnp.int32, (depth2, width), 1)
    for t in range(frames):
        for h in range(2):
            sides = []
            for s in range(2):
                sides.append(
                    jnp.concatenate(
                        [
                            f_ref[t + dt, h + dh, s * half : (s + 1) * half]
                            for dt in range(3)
                            for dh in range(3)
                        ],
                        axis=0,
                    )
                )
            y = jnp.dot(w2, jnp.concatenate(sides, axis=1), preferred_element_type=F32)
            outs = []
            for s in range(2):
                y0, y1, y2 = (
                    y[d * depth2 : (d + 1) * depth2, s * width : (s + 1) * width] for d in range(3)
                )
                total = (
                    y1
                    + jnp.where(colw == 0, 0.0, pltpu.roll(y0, 1, 1))
                    + jnp.where(colw == width - 1, 0.0, pltpu.roll(y2, width - 1, 1))
                )
                outs.append(leaky(total).astype(BF16).astype(F32))
            far = jnp.mean(jnp.abs(outs[0] - outs[1]), axis=0, keepdims=True)
            out_ref[t, h : h + 1] = near[t, h] + far


def per_device(
    latent_feat, norm_gain, conv_weight, rgb_weight, real_frames, disc_first, disc_second
):
    frames, height, width, chans = latent_feat.shape
    depth1, depth2 = disc_first.shape[1], disc_second.shape[1]
    cells = frames * width

    to_a, to_b, tail = local(
        act_kernel,
        (kept(frames, width, chans), kept(frames, width, chans), kept(2, 2, width, chans)),
        (latent_feat, norm_gain),
        hbm=(0, 1),
        scratch=[
            pltpu.VMEM(latent_feat.shape, BF16),
            pltpu.VMEM(norm_gain.shape, F32),
            pltpu.SemaphoreType.DMA((frames + 1,)),
        ],
    )
    past = onward(tail, "tm")
    from_b = swap(to_b, "rows", 1)
    from_a = swap(to_a, "rows", 0)

    line = 2 * width * chans * chans
    weight = local(
        fetch_kernel,
        kept(*conv_weight.shape),
        (conv_weight,),
        hbm=(0,),
        scratch=[pltpu.SemaphoreType.DMA((27,))],
    )
    y = local(
        own_kernel,
        kept(cells, 6 * chans, dtype=F32),
        (to_a, to_b, past, weight),
        scratch=[pltpu.VMEM((2, frames + 2, width, chans), BF16)],
        flops=48 * 3 * line,
    )
    corner = onward(jnp.stack([from_a[frames - 2 :], from_b[frames - 2 :]]), "tm")
    rgb = rgb_weight.T
    y, done, shown = local(
        rows_kernel,
        (
            kept(2 * width, 6 * chans, dtype=F32),
            kept(frames, height, width, chans),
            kept(frames, height, 8, width),
        ),
        (from_a, from_b, weight, y, latent_feat, rgb, real_frames),
        scratch=[
            pltpu.VMEM((2, frames, width, chans), BF16),
            pltpu.VMEM((cells - 2 * width, 6 * chans), F32),
        ],
        flops=18 * 3 * line,
    )
    decoded, colour = local(
        corner_kernel,
        (kept(frames, height, width, chans), kept(frames, height, 8, width)),
        (corner, weight, y, latent_feat, rgb, real_frames, done, shown),
        scratch=[
            pltpu.VMEM((2 * width, 6 * chans), F32),
            pltpu.VMEM((2, 2, width, chans), BF16),
        ],
        aliases={6: 0, 7: 1},
        flops=6 * 3 * line,
    )
    w2, w1 = local(
        prep_kernel,
        (kept(3 * depth2, 9 * depth1), kept(2 * depth1, 27 * 8)),
        (jnp.transpose(disc_second, (0, 2, 1)), jnp.transpose(disc_first, (2, 0, 1))),
    )

    side_b = swap(colour, "rows", 1)
    side_a = swap(colour, "rows", 0)
    ends = kept(2, height + 4, 8, width)
    for_a, for_b = local(pack_kernel, (ends, ends), (side_a, colour, side_b))
    time_b = swap(for_b, "tm", 1)
    time_a = swap(for_a, "tm", 0)

    match_map = local(
        disc_kernel,
        jax.ShapeDtypeStruct((frames, height, width), F32),
        (side_a, colour, side_b, time_a, time_b, w1, w2),
        scratch=[
            pltpu.VMEM((frames + 4, height + 4, 24, width), F32),
            pltpu.VMEM((frames + 2, height + 2, 2 * depth1, width), BF16),
        ],
    )
    return (decoded, match_map)


def solution(mesh):
    placed = (P("tm", "rows", None, None), P(), P(), P(), P(None, "tm", "rows", None), P(), P())
    return jax.shard_map(
        per_device,
        mesh=mesh,
        in_specs=placed,
        out_specs=(P("tm", "rows", None, None), P("tm", "rows", None)),
        check_vma=False,
    )
```

```python
import functools

import jax
import jax.numpy as jnp
from jax import lax
from jax.experimental import pallas as pl
from jax.experimental.pallas import tpu as pltpu
from jax.sharding import PartitionSpec as P


F32 = jnp.float32
BF16 = jnp.bfloat16
VMEM = pl.BlockSpec(memory_space=pltpu.VMEM)
HBM = pl.BlockSpec(memory_space=pltpu.HBM)
NT = (((1,), (1,)), ((), ()))


def pairs(count, first):
    route = []
    for i in range(first, count - 1, 2):
        route += [(i, i + 1), (i + 1, i)]
    return route


def swap(block, axis, first):
    return lax.ppermute(block, axis, pairs(lax.axis_size(axis), first))


def onward(block, axis):
    return lax.ppermute(block, axis, [(i, i + 1) for i in range(lax.axis_size(axis) - 1)])


def local(kernel, outs, args, scratch=(), aliases=None, flops=0, hbm=(), limit=24):
    args = [
        pltpu.with_memory_space_constraint(a, pltpu.HBM if i in hbm else pltpu.VMEM)
        for i, a in enumerate(args)
    ]
    return pl.pallas_call(
        kernel,
        out_shape=outs,
        in_specs=[HBM if i in hbm else VMEM for i in range(len(args))],
        out_specs=jax.tree.map(lambda _: VMEM, outs),
        scratch_shapes=scratch,
        input_output_aliases=aliases or {},
        compiler_params=pltpu.CompilerParams(vmem_limit_bytes=limit << 20),
        cost_estimate=pl.CostEstimate(flops=flops, bytes_accessed=10**6, transcendentals=0),
    )(*args)


def kept(*dims, dtype=BF16):
    return pltpu.VMEM(dims, dtype)


def leaky(value):
    return jnp.maximum(value, 0.2 * value)


def act_kernel(feat_ref, gain_ref, to_a_ref, to_b_ref, tail_ref, feats_ref, scale_ref, sems):
    odd = lax.rem(lax.axis_index("rows"), 2)
    frames = feat_ref.shape[0]
    order = [frames - 2, frames - 1] + list(range(frames - 2))
    fetch_gain = pltpu.make_async_copy(gain_ref, scale_ref, sems.at[frames])
    fetch = [pltpu.make_async_copy(feat_ref.at[t], feats_ref.at[t], sems.at[t]) for t in range(frames)]
    fetch_gain.start()
    for t in order:
        fetch[t].start()
    fetch_gain.wait()
    gain = scale_ref[...]
    for t in order:
        fetch[t].wait()
        for k, (row, out_ref) in enumerate(((1 - odd, to_a_ref), (odd, to_b_ref))):
            feats = feats_ref[t, row].astype(F32)
            mean = jnp.mean(feats * feats, axis=-1, keepdims=True)
            normed = feats * lax.rsqrt(mean + 1e-06) * gain
            act = (normed * jax.nn.sigmoid(normed)).astype(BF16)
            out_ref[t] = act
            if t >= frames - 2:
                tail_ref[k, t - frames + 2] = act


def column_blocks(chans):
    return [(dw, off) for dw in range(3) for off in range(0, chans, 128)]


def rhs_block(w_ref, dw, off, taps):
    return jnp.concatenate([w_ref[9 * dt + 3 * dh + dw, :, off : off + 128] for dt, dh in taps], axis=0)


def load_taps(weight_ref, w_ref, sems, dws):
    loads = {
        dw: [
            pltpu.make_async_copy(weight_ref.at[tap], w_ref.at[tap], sems.at[tap])
            for tap in range(dw, 27, 3)
        ]
        for dw in dws
    }
    for dw in dws:
        for load in loads[dw]:
            load.start()
    return loads


def fetch_kernel(weight_ref, w_ref, sems):
    for load in load_taps(weight_ref, w_ref, sems, (0,))[0]:
        load.wait()


def own_kernel(a_ref, b_ref, past_ref, weight_ref, some_ref, y_ref, w_ref, lines_ref, sems):
    odd = lax.rem(lax.axis_index("rows"), 2)
    frames, width, chans = a_ref.shape
    loads = load_taps(weight_ref, w_ref, sems, (1, 2))
    for k, (row, line_ref) in enumerate(((1 - odd, a_ref), (odd, b_ref))):
        lines_ref[row, pl.ds(0, 2)] = past_ref[k]
        lines_ref[row, pl.ds(2, frames)] = line_ref[...]
    inputs = [(dt, i) for dt in range(3) for i in range(2)]
    lhs = jnp.concatenate(
        [lines_ref[i, dt : dt + frames].reshape(frames * width, chans) for dt, i in inputs], axis=1
    )
    for dw in range(3):
        for load in loads.get(dw, ()):
            load.wait()
        blocks = [(o, off) for o in range(2) for off in range(0, chans, 128)]
        for j in range(0, len(blocks), 2):
            pair = blocks[j : j + 2]
            rhs = [rhs_block(w_ref, dw, off, [(dt, i - o + 1) for dt, i in inputs]) for o, off in pair]
            got = jnp.dot(lhs, jnp.concatenate(rhs, axis=1), preferred_element_type=F32)
            for k, (o, off) in enumerate(pair):
                at = dw * chans + off
                y_ref[o, :, at : at + 128] = got[:, k * 128 : (k + 1) * 128]


def prep_kernel(d2_ref, d1_ref, w2_ref, w1_ref):
    depth1, depth2 = d2_ref.shape[1:]
    for tap in range(27):
        dw, rest = tap % 3, tap // 3
        if rest % 2 == 0:
            parts = [d2_ref[tap].astype(F32)]
            if rest < 8:
                parts.append(d2_ref[tap + 3].astype(F32))
            wide = jnp.concatenate(parts, axis=0)
            w2_ref[dw * depth2 : (dw + 1) * depth2, rest * depth1 : rest * depth1 + wide.shape[0]] = (
                wide.T.astype(BF16)
            )
    tap = lax.broadcasted_iota(jnp.int32, (27, 27 * 8), 0)
    place = lax.broadcasted_iota(jnp.int32, (27, 27 * 8), 1)
    for side in range(2):
        total = jnp.zeros((depth1, 27 * 8), F32)
        for c in range(3):
            pick = jnp.where(place == 8 * tap + 3 * side + c, 1.0, 0.0).astype(BF16)
            total = total + lax.dot_general(
                d1_ref[c], pick, (((0,), (0,)), ((), ())), preferred_element_type=F32
            )
        w1_ref[side * depth1 : (side + 1) * depth1] = total.astype(BF16)


def finish(ys, feats, rgb, reals):
    width, chans = ys[1].shape
    col = lax.broadcasted_iota(jnp.int32, (width, chans), 0)
    total = (
        ys[1]
        + jnp.where(col == 0, 0.0, pltpu.roll(ys[0], 1, 0))
        + jnp.where(col == width - 1, 0.0, pltpu.roll(ys[2], width - 1, 0))
    )
    decoded = (feats.astype(F32) + total).astype(BF16)
    colour = lax.dot_general(rgb, decoded, NT, preferred_element_type=F32)
    both = jnp.concatenate(
        [colour.astype(BF16).astype(F32)]
        + [real.astype(F32) for real in reals]
        + [jnp.zeros((2, width), F32)],
        axis=0,
    )
    return decoded, both.astype(BF16)


def add_row(lhs, dts, row, w_ref, sums_ref, out_ref):
    chans = w_ref.shape[1]
    blocks = column_blocks(chans)
    for j in range(0, len(blocks), 2):
        some = blocks[j : j + 2]
        rhs = [rhs_block(w_ref, dw, off, [(dt, 2 * row) for dt in dts]) for dw, off in some]
        cols = slice(j * 128, (j + len(some)) * 128)
        out_ref[:, cols] = sums_ref[:, cols] + jnp.dot(
            lhs, rhs[0] if len(rhs) == 1 else jnp.concatenate(rhs, axis=1), preferred_element_type=F32
        )


def finish_row(ts, row, sums, feat_ref, rgb_ref, real_ref, decoded_ref, colour_ref):
    width, chans = feat_ref.shape[2:]
    for k, t in enumerate(ts):
        ys = [sums[k * width : (k + 1) * width, dw * chans : (dw + 1) * chans] for dw in range(3)]
        reals = []
        for c in range(3):
            both = real_ref[c, t].astype(F32)
            reals.append(jnp.where(row == 0, both[0:1], both[1:2]))
        decoded_ref[t, row], colour_ref[t, row] = finish(ys, feat_ref[t, row], rgb_ref[...], reals)


def side_row(side):
    odd = lax.rem(lax.axis_index("rows"), 2)
    return 1 - odd if side == 0 else odd


def near_kernel(side, line_ref, w_ref, sums_ref, feat_ref, rgb_ref, real_ref, *refs):
    y_ref, decoded_ref, colour_ref, all_ref = refs[-4:]
    row = side_row(side)
    frames, width, chans = line_ref.shape
    zeros = jnp.zeros((width, chans), BF16)
    line = [zeros, zeros] + [line_ref[t] for t in range(frames)]
    lhs = jnp.concatenate(
        [jnp.concatenate(line[dt : dt + frames], axis=0) for dt in range(3)], axis=1
    )
    add_row(lhs, range(3), row, w_ref, sums_ref.at[row], all_ref)
    y_ref[...] = all_ref[: 2 * width]
    late = range(2, frames)
    finish_row(
        late, row, all_ref.at[2 * width :], feat_ref, rgb_ref, real_ref, decoded_ref, colour_ref
    )


def corner_kernel(side, past_ref, w_ref, sums_ref, feat_ref, rgb_ref, real_ref, *refs):
    decoded_ref, colour_ref, all_ref = refs[-3:]
    row = side_row(side)
    width, chans = past_ref.shape[1:]
    lhs = jnp.concatenate(
        [
            jnp.concatenate([past_ref[0], past_ref[1]], axis=0),
            jnp.concatenate([past_ref[1], jnp.zeros((width, chans), BF16)], axis=0),
        ],
        axis=1,
    )
    add_row(lhs, range(2), row, w_ref, sums_ref, all_ref)
    finish_row(range(2), row, all_ref, feat_ref, rgb_ref, real_ref, decoded_ref, colour_ref)


def pack_kernel(a_ref, own_ref, b_ref, for_a_ref, for_b_ref):
    odd = lax.rem(lax.axis_index("tm"), 2)
    frames = own_ref.shape[0]
    for start, out_ref in (((frames - 2) * (1 - odd), for_a_ref), ((frames - 2) * odd, for_b_ref)):
        for k, ref in enumerate((a_ref, own_ref, b_ref)):
            out_ref[:, 2 * k : 2 * k + 2] = ref[pl.ds(start, 2)]


def disc_kernel(a_ref, own_ref, b_ref, ta_ref, tb_ref, w1_ref, w2_ref, out_ref, x_ref, f_ref):
    tm, band = lax.axis_index("tm"), lax.axis_index("rows")
    tm_count, row_count = lax.axis_size("tm"), lax.axis_size("rows")
    odd_t, odd_r = lax.rem(tm, 2), lax.rem(band, 2)
    width = out_ref.shape[-1]
    frames = out_ref.shape[0]
    col = lax.broadcasted_iota(jnp.int32, (8, width), 1)

    def put(t, h, line):
        x = line.astype(F32)
        x_ref[t, h, 0:8] = jnp.where(col == 0, 0.0, pltpu.roll(x, 1, 1))
        x_ref[t, h, 8:16] = x
        x_ref[t, h, 16:24] = jnp.where(col == width - 1, 0.0, pltpu.roll(x, width - 1, 1))

    row_at = [4 * (1 - odd_r), 4 * (1 - odd_r) + 1, 2, 3, 4 * odd_r, 4 * odd_r + 1]
    a_at = (frames + 2) * (1 - odd_t)
    b_at = (frames + 2) * odd_t
    for k in range(6):
        for t in range(frames):
            put(t + 2, row_at[k], (a_ref, own_ref, b_ref)[k // 2][t, k % 2])
        for t in range(2):
            put(a_at + t, row_at[k], ta_ref[t, k])
            put(b_at + t, row_at[k], tb_ref[t, k])

    w1 = w1_ref[...]
    near = {}
    for t in range(frames + 2):
        for h in range(0, 4, 2):
            cols = []
            for hh in (h, h + 1):
                cols.append(
                    jnp.concatenate(
                        [x_ref[t + dt, hh + dh] for dt in range(3) for dh in range(3)], axis=0
                    ).astype(BF16)
                )
            first = leaky(jnp.dot(w1, jnp.concatenate(cols, axis=1), preferred_element_type=F32))
            for i, hh in enumerate((h, h + 1)):
                part = first[:, i * width : (i + 1) * width]
                inside = []
                if t == 0:
                    inside.append(tm > 0)
                if t == frames + 1:
                    inside.append(tm < tm_count - 1)
                if hh == 0:
                    inside.append(band > 0)
                if hh == 3:
                    inside.append(band < row_count - 1)
                if inside:
                    keep = inside[0] if len(inside) == 1 else jnp.logical_and(*inside)
                    part = jnp.where(keep, part, 0.0)
                part = part.astype(BF16)
                f_ref[t, hh] = part
                if 1 <= t <= frames and 1 <= hh <= 2:
                    wide = part.astype(F32)
                    half = wide.shape[0] // 2
                    near[t - 1, hh - 1] = jnp.mean(
                        jnp.abs(wide[:half] - wide[half:]), axis=0, keepdims=True
                    )

    w2 = w2_ref[...]
    depth2 = w2.shape[0] // 3
    half = f_ref.shape[2] // 2
    colw = lax.broadcasted_iota(jnp.int32, (depth2, width), 1)
    for t in range(frames):
        for h in range(2):
            sides = []
            for s in range(2):
                sides.append(
                    jnp.concatenate(
                        [
                            f_ref[t + dt, h + dh, s * half : (s + 1) * half]
                            for dt in range(3)
                            for dh in range(3)
                        ],
                        axis=0,
                    )
                )
            y = jnp.dot(w2, jnp.concatenate(sides, axis=1), preferred_element_type=F32)
            outs = []
            for s in range(2):
                y0, y1, y2 = (
                    y[d * depth2 : (d + 1) * depth2, s * width : (s + 1) * width] for d in range(3)
                )
                total = (
                    y1
                    + jnp.where(colw == 0, 0.0, pltpu.roll(y0, 1, 1))
                    + jnp.where(colw == width - 1, 0.0, pltpu.roll(y2, width - 1, 1))
                )
                outs.append(leaky(total).astype(BF16).astype(F32))
            far = jnp.mean(jnp.abs(outs[0] - outs[1]), axis=0, keepdims=True)
            out_ref[t, h : h + 1] = near[t, h] + far


def per_device(
    latent_feat, norm_gain, conv_weight, rgb_weight, real_frames, disc_first, disc_second
):
    frames, height, width, chans = latent_feat.shape
    depth1, depth2 = disc_first.shape[1], disc_second.shape[1]
    cells = frames * width

    to_a, to_b, tail = local(
        act_kernel,
        (kept(frames, width, chans), kept(frames, width, chans), kept(2, 2, width, chans)),
        (latent_feat, norm_gain),
        hbm=(0, 1),
        scratch=[
            pltpu.VMEM(latent_feat.shape, BF16),
            pltpu.VMEM(norm_gain.shape, F32),
            pltpu.SemaphoreType.DMA((frames + 1,)),
        ],
    )
    past = onward(tail, "tm")
    from_b = swap(to_b, "rows", 1)
    from_a = swap(to_a, "rows", 0)

    line = 2 * width * chans * chans
    first_taps = local(
        fetch_kernel,
        kept(*conv_weight.shape),
        (conv_weight,),
        hbm=(0,),
        scratch=[pltpu.SemaphoreType.DMA((27,))],
    )
    sums, weight = local(
        own_kernel,
        (kept(height, cells, 3 * chans, dtype=F32), kept(*conv_weight.shape)),
        (to_a, to_b, past, conv_weight, first_taps),
        hbm=(3,),
        scratch=[
            pltpu.VMEM((2, frames + 2, width, chans), BF16),
            pltpu.SemaphoreType.DMA((27,)),
        ],
        aliases={4: 1},
        flops=48 * 3 * line,
    )
    corner_a = onward(from_a[frames - 2 :], "tm")
    corner_b = onward(from_b[frames - 2 :], "tm")
    rest = (latent_feat, rgb_weight.T, real_frames)
    early = kept(2 * width, 3 * chans, dtype=F32)
    shown = (kept(frames, height, width, chans), kept(frames, height, 8, width))
    ends = []
    outs = ()
    for side, row in enumerate((from_a, from_b)):
        y, *outs = local(
            functools.partial(near_kernel, side),
            (early,) + shown,
            (row, weight, sums) + rest + tuple(outs),
            scratch=[pltpu.VMEM((cells, 3 * chans), F32)],
            aliases={6: 1, 7: 2} if side else {},
            flops=12 * 3 * line,
        )
        ends.append(y)
    for side, row in enumerate((corner_a, corner_b)):
        outs = local(
            functools.partial(corner_kernel, side),
            shown,
            (row, weight, ends[side]) + rest + tuple(outs),
            scratch=[pltpu.VMEM((2 * width, 3 * chans), F32)],
            aliases={6: 0, 7: 1},
            flops=4 * 3 * line,
        )
    decoded, colour = outs
    w2, w1 = local(
        prep_kernel,
        (kept(3 * depth2, 9 * depth1), kept(2 * depth1, 27 * 8)),
        (jnp.transpose(disc_second, (0, 2, 1)), jnp.transpose(disc_first, (2, 0, 1))),
    )

    side_b = swap(colour, "rows", 1)
    side_a = swap(colour, "rows", 0)
    ends = kept(2, height + 4, 8, width)
    for_a, for_b = local(pack_kernel, (ends, ends), (side_a, colour, side_b))
    time_b = swap(for_b, "tm", 1)
    time_a = swap(for_a, "tm", 0)

    match_map = local(
        disc_kernel,
        jax.ShapeDtypeStruct((frames, height, width), F32),
        (side_a, colour, side_b, time_a, time_b, w1, w2),
        scratch=[
            pltpu.VMEM((frames + 4, height + 4, 24, width), F32),
            pltpu.VMEM((frames + 2, height + 2, 2 * depth1, width), BF16),
        ],
    )
    return (decoded, match_map)


def solution(mesh):
    placed = (P("tm", "rows", None, None), P(), P(), P(), P(None, "tm", "rows", None), P(), P())
    return jax.shard_map(
        per_device,
        mesh=mesh,
        in_specs=placed,
        out_specs=(P("tm", "rows", None, None), P("tm", "rows", None)),
        check_vma=False,
    )
```

```python
import functools

import jax
import jax.numpy as jnp
from jax import lax
from jax.experimental import pallas as pl
from jax.experimental.pallas import tpu as pltpu
from jax.sharding import PartitionSpec as P


F32 = jnp.float32
BF16 = jnp.bfloat16
VMEM = pl.BlockSpec(memory_space=pltpu.VMEM)
HBM = pl.BlockSpec(memory_space=pltpu.HBM)
NT = (((1,), (1,)), ((), ()))


def pairs(count, first):
    route = []
    for i in range(first, count - 1, 2):
        route += [(i, i + 1), (i + 1, i)]
    return route


def swap(block, axis, first):
    return lax.ppermute(block, axis, pairs(lax.axis_size(axis), first))


def onward(block, axis):
    return lax.ppermute(block, axis, [(i, i + 1) for i in range(lax.axis_size(axis) - 1)])


def local(kernel, outs, args, scratch=(), aliases=None, flops=0, hbm=(), limit=24):
    args = [
        pltpu.with_memory_space_constraint(a, pltpu.HBM if i in hbm else pltpu.VMEM)
        for i, a in enumerate(args)
    ]
    return pl.pallas_call(
        kernel,
        out_shape=outs,
        in_specs=[HBM if i in hbm else VMEM for i in range(len(args))],
        out_specs=jax.tree.map(lambda _: VMEM, outs),
        scratch_shapes=scratch,
        input_output_aliases=aliases or {},
        compiler_params=pltpu.CompilerParams(vmem_limit_bytes=limit << 20),
        cost_estimate=pl.CostEstimate(flops=flops, bytes_accessed=10**6, transcendentals=0),
    )(*args)


def kept(*dims, dtype=BF16):
    return pltpu.VMEM(dims, dtype)


def leaky(value):
    return jnp.maximum(value, 0.2 * value)


def act_kernel(feat_ref, gain_ref, to_a_ref, to_b_ref, tail_ref, feats_ref, scale_ref, sems):
    odd = lax.rem(lax.axis_index("rows"), 2)
    frames = feat_ref.shape[0]
    order = [frames - 2, frames - 1] + list(range(frames - 2))
    fetch_gain = pltpu.make_async_copy(gain_ref, scale_ref, sems.at[frames])
    fetch = [pltpu.make_async_copy(feat_ref.at[t], feats_ref.at[t], sems.at[t]) for t in range(frames)]
    fetch_gain.start()
    for t in order:
        fetch[t].start()
    fetch_gain.wait()
    gain = scale_ref[...]
    for t in order:
        fetch[t].wait()
        for k, (row, out_ref) in enumerate(((1 - odd, to_a_ref), (odd, to_b_ref))):
            feats = feats_ref[t, row].astype(F32)
            mean = jnp.mean(feats * feats, axis=-1, keepdims=True)
            normed = feats * lax.rsqrt(mean + 1e-06) * gain
            act = (normed * jax.nn.sigmoid(normed)).astype(BF16)
            out_ref[t] = act
            if t >= frames - 2:
                tail_ref[k, t - frames + 2] = act


def column_blocks(chans):
    return [(dw, off) for dw in range(3) for off in range(0, chans, 128)]


def rhs_block(w_ref, dw, off, taps):
    return jnp.concatenate([w_ref[9 * dt + 3 * dh + dw, :, off : off + 128] for dt, dh in taps], axis=0)


def start_taps(weight_ref, w_ref, sems, taps):
    for tap in taps:
        pltpu.make_async_copy(weight_ref.at[tap], w_ref.at[tap], sems.at[tap]).start()


def wait_taps(weight_ref, w_ref, sems, taps):
    for tap in taps:
        pltpu.make_async_copy(weight_ref.at[tap], w_ref.at[tap], sems.at[tap]).wait()


def taps_of(dts, dws):
    return [9 * dt + 3 * dh + dw for dw in dws for dt in dts for dh in range(3)]


def own_products(lhs, w_ref, inputs, dw):
    chans = w_ref.shape[1]
    blocks = [(o, off) for o in range(2) for off in range(0, chans, 128)]
    for j in range(0, len(blocks), 2):
        pair = blocks[j : j + 2]
        rhs = [rhs_block(w_ref, dw, off, [(dt, i - o + 1) for dt, i in inputs]) for o, off in pair]
        got = jnp.dot(lhs, jnp.concatenate(rhs, axis=1), preferred_element_type=F32)
        for k, (o, off) in enumerate(pair):
            at = dw * chans + off
            yield o, slice(at, at + 128), got[:, k * 128 : (k + 1) * 128]


def ahead_kernel(a_ref, b_ref, weight_ref, y_ref, w_ref, lines_ref, sems):
    odd = lax.rem(lax.axis_index("rows"), 2)
    frames, width, chans = a_ref.shape
    more = taps_of((0, 1), (0,))
    start_taps(weight_ref, w_ref, sems, taps_of((2,), range(3)) + more)
    lines_ref[1 - odd] = a_ref[...]
    lines_ref[odd] = b_ref[...]
    lhs = jnp.concatenate([lines_ref[i].reshape(frames * width, chans) for i in range(2)], axis=1)
    for dw in range(3):
        wait_taps(weight_ref, w_ref, sems, taps_of((2,), (dw,)))
        for o, cols, got in own_products(lhs, w_ref, [(2, 0), (2, 1)], dw):
            y_ref[o, :, cols] = got
    wait_taps(weight_ref, w_ref, sems, more)


def own_kernel(
    a_ref, b_ref, past_ref, weight_ref, some_ref, sums_ref, y_ref, w_ref, lines_ref, sems
):
    odd = lax.rem(lax.axis_index("rows"), 2)
    frames, width, chans = a_ref.shape
    start_taps(weight_ref, w_ref, sems, taps_of((0, 1), (1, 2)))
    for k, (row, line_ref) in enumerate(((1 - odd, a_ref), (odd, b_ref))):
        lines_ref[row, pl.ds(0, 2)] = past_ref[k]
        lines_ref[row, pl.ds(2, frames - 1)] = line_ref[: frames - 1]
    inputs = [(dt, i) for dt in range(2) for i in range(2)]
    lhs = jnp.concatenate(
        [lines_ref[i, dt : dt + frames].reshape(frames * width, chans) for dt, i in inputs], axis=1
    )
    for dw in range(3):
        if dw:
            wait_taps(weight_ref, w_ref, sems, taps_of((0, 1), (dw,)))
        for o, cols, got in own_products(lhs, w_ref, inputs, dw):
            y_ref[o, :, cols] = sums_ref[o, :, cols] + got


def prep_kernel(d2_ref, d1_ref, w2_ref, w1_ref):
    depth1, depth2 = d2_ref.shape[1:]
    for tap in range(27):
        dw, rest = tap % 3, tap // 3
        if rest % 2 == 0:
            parts = [d2_ref[tap].astype(F32)]
            if rest < 8:
                parts.append(d2_ref[tap + 3].astype(F32))
            wide = jnp.concatenate(parts, axis=0)
            w2_ref[dw * depth2 : (dw + 1) * depth2, rest * depth1 : rest * depth1 + wide.shape[0]] = (
                wide.T.astype(BF16)
            )
    tap = lax.broadcasted_iota(jnp.int32, (27, 27 * 8), 0)
    place = lax.broadcasted_iota(jnp.int32, (27, 27 * 8), 1)
    for side in range(2):
        total = jnp.zeros((depth1, 27 * 8), F32)
        for c in range(3):
            pick = jnp.where(place == 8 * tap + 3 * side + c, 1.0, 0.0).astype(BF16)
            total = total + lax.dot_general(
                d1_ref[c], pick, (((0,), (0,)), ((), ())), preferred_element_type=F32
            )
        w1_ref[side * depth1 : (side + 1) * depth1] = total.astype(BF16)


def finish(ys, feats, rgb, reals):
    width, chans = ys[1].shape
    col = lax.broadcasted_iota(jnp.int32, (width, chans), 0)
    total = (
        ys[1]
        + jnp.where(col == 0, 0.0, pltpu.roll(ys[0], 1, 0))
        + jnp.where(col == width - 1, 0.0, pltpu.roll(ys[2], width - 1, 0))
    )
    decoded = (feats.astype(F32) + total).astype(BF16)
    colour = lax.dot_general(rgb, decoded, NT, preferred_element_type=F32)
    both = jnp.concatenate(
        [colour.astype(BF16).astype(F32)]
        + [real.astype(F32) for real in reals]
        + [jnp.zeros((2, width), F32)],
        axis=0,
    )
    return decoded, both.astype(BF16)


def add_row(lhs, dts, row, w_ref, sums_ref, out_ref):
    chans = w_ref.shape[1]
    blocks = column_blocks(chans)
    for j in range(0, len(blocks), 2):
        some = blocks[j : j + 2]
        rhs = [rhs_block(w_ref, dw, off, [(dt, 2 * row) for dt in dts]) for dw, off in some]
        cols = slice(j * 128, (j + len(some)) * 128)
        out_ref[:, cols] = sums_ref[:, cols] + jnp.dot(
            lhs, rhs[0] if len(rhs) == 1 else jnp.concatenate(rhs, axis=1), preferred_element_type=F32
        )


def finish_row(ts, row, sums, feat_ref, rgb_ref, real_ref, decoded_ref, colour_ref):
    width, chans = feat_ref.shape[2:]
    for k, t in enumerate(ts):
        ys = [sums[k * width : (k + 1) * width, dw * chans : (dw + 1) * chans] for dw in range(3)]
        reals = []
        for c in range(3):
            both = real_ref[c, t].astype(F32)
            reals.append(jnp.where(row == 0, both[0:1], both[1:2]))
        decoded_ref[t, row], colour_ref[t, row] = finish(ys, feat_ref[t, row], rgb_ref[...], reals)


def side_row(side):
    odd = lax.rem(lax.axis_index("rows"), 2)
    return 1 - odd if side == 0 else odd


def near_kernel(side, line_ref, w_ref, sums_ref, feat_ref, rgb_ref, real_ref, *refs):
    y_ref, decoded_ref, colour_ref, all_ref = refs[-4:]
    row = side_row(side)
    frames, width, chans = line_ref.shape
    zeros = jnp.zeros((width, chans), BF16)
    line = [zeros, zeros] + [line_ref[t] for t in range(frames)]
    lhs = jnp.concatenate(
        [jnp.concatenate(line[dt : dt + frames], axis=0) for dt in range(3)], axis=1
    )
    add_row(lhs, range(3), row, w_ref, sums_ref.at[row], all_ref)
    y_ref[...] = all_ref[: 2 * width]
    late = range(2, frames)
    finish_row(
        late, row, all_ref.at[2 * width :], feat_ref, rgb_ref, real_ref, decoded_ref, colour_ref
    )


def corner_kernel(side, past_ref, w_ref, sums_ref, feat_ref, rgb_ref, real_ref, *refs):
    decoded_ref, colour_ref, all_ref = refs[-3:]
    row = side_row(side)
    width, chans = past_ref.shape[1:]
    lhs = jnp.concatenate(
        [
            jnp.concatenate([past_ref[0], past_ref[1]], axis=0),
            jnp.concatenate([past_ref[1], jnp.zeros((width, chans), BF16)], axis=0),
        ],
        axis=1,
    )
    add_row(lhs, range(2), row, w_ref, sums_ref, all_ref)
    finish_row(range(2), row, all_ref, feat_ref, rgb_ref, real_ref, decoded_ref, colour_ref)


def pack_kernel(a_ref, own_ref, b_ref, for_a_ref, for_b_ref):
    odd = lax.rem(lax.axis_index("tm"), 2)
    frames = own_ref.shape[0]
    for start, out_ref in (((frames - 2) * (1 - odd), for_a_ref), ((frames - 2) * odd, for_b_ref)):
        for k, ref in enumerate((a_ref, own_ref, b_ref)):
            out_ref[:, 2 * k : 2 * k + 2] = ref[pl.ds(start, 2)]


def disc_kernel(a_ref, own_ref, b_ref, ta_ref, tb_ref, w1_ref, w2_ref, out_ref, x_ref, f_ref):
    tm, band = lax.axis_index("tm"), lax.axis_index("rows")
    tm_count, row_count = lax.axis_size("tm"), lax.axis_size("rows")
    odd_t, odd_r = lax.rem(tm, 2), lax.rem(band, 2)
    width = out_ref.shape[-1]
    frames = out_ref.shape[0]
    col = lax.broadcasted_iota(jnp.int32, (8, width), 1)

    def put(t, h, line):
        x = line.astype(F32)
        x_ref[t, h, 0:8] = jnp.where(col == 0, 0.0, pltpu.roll(x, 1, 1))
        x_ref[t, h, 8:16] = x
        x_ref[t, h, 16:24] = jnp.where(col == width - 1, 0.0, pltpu.roll(x, width - 1, 1))

    row_at = [4 * (1 - odd_r), 4 * (1 - odd_r) + 1, 2, 3, 4 * odd_r, 4 * odd_r + 1]
    a_at = (frames + 2) * (1 - odd_t)
    b_at = (frames + 2) * odd_t
    for k in range(6):
        for t in range(frames):
            put(t + 2, row_at[k], (a_ref, own_ref, b_ref)[k // 2][t, k % 2])
        for t in range(2):
            put(a_at + t, row_at[k], ta_ref[t, k])
            put(b_at + t, row_at[k], tb_ref[t, k])

    w1 = w1_ref[...]
    near = {}
    for t in range(frames + 2):
        for h in range(0, 4, 2):
            cols = []
            for hh in (h, h + 1):
                cols.append(
                    jnp.concatenate(
                        [x_ref[t + dt, hh + dh] for dt in range(3) for dh in range(3)], axis=0
                    ).astype(BF16)
                )
            first = leaky(jnp.dot(w1, jnp.concatenate(cols, axis=1), preferred_element_type=F32))
            for i, hh in enumerate((h, h + 1)):
                part = first[:, i * width : (i + 1) * width]
                inside = []
                if t == 0:
                    inside.append(tm > 0)
                if t == frames + 1:
                    inside.append(tm < tm_count - 1)
                if hh == 0:
                    inside.append(band > 0)
                if hh == 3:
                    inside.append(band < row_count - 1)
                if inside:
                    keep = inside[0] if len(inside) == 1 else jnp.logical_and(*inside)
                    part = jnp.where(keep, part, 0.0)
                part = part.astype(BF16)
                f_ref[t, hh] = part
                if 1 <= t <= frames and 1 <= hh <= 2:
                    wide = part.astype(F32)
                    half = wide.shape[0] // 2
                    near[t - 1, hh - 1] = jnp.mean(
                        jnp.abs(wide[:half] - wide[half:]), axis=0, keepdims=True
                    )

    w2 = w2_ref[...]
    depth2 = w2.shape[0] // 3
    half = f_ref.shape[2] // 2
    colw = lax.broadcasted_iota(jnp.int32, (depth2, width), 1)
    for t in range(frames):
        for h in range(2):
            sides = []
            for s in range(2):
                sides.append(
                    jnp.concatenate(
                        [
                            f_ref[t + dt, h + dh, s * half : (s + 1) * half]
                            for dt in range(3)
                            for dh in range(3)
                        ],
                        axis=0,
                    )
                )
            y = jnp.dot(w2, jnp.concatenate(sides, axis=1), preferred_element_type=F32)
            outs = []
            for s in range(2):
                y0, y1, y2 = (
                    y[d * depth2 : (d + 1) * depth2, s * width : (s + 1) * width] for d in range(3)
                )
                total = (
                    y1
                    + jnp.where(colw == 0, 0.0, pltpu.roll(y0, 1, 1))
                    + jnp.where(colw == width - 1, 0.0, pltpu.roll(y2, width - 1, 1))
                )
                outs.append(leaky(total).astype(BF16).astype(F32))
            far = jnp.mean(jnp.abs(outs[0] - outs[1]), axis=0, keepdims=True)
            out_ref[t, h : h + 1] = near[t, h] + far


def per_device(
    latent_feat, norm_gain, conv_weight, rgb_weight, real_frames, disc_first, disc_second
):
    frames, height, width, chans = latent_feat.shape
    depth1, depth2 = disc_first.shape[1], disc_second.shape[1]
    cells = frames * width

    to_a, to_b, tail = local(
        act_kernel,
        (kept(frames, width, chans), kept(frames, width, chans), kept(2, 2, width, chans)),
        (latent_feat, norm_gain),
        hbm=(0, 1),
        scratch=[
            pltpu.VMEM(latent_feat.shape, BF16),
            pltpu.VMEM(norm_gain.shape, F32),
            pltpu.SemaphoreType.DMA((frames + 1,)),
        ],
    )
    past = onward(tail, "tm")
    from_b = swap(to_b, "rows", 1)
    from_a = swap(to_a, "rows", 0)

    line = 2 * width * chans * chans
    partial = kept(height, cells, 3 * chans, dtype=F32)
    held = kept(*conv_weight.shape)
    sums, some_taps = local(
        ahead_kernel,
        (partial, held),
        (to_a, to_b, conv_weight),
        hbm=(2,),
        scratch=[pltpu.VMEM((2, frames, width, chans), BF16), pltpu.SemaphoreType.DMA((27,))],
        flops=16 * 3 * line,
    )
    sums, weight = local(
        own_kernel,
        (partial, held),
        (to_a, to_b, past, conv_weight, some_taps, sums),
        hbm=(3,),
        scratch=[
            pltpu.VMEM((2, frames + 1, width, chans), BF16),
            pltpu.SemaphoreType.DMA((27,)),
        ],
        aliases={4: 1, 5: 0},
        flops=32 * 3 * line,
    )
    corner_a = onward(from_a[frames - 2 :], "tm")
    corner_b = onward(from_b[frames - 2 :], "tm")
    rest = (latent_feat, rgb_weight.T, real_frames)
    early = kept(2 * width, 3 * chans, dtype=F32)
    shown = (kept(frames, height, width, chans), kept(frames, height, 8, width))
    ends = []
    outs = ()
    for side, row in enumerate((from_a, from_b)):
        y, *outs = local(
            functools.partial(near_kernel, side),
            (early,) + shown,
            (row, weight, sums) + rest + tuple(outs),
            scratch=[pltpu.VMEM((cells, 3 * chans), F32)],
            aliases={6: 1, 7: 2} if side else {},
            flops=12 * 3 * line,
        )
        ends.append(y)
    for side, row in enumerate((corner_a, corner_b)):
        outs = local(
            functools.partial(corner_kernel, side),
            shown,
            (row, weight, ends[side]) + rest + tuple(outs),
            scratch=[pltpu.VMEM((2 * width, 3 * chans), F32)],
            aliases={6: 0, 7: 1},
            flops=4 * 3 * line,
        )
    decoded, colour = outs
    w2, w1 = local(
        prep_kernel,
        (kept(3 * depth2, 9 * depth1), kept(2 * depth1, 27 * 8)),
        (jnp.transpose(disc_second, (0, 2, 1)), jnp.transpose(disc_first, (2, 0, 1))),
    )

    side_b = swap(colour, "rows", 1)
    side_a = swap(colour, "rows", 0)
    ends = kept(2, height + 4, 8, width)
    for_a, for_b = local(pack_kernel, (ends, ends), (side_a, colour, side_b))
    time_b = swap(for_b, "tm", 1)
    time_a = swap(for_a, "tm", 0)

    match_map = local(
        disc_kernel,
        jax.ShapeDtypeStruct((frames, height, width), F32),
        (side_a, colour, side_b, time_a, time_b, w1, w2),
        scratch=[
            pltpu.VMEM((frames + 4, height + 4, 24, width), F32),
            pltpu.VMEM((frames + 2, height + 2, 2 * depth1, width), BF16),
        ],
    )
    return (decoded, match_map)


def solution(mesh):
    placed = (P("tm", "rows", None, None), P(), P(), P(), P(None, "tm", "rows", None), P(), P())
    return jax.shard_map(
        per_device,
        mesh=mesh,
        in_specs=placed,
        out_specs=(P("tm", "rows", None, None), P("tm", "rows", None)),
        check_vma=False,
    )
```

```python
import functools

import jax
import jax.numpy as jnp
from jax import lax
from jax.experimental import pallas as pl
from jax.experimental.pallas import tpu as pltpu
from jax.sharding import PartitionSpec as P


F32 = jnp.float32
BF16 = jnp.bfloat16
VMEM = pl.BlockSpec(memory_space=pltpu.VMEM)
HBM = pl.BlockSpec(memory_space=pltpu.HBM)
NT = (((1,), (1,)), ((), ()))


def pairs(count, first):
    route = []
    for i in range(first, count - 1, 2):
        route += [(i, i + 1), (i + 1, i)]
    return route


def swap(block, axis, first):
    return lax.ppermute(block, axis, pairs(lax.axis_size(axis), first))


def onward(block, axis):
    return lax.ppermute(block, axis, [(i, i + 1) for i in range(lax.axis_size(axis) - 1)])


def local(kernel, outs, args, scratch=(), aliases=None, flops=0, hbm=(), stored=(), limit=24):
    args = [
        pltpu.with_memory_space_constraint(a, pltpu.HBM if i in hbm else pltpu.VMEM)
        for i, a in enumerate(args)
    ]
    return pl.pallas_call(
        kernel,
        out_shape=outs,
        in_specs=[HBM if i in hbm else VMEM for i in range(len(args))],
        out_specs=tuple(HBM if i in stored else VMEM for i in range(len(outs)))
        if isinstance(outs, tuple)
        else VMEM,
        scratch_shapes=scratch,
        input_output_aliases=aliases or {},
        compiler_params=pltpu.CompilerParams(vmem_limit_bytes=limit << 20),
        cost_estimate=pl.CostEstimate(flops=flops, bytes_accessed=10**6, transcendentals=0),
    )(*args)


def kept(*dims, dtype=BF16):
    return pltpu.VMEM(dims, dtype)


def leaky(value):
    return jnp.maximum(value, 0.2 * value)


def act_kernel(feat_ref, gain_ref, to_a_ref, to_b_ref, tail_ref, feats_ref, scale_ref, sems):
    odd = lax.rem(lax.axis_index("rows"), 2)
    frames = feat_ref.shape[0]
    order = [frames - 2, frames - 1] + list(range(frames - 2))
    fetch_gain = pltpu.make_async_copy(gain_ref, scale_ref, sems.at[frames])
    fetch = [pltpu.make_async_copy(feat_ref.at[t], feats_ref.at[t], sems.at[t]) for t in range(frames)]
    fetch_gain.start()
    for t in order:
        fetch[t].start()
    fetch_gain.wait()
    gain = scale_ref[...]
    for t in order:
        fetch[t].wait()
        for k, (row, out_ref) in enumerate(((1 - odd, to_a_ref), (odd, to_b_ref))):
            feats = feats_ref[t, row].astype(F32)
            mean = jnp.mean(feats * feats, axis=-1, keepdims=True)
            normed = feats * lax.rsqrt(mean + 1e-06) * gain
            act = (normed * jax.nn.sigmoid(normed)).astype(BF16)
            out_ref[t] = act
            if t >= frames - 2:
                tail_ref[k, t - frames + 2] = act


def column_blocks(chans):
    return [(dw, off) for dw in range(3) for off in range(0, chans, 128)]


def rhs_block(w_ref, dw, off, taps):
    return jnp.concatenate([w_ref[9 * dt + 3 * dh + dw, :, off : off + 128] for dt, dh in taps], axis=0)


def start_taps(weight_ref, w_ref, sems, dw):
    for tap in range(dw, 27, 3):
        pltpu.make_async_copy(weight_ref.at[tap], w_ref.at[tap], sems.at[tap]).start()


def wait_taps(weight_ref, w_ref, sems, dw):
    for tap in range(dw, 27, 3):
        pltpu.make_async_copy(weight_ref.at[tap], w_ref.at[tap], sems.at[tap]).wait()


def fetch_kernel(weight_ref, w_ref, sems):
    start_taps(weight_ref, w_ref, sems, 0)
    wait_taps(weight_ref, w_ref, sems, 0)


def own_kernel(a_ref, b_ref, past_ref, weight_ref, some_ref, y_ref, w_ref, lines_ref, sems):
    odd = lax.rem(lax.axis_index("rows"), 2)
    frames, width, chans = a_ref.shape
    start_taps(weight_ref, w_ref, sems, 1)
    for k, (row, line_ref) in enumerate(((1 - odd, a_ref), (odd, b_ref))):
        lines_ref[row, pl.ds(0, 2)] = past_ref[k]
        lines_ref[row, pl.ds(2, frames)] = line_ref[...]
    inputs = [(dt, i) for dt in range(3) for i in range(2)]
    lhs = jnp.concatenate(
        [lines_ref[i, dt : dt + frames].reshape(frames * width, chans) for dt, i in inputs], axis=1
    )
    for dw in range(3):
        if dw:
            wait_taps(weight_ref, w_ref, sems, dw)
        if dw == 1:
            start_taps(weight_ref, w_ref, sems, 2)
        blocks = [(o, off) for o in range(2) for off in range(0, chans, 128)]
        for j in range(0, len(blocks), 2):
            pair = blocks[j : j + 2]
            rhs = [rhs_block(w_ref, dw, off, [(dt, i - o + 1) for dt, i in inputs]) for o, off in pair]
            got = jnp.dot(lhs, jnp.concatenate(rhs, axis=1), preferred_element_type=F32)
            for k, (o, off) in enumerate(pair):
                at = dw * chans + off
                y_ref[o, :, at : at + 128] = got[:, k * 128 : (k + 1) * 128]


def prep_kernel(d2_ref, d1_ref, decoded_ref, w2_ref, w1_ref, out_ref, sem):
    store = pltpu.make_async_copy(decoded_ref, out_ref, sem)
    store.start()
    depth1, depth2 = d2_ref.shape[1:]
    for dt in range(3):
        for dw in range(3):
            parts = [d2_ref[9 * dt + 3 * dh + dw].astype(F32) for dh in range(3)]
            parts.append(jnp.zeros((depth1, depth2), F32))
            for k in range(2):
                wide = jnp.concatenate(parts[2 * k : 2 * k + 2], axis=0)
                at = 4 * dt * depth1 + 2 * k * depth1
                w2_ref[dw * depth2 : (dw + 1) * depth2, at : at + 2 * depth1] = wide.T.astype(BF16)
    tap = lax.broadcasted_iota(jnp.int32, (27, 27 * 8), 0)
    place = lax.broadcasted_iota(jnp.int32, (27, 27 * 8), 1)
    for side in range(2):
        total = jnp.zeros((depth1, 27 * 8), F32)
        for c in range(3):
            pick = jnp.where(place == 8 * tap + 3 * side + c, 1.0, 0.0).astype(BF16)
            total = total + lax.dot_general(
                d1_ref[c], pick, (((0,), (0,)), ((), ())), preferred_element_type=F32
            )
        w1_ref[side * depth1 : (side + 1) * depth1] = total.astype(BF16)
    store.wait()


def finish(ys, feats, rgb, reals):
    width, chans = ys[1].shape
    col = lax.broadcasted_iota(jnp.int32, (width, chans), 0)
    total = (
        ys[1]
        + jnp.where(col == 0, 0.0, pltpu.roll(ys[0], 1, 0))
        + jnp.where(col == width - 1, 0.0, pltpu.roll(ys[2], width - 1, 0))
    )
    decoded = (feats.astype(F32) + total).astype(BF16)
    colour = lax.dot_general(rgb, decoded, NT, preferred_element_type=F32)
    both = jnp.concatenate(
        [colour.astype(BF16).astype(F32)]
        + [real.astype(F32) for real in reals]
        + [jnp.zeros((2, width), F32)],
        axis=0,
    )
    return decoded, both.astype(BF16)


def add_row(lhs, dts, row, w_ref, sums_ref, out_ref):
    chans = w_ref.shape[1]
    blocks = column_blocks(chans)
    for j in range(0, len(blocks), 2):
        some = blocks[j : j + 2]
        rhs = [rhs_block(w_ref, dw, off, [(dt, 2 * row) for dt in dts]) for dw, off in some]
        cols = slice(j * 128, (j + len(some)) * 128)
        out_ref[:, cols] = sums_ref[:, cols] + jnp.dot(
            lhs, rhs[0] if len(rhs) == 1 else jnp.concatenate(rhs, axis=1), preferred_element_type=F32
        )


def finish_row(ts, row, sums, feat_ref, rgb_ref, real_ref, decoded_ref, colour_ref):
    width, chans = feat_ref.shape[2:]
    for k, t in enumerate(ts):
        ys = [sums[k * width : (k + 1) * width, dw * chans : (dw + 1) * chans] for dw in range(3)]
        reals = []
        for c in range(3):
            both = real_ref[c, t].astype(F32)
            reals.append(jnp.where(row == 0, both[0:1], both[1:2]))
        decoded_ref[t, row], colour_ref[t, row] = finish(ys, feat_ref[t, row], rgb_ref[...], reals)


def side_row(side):
    odd = lax.rem(lax.axis_index("rows"), 2)
    return 1 - odd if side == 0 else odd


def near_kernel(side, line_ref, w_ref, sums_ref, feat_ref, rgb_ref, real_ref, *refs):
    y_ref, decoded_ref, colour_ref, all_ref = refs[-4:]
    row = side_row(side)
    frames, width, chans = line_ref.shape
    zeros = jnp.zeros((width, chans), BF16)
    line = [zeros, zeros] + [line_ref[t] for t in range(frames)]
    lhs = jnp.concatenate(
        [jnp.concatenate(line[dt : dt + frames], axis=0) for dt in range(3)], axis=1
    )
    add_row(lhs, range(3), row, w_ref, sums_ref.at[row], all_ref)
    y_ref[...] = all_ref[: 2 * width]
    late = range(2, frames)
    finish_row(
        late, row, all_ref.at[2 * width :], feat_ref, rgb_ref, real_ref, decoded_ref, colour_ref
    )


def corner_kernel(side, past_ref, w_ref, sums_ref, feat_ref, rgb_ref, real_ref, *refs):
    decoded_ref, colour_ref, all_ref = refs[-3:]
    row = side_row(side)
    width, chans = past_ref.shape[1:]
    lhs = jnp.concatenate(
        [
            jnp.concatenate([past_ref[0], past_ref[1]], axis=0),
            jnp.concatenate([past_ref[1], jnp.zeros((width, chans), BF16)], axis=0),
        ],
        axis=1,
    )
    add_row(lhs, range(2), row, w_ref, sums_ref, all_ref)
    finish_row(range(2), row, all_ref, feat_ref, rgb_ref, real_ref, decoded_ref, colour_ref)


def pack_kernel(a_ref, own_ref, b_ref, for_a_ref, for_b_ref):
    odd = lax.rem(lax.axis_index("tm"), 2)
    frames = own_ref.shape[0]
    for start, out_ref in (((frames - 2) * (1 - odd), for_a_ref), ((frames - 2) * odd, for_b_ref)):
        for k, ref in enumerate((a_ref, own_ref, b_ref)):
            out_ref[:, 2 * k : 2 * k + 2] = ref[pl.ds(start, 2)]


def put_line(x_ref, t, h, line):
    x = line.astype(F32)
    width = x.shape[1]
    col = lax.broadcasted_iota(jnp.int32, x.shape, 1)
    x_ref[t, h, 0:8] = jnp.where(col == 0, 0.0, pltpu.roll(x, 1, 1))
    x_ref[t, h, 8:16] = x
    x_ref[t, h, 16:24] = jnp.where(col == width - 1, 0.0, pltpu.roll(x, width - 1, 1))


def band_rows():
    odd = lax.rem(lax.axis_index("rows"), 2)
    return [4 * (1 - odd), 4 * (1 - odd) + 1, 2, 3, 4 * odd, 4 * odd + 1]


def first_layer(t, frames, x_ref, w1_ref, f_ref, near_ref):
    tm, band = lax.axis_index("tm"), lax.axis_index("rows")
    width = x_ref.shape[3]
    for h in range(0, 4, 2):
        cols = []
        for hh in (h, h + 1):
            cols.append(
                jnp.concatenate(
                    [x_ref[t + dt, hh + dh] for dt in range(3) for dh in range(3)], axis=0
                ).astype(BF16)
            )
        first = leaky(
            jnp.dot(w1_ref[...], jnp.concatenate(cols, axis=1), preferred_element_type=F32)
        )
        for i, hh in enumerate((h, h + 1)):
            part = first[:, i * width : (i + 1) * width]
            inside = []
            if t == 0:
                inside.append(tm > 0)
            if t == frames + 1:
                inside.append(tm < lax.axis_size("tm") - 1)
            if hh == 0:
                inside.append(band > 0)
            if hh == 3:
                inside.append(band < lax.axis_size("rows") - 1)
            if inside:
                keep = inside[0] if len(inside) == 1 else jnp.logical_and(*inside)
                part = jnp.where(keep, part, 0.0)
            part = part.astype(BF16)
            f_ref[t, hh] = part
            if 1 <= t <= frames and 1 <= hh <= 2:
                wide = part.astype(F32)
                half = wide.shape[0] // 2
                at = 2 * (t - 1) + hh - 1
                near_ref[at : at + 1] = jnp.mean(
                    jnp.abs(wide[:half] - wide[half:]), axis=0, keepdims=True
                )


def second_sums(t, h, dts, w2_ref, f_ref):
    half, width = f_ref.shape[2] // 2, f_ref.shape[3]
    zeros = jnp.zeros((half, width), BF16)
    sides = []
    for s in range(2):
        rows = []
        for dt in dts:
            rows += [f_ref[t + dt, h + dh, s * half : (s + 1) * half] for dh in range(3)] + [zeros]
        sides.append(jnp.concatenate(rows, axis=0))
    return jnp.dot(
        w2_ref[:, 4 * half * dts[0] : 4 * half * (dts[-1] + 1)],
        jnp.concatenate(sides, axis=1),
        preferred_element_type=F32,
    )


def inner_dts(t, frames):
    return [dt for dt in range(3) if 2 <= t + dt <= frames - 1]


def inner_kernel(a_ref, own_ref, b_ref, w1_ref, w2_ref, x_ref, f_ref, near_ref, part_ref):
    frames = own_ref.shape[0]
    rows = band_rows()
    for t in range(frames):
        for k in range(6):
            put_line(x_ref, t + 2, rows[k], (a_ref, own_ref, b_ref)[k // 2][t, k % 2])
    for t in range(2, frames):
        first_layer(t, frames, x_ref, w1_ref, f_ref, near_ref)
    for t in range(frames):
        for h in range(2):
            part_ref[2 * t + h] = second_sums(t, h, inner_dts(t, frames), w2_ref, f_ref)


def disc_kernel(
    ta_ref, tb_ref, w1_ref, w2_ref, part_ref, x_in, f_in, near_in, out_ref, x_ref, f_ref, near_ref
):
    odd = lax.rem(lax.axis_index("tm"), 2)
    frames, height, width = out_ref.shape
    rows = band_rows()
    for k in range(6):
        for t in range(2):
            put_line(x_ref, (frames + 2) * (1 - odd) + t, rows[k], ta_ref[t, k])
            put_line(x_ref, (frames + 2) * odd + t, rows[k], tb_ref[t, k])
    for t in (0, 1, frames, frames + 1):
        first_layer(t, frames, x_ref, w1_ref, f_ref, near_ref)
    depth2 = w2_ref.shape[0] // 3
    col = lax.broadcasted_iota(jnp.int32, (depth2, width), 1)
    for t in range(frames):
        dts = [dt for dt in range(3) if dt not in inner_dts(t, frames)]
        for h in range(height):
            y = part_ref[2 * t + h] + second_sums(t, h, dts, w2_ref, f_ref)
            outs = []
            for s in range(2):
                y0, y1, y2 = (
                    y[d * depth2 : (d + 1) * depth2, s * width : (s + 1) * width] for d in range(3)
                )
                total = (
                    y1
                    + jnp.where(col == 0, 0.0, pltpu.roll(y0, 1, 1))
                    + jnp.where(col == width - 1, 0.0, pltpu.roll(y2, width - 1, 1))
                )
                outs.append(leaky(total).astype(BF16).astype(F32))
            far = jnp.mean(jnp.abs(outs[0] - outs[1]), axis=0, keepdims=True)
            at = 2 * t + h
            out_ref[t, h : h + 1] = near_ref[at : at + 1] + far


def per_device(
    latent_feat, norm_gain, conv_weight, rgb_weight, real_frames, disc_first, disc_second
):
    frames, height, width, chans = latent_feat.shape
    depth1, depth2 = disc_first.shape[1], disc_second.shape[1]
    cells = frames * width

    to_a, to_b, tail = local(
        act_kernel,
        (kept(frames, width, chans), kept(frames, width, chans), kept(2, 2, width, chans)),
        (latent_feat, norm_gain),
        hbm=(0, 1),
        scratch=[
            pltpu.VMEM(latent_feat.shape, BF16),
            pltpu.VMEM(norm_gain.shape, F32),
            pltpu.SemaphoreType.DMA((frames + 1,)),
        ],
    )
    past = onward(tail, "tm")
    from_b = swap(to_b, "rows", 1)
    from_a = swap(to_a, "rows", 0)

    line = 2 * width * chans * chans
    first_taps = local(
        fetch_kernel,
        kept(*conv_weight.shape),
        (conv_weight,),
        hbm=(0,),
        scratch=[pltpu.SemaphoreType.DMA((27,))],
    )
    sums, weight = local(
        own_kernel,
        (kept(height, cells, 3 * chans, dtype=F32), kept(*conv_weight.shape)),
        (to_a, to_b, past, conv_weight, first_taps),
        hbm=(3,),
        scratch=[
            pltpu.VMEM((2, frames + 2, width, chans), BF16),
            pltpu.SemaphoreType.DMA((27,)),
        ],
        aliases={4: 1},
        flops=48 * 3 * line,
    )
    corner_a = onward(from_a[frames - 2 :], "tm")
    corner_b = onward(from_b[frames - 2 :], "tm")
    rest = (latent_feat, rgb_weight.T, real_frames)
    early = kept(2 * width, 3 * chans, dtype=F32)
    shown = (kept(frames, height, width, chans), kept(frames, height, 8, width))
    ends = []
    outs = ()
    for side, row in enumerate((from_a, from_b)):
        y, *outs = local(
            functools.partial(near_kernel, side),
            (early,) + shown,
            (row, weight, sums) + rest + tuple(outs),
            scratch=[pltpu.VMEM((cells, 3 * chans), F32)],
            aliases={6: 1, 7: 2} if side else {},
            flops=12 * 3 * line,
        )
        ends.append(y)
    for side, row in enumerate((corner_a, corner_b)):
        outs = local(
            functools.partial(corner_kernel, side),
            shown,
            (row, weight, ends[side]) + rest + tuple(outs),
            scratch=[pltpu.VMEM((2 * width, 3 * chans), F32)],
            aliases={6: 0, 7: 1},
            flops=4 * 3 * line,
        )
    decoded, colour = outs
    w2, w1, stored = local(
        prep_kernel,
        (
            kept(3 * depth2, 12 * depth1),
            kept(2 * depth1, 27 * 8),
            jax.ShapeDtypeStruct(decoded.shape, BF16),
        ),
        (jnp.transpose(disc_second, (0, 2, 1)), jnp.transpose(disc_first, (2, 0, 1)), decoded),
        stored=(2,),
        scratch=[pltpu.SemaphoreType.DMA],
    )

    side_b = swap(colour, "rows", 1)
    side_a = swap(colour, "rows", 0)
    ends = kept(2, height + 4, 8, width)
    for_a, for_b = local(pack_kernel, (ends, ends), (side_a, colour, side_b))
    time_b = swap(for_b, "tm", 1)
    time_a = swap(for_a, "tm", 0)

    inner = local(
        inner_kernel,
        (
            kept(frames + 4, height + 4, 24, width, dtype=F32),
            kept(frames + 2, height + 2, 2 * depth1, width),
            kept(frames * height, width, dtype=F32),
            kept(frames * height, 3 * depth2, 2 * width, dtype=F32),
        ),
        (side_a, colour, side_b, w1, w2),
    )
    match_map, *_ = local(
        disc_kernel,
        (jax.ShapeDtypeStruct((frames, height, width), F32),)
        + tuple(kept(*x.shape, dtype=x.dtype) for x in inner[:3]),
        (time_a, time_b, w1, w2, inner[3]) + tuple(inner[:3]),
        aliases={5: 1, 6: 2, 7: 3},
    )
    return (stored, match_map)


def solution(mesh):
    placed = (P("tm", "rows", None, None), P(), P(), P(), P(None, "tm", "rows", None), P(), P())
    return jax.shard_map(
        per_device,
        mesh=mesh,
        in_specs=placed,
        out_specs=(P("tm", "rows", None, None), P("tm", "rows", None)),
        check_vma=False,
    )
```

```python
import functools

import jax
import jax.numpy as jnp
from jax import lax
from jax.experimental import pallas as pl
from jax.experimental.pallas import tpu as pltpu
from jax.sharding import PartitionSpec as P


F32 = jnp.float32
BF16 = jnp.bfloat16
VMEM = pl.BlockSpec(memory_space=pltpu.VMEM)
HBM = pl.BlockSpec(memory_space=pltpu.HBM)
NT = (((1,), (1,)), ((), ()))


def pairs(count, first):
    route = []
    for i in range(first, count - 1, 2):
        route += [(i, i + 1), (i + 1, i)]
    return route


def swap(block, axis, first):
    return lax.ppermute(block, axis, pairs(lax.axis_size(axis), first))


def onward(block, axis):
    return lax.ppermute(block, axis, [(i, i + 1) for i in range(lax.axis_size(axis) - 1)])


def local(kernel, outs, args, scratch=(), aliases=None, flops=0, hbm=(), stored=(), limit=24):
    args = [
        pltpu.with_memory_space_constraint(a, pltpu.HBM if i in hbm else pltpu.VMEM)
        for i, a in enumerate(args)
    ]
    return pl.pallas_call(
        kernel,
        out_shape=outs,
        in_specs=[HBM if i in hbm else VMEM for i in range(len(args))],
        out_specs=tuple(HBM if i in stored else VMEM for i in range(len(outs)))
        if isinstance(outs, tuple)
        else VMEM,
        scratch_shapes=scratch,
        input_output_aliases=aliases or {},
        compiler_params=pltpu.CompilerParams(vmem_limit_bytes=limit << 20),
        cost_estimate=pl.CostEstimate(flops=flops, bytes_accessed=10**6, transcendentals=0),
    )(*args)


def kept(*dims, dtype=BF16):
    return pltpu.VMEM(dims, dtype)


def leaky(value):
    return jnp.maximum(value, 0.2 * value)


def act_kernel(feat_ref, gain_ref, to_a_ref, to_b_ref, tail_ref, feats_ref, scale_ref, sems):
    odd = lax.rem(lax.axis_index("rows"), 2)
    frames = feat_ref.shape[0]
    order = [frames - 2, frames - 1] + list(range(frames - 2))
    fetch_gain = pltpu.make_async_copy(gain_ref, scale_ref, sems.at[frames])
    fetch = [pltpu.make_async_copy(feat_ref.at[t], feats_ref.at[t], sems.at[t]) for t in range(frames)]
    fetch_gain.start()
    for t in order:
        fetch[t].start()
    fetch_gain.wait()
    gain = scale_ref[...]
    for t in order:
        fetch[t].wait()
        for k, (row, out_ref) in enumerate(((1 - odd, to_a_ref), (odd, to_b_ref))):
            feats = feats_ref[t, row].astype(F32)
            mean = jnp.mean(feats * feats, axis=-1, keepdims=True)
            normed = feats * lax.rsqrt(mean + 1e-06) * gain
            act = (normed * jax.nn.sigmoid(normed)).astype(BF16)
            out_ref[t] = act
            if t >= frames - 2:
                tail_ref[k, t - frames + 2] = act


def column_blocks(chans):
    return [(dw, off) for dw in range(3) for off in range(0, chans, 128)]


def rhs_block(w_ref, dw, off, taps):
    return jnp.concatenate([w_ref[9 * dt + 3 * dh + dw, :, off : off + 128] for dt, dh in taps], axis=0)


def own_kernel(lines_ref, past_ref, w_ref, y_ref):
    odd = lax.rem(lax.axis_index("rows"), 2)
    frames, _, chans = lines_ref.shape[1:]
    past = [past_ref[lax.rem(1 + i + odd, 2)] for i in range(2)]
    inputs = [(dt, i) for dt in range(3) for i in range(2)]
    parts = []
    for dt, i in inputs:
        part = [past[i][dt:].reshape(-1, chans)] if dt < 2 else []
        part.append(lines_ref[i, : frames - 2 + dt].reshape(-1, chans))
        parts.append(jnp.concatenate(part, axis=0))
    lhs = jnp.concatenate(parts, axis=1)
    blocks = [(o, off) for o in range(2) for off in range(0, chans, 128)]
    for dw in range(3):
        for j in range(0, len(blocks), 2):
            pair = blocks[j : j + 2]
            rhs = [rhs_block(w_ref, dw, off, [(dt, i - o + 1) for dt, i in inputs]) for o, off in pair]
            got = jnp.dot(lhs, jnp.concatenate(rhs, axis=1), preferred_element_type=F32)
            for k, (o, off) in enumerate(pair):
                at = dw * chans + off
                y_ref[o, :, at : at + 128] = got[:, k * 128 : (k + 1) * 128]


def store_kernel(decoded_ref, out_ref, sem):
    store = pltpu.make_async_copy(decoded_ref, out_ref, sem)
    store.start()
    store.wait()


def prep_kernel(a_ref, b_ref, d2_ref, d1_ref, lines_ref, w2_ref, w1_ref):
    odd = lax.rem(lax.axis_index("rows"), 2)
    lines_ref[1 - odd] = a_ref[...]
    lines_ref[odd] = b_ref[...]
    depth1, depth2 = d2_ref.shape[1:]
    for dt in range(3):
        for dw in range(3):
            parts = [d2_ref[9 * dt + 3 * dh + dw].astype(F32) for dh in range(3)]
            parts.append(jnp.zeros((depth1, depth2), F32))
            for k in range(2):
                wide = jnp.concatenate(parts[2 * k : 2 * k + 2], axis=0)
                at = 4 * dt * depth1 + 2 * k * depth1
                w2_ref[dw * depth2 : (dw + 1) * depth2, at : at + 2 * depth1] = wide.T.astype(BF16)
    tap = lax.broadcasted_iota(jnp.int32, (27, 27 * 8), 0)
    place = lax.broadcasted_iota(jnp.int32, (27, 27 * 8), 1)
    for side in range(2):
        total = jnp.zeros((depth1, 27 * 8), F32)
        for c in range(3):
            pick = jnp.where(place == 8 * tap + 3 * side + c, 1.0, 0.0).astype(BF16)
            total = total + lax.dot_general(
                d1_ref[c], pick, (((0,), (0,)), ((), ())), preferred_element_type=F32
            )
        w1_ref[side * depth1 : (side + 1) * depth1] = total.astype(BF16)


def finish(ys, feats, rgb, reals):
    width, chans = ys[1].shape
    col = lax.broadcasted_iota(jnp.int32, (width, chans), 0)
    total = (
        ys[1]
        + jnp.where(col == 0, 0.0, pltpu.roll(ys[0], 1, 0))
        + jnp.where(col == width - 1, 0.0, pltpu.roll(ys[2], width - 1, 0))
    )
    decoded = (feats.astype(F32) + total).astype(BF16)
    colour = lax.dot_general(rgb, decoded, NT, preferred_element_type=F32)
    both = jnp.concatenate(
        [colour.astype(BF16).astype(F32)]
        + [real.astype(F32) for real in reals]
        + [jnp.zeros((2, width), F32)],
        axis=0,
    )
    return decoded, both.astype(BF16)


def add_row(lhs, dts, row, w_ref, sums_ref, out_ref):
    chans = w_ref.shape[1]
    blocks = column_blocks(chans)
    for j in range(0, len(blocks), 2):
        some = blocks[j : j + 2]
        rhs = [rhs_block(w_ref, dw, off, [(dt, 2 * row) for dt in dts]) for dw, off in some]
        cols = slice(j * 128, (j + len(some)) * 128)
        out_ref[:, cols] = sums_ref[:, cols] + jnp.dot(
            lhs, rhs[0] if len(rhs) == 1 else jnp.concatenate(rhs, axis=1), preferred_element_type=F32
        )


def finish_row(ts, row, sums, feat_ref, rgb_ref, real_ref, decoded_ref, colour_ref):
    width, chans = feat_ref.shape[2:]
    for k, t in enumerate(ts):
        ys = [sums[k * width : (k + 1) * width, dw * chans : (dw + 1) * chans] for dw in range(3)]
        reals = []
        for c in range(3):
            both = real_ref[c, t].astype(F32)
            reals.append(jnp.where(row == 0, both[0:1], both[1:2]))
        decoded_ref[t, row], colour_ref[t, row] = finish(ys, feat_ref[t, row], rgb_ref[...], reals)


def side_row(side):
    odd = lax.rem(lax.axis_index("rows"), 2)
    return 1 - odd if side == 0 else odd


def near_kernel(side, line_ref, w_ref, sums_ref, feat_ref, rgb_ref, real_ref, *refs):
    y_ref, decoded_ref, colour_ref, all_ref = refs[-4:]
    row = side_row(side)
    frames, width, chans = line_ref.shape
    zeros = jnp.zeros((width, chans), BF16)
    line = [zeros, zeros] + [line_ref[t] for t in range(frames)]
    lhs = jnp.concatenate(
        [jnp.concatenate(line[dt : dt + frames], axis=0) for dt in range(3)], axis=1
    )
    add_row(lhs, range(3), row, w_ref, sums_ref.at[row], all_ref)
    y_ref[...] = all_ref[: 2 * width]
    late = range(2, frames)
    finish_row(
        late, row, all_ref.at[2 * width :], feat_ref, rgb_ref, real_ref, decoded_ref, colour_ref
    )


def corner_kernel(side, past_ref, w_ref, sums_ref, feat_ref, rgb_ref, real_ref, *refs):
    decoded_ref, colour_ref, all_ref = refs[-3:]
    row = side_row(side)
    width, chans = past_ref.shape[1:]
    lhs = jnp.concatenate(
        [
            jnp.concatenate([past_ref[0], past_ref[1]], axis=0),
            jnp.concatenate([past_ref[1], jnp.zeros((width, chans), BF16)], axis=0),
        ],
        axis=1,
    )
    add_row(lhs, range(2), row, w_ref, sums_ref, all_ref)
    finish_row(range(2), row, all_ref, feat_ref, rgb_ref, real_ref, decoded_ref, colour_ref)


def pack_kernel(a_ref, own_ref, b_ref, for_a_ref, for_b_ref):
    odd = lax.rem(lax.axis_index("tm"), 2)
    frames = own_ref.shape[0]
    for start, out_ref in (((frames - 2) * (1 - odd), for_a_ref), ((frames - 2) * odd, for_b_ref)):
        for k, ref in enumerate((a_ref, own_ref, b_ref)):
            out_ref[:, 2 * k : 2 * k + 2] = ref[pl.ds(start, 2)]


def put_line(x_ref, t, h, line):
    x = line.astype(F32)
    width = x.shape[1]
    col = lax.broadcasted_iota(jnp.int32, x.shape, 1)
    x_ref[t, h, 0:8] = jnp.where(col == 0, 0.0, pltpu.roll(x, 1, 1))
    x_ref[t, h, 8:16] = x
    x_ref[t, h, 16:24] = jnp.where(col == width - 1, 0.0, pltpu.roll(x, width - 1, 1))


def band_rows():
    odd = lax.rem(lax.axis_index("rows"), 2)
    return [4 * (1 - odd), 4 * (1 - odd) + 1, 2, 3, 4 * odd, 4 * odd + 1]


def first_layer(t, frames, x_ref, w1_ref, f_ref, near_ref):
    tm, band = lax.axis_index("tm"), lax.axis_index("rows")
    width = x_ref.shape[3]
    for h in range(0, 4, 2):
        cols = []
        for hh in (h, h + 1):
            cols.append(
                jnp.concatenate(
                    [x_ref[t + dt, hh + dh] for dt in range(3) for dh in range(3)], axis=0
                ).astype(BF16)
            )
        first = leaky(
            jnp.dot(w1_ref[...], jnp.concatenate(cols, axis=1), preferred_element_type=F32)
        )
        for i, hh in enumerate((h, h + 1)):
            part = first[:, i * width : (i + 1) * width]
            inside = []
            if t == 0:
                inside.append(tm > 0)
            if t == frames + 1:
                inside.append(tm < lax.axis_size("tm") - 1)
            if hh == 0:
                inside.append(band > 0)
            if hh == 3:
                inside.append(band < lax.axis_size("rows") - 1)
            if inside:
                keep = inside[0] if len(inside) == 1 else jnp.logical_and(*inside)
                part = jnp.where(keep, part, 0.0)
            part = part.astype(BF16)
            f_ref[t, hh] = part
            if 1 <= t <= frames and 1 <= hh <= 2:
                wide = part.astype(F32)
                half = wide.shape[0] // 2
                at = 2 * (t - 1) + hh - 1
                near_ref[at : at + 1] = jnp.mean(
                    jnp.abs(wide[:half] - wide[half:]), axis=0, keepdims=True
                )


def second_sums(t, h, dts, w2_ref, f_ref):
    half, width = f_ref.shape[2] // 2, f_ref.shape[3]
    zeros = jnp.zeros((half, width), BF16)
    sides = []
    for s in range(2):
        rows = []
        for dt in dts:
            rows += [f_ref[t + dt, h + dh, s * half : (s + 1) * half] for dh in range(3)] + [zeros]
        sides.append(jnp.concatenate(rows, axis=0))
    return jnp.dot(
        w2_ref[:, 4 * half * dts[0] : 4 * half * (dts[-1] + 1)],
        jnp.concatenate(sides, axis=1),
        preferred_element_type=F32,
    )


def inner_dts(t, frames):
    return [dt for dt in range(3) if 2 <= t + dt <= frames - 1]


def inner_kernel(a_ref, own_ref, b_ref, w1_ref, w2_ref, x_ref, f_ref, near_ref, part_ref):
    frames = own_ref.shape[0]
    rows = band_rows()
    for t in range(frames):
        for k in range(6):
            put_line(x_ref, t + 2, rows[k], (a_ref, own_ref, b_ref)[k // 2][t, k % 2])
    for t in range(2, frames):
        first_layer(t, frames, x_ref, w1_ref, f_ref, near_ref)
    for t in range(frames):
        for h in range(2):
            part_ref[2 * t + h] = second_sums(t, h, inner_dts(t, frames), w2_ref, f_ref)


def disc_kernel(
    ta_ref, tb_ref, w1_ref, w2_ref, part_ref, x_in, f_in, near_in, out_ref, x_ref, f_ref, near_ref
):
    odd = lax.rem(lax.axis_index("tm"), 2)
    frames, height, width = out_ref.shape
    rows = band_rows()
    for k in range(6):
        for t in range(2):
            put_line(x_ref, (frames + 2) * (1 - odd) + t, rows[k], ta_ref[t, k])
            put_line(x_ref, (frames + 2) * odd + t, rows[k], tb_ref[t, k])
    for t in (0, 1, frames, frames + 1):
        first_layer(t, frames, x_ref, w1_ref, f_ref, near_ref)
    depth2 = w2_ref.shape[0] // 3
    col = lax.broadcasted_iota(jnp.int32, (depth2, width), 1)
    for t in range(frames):
        dts = [dt for dt in range(3) if dt not in inner_dts(t, frames)]
        for h in range(height):
            y = part_ref[2 * t + h] + second_sums(t, h, dts, w2_ref, f_ref)
            outs = []
            for s in range(2):
                y0, y1, y2 = (
                    y[d * depth2 : (d + 1) * depth2, s * width : (s + 1) * width] for d in range(3)
                )
                total = (
                    y1
                    + jnp.where(col == 0, 0.0, pltpu.roll(y0, 1, 1))
                    + jnp.where(col == width - 1, 0.0, pltpu.roll(y2, width - 1, 1))
                )
                outs.append(leaky(total).astype(BF16).astype(F32))
            far = jnp.mean(jnp.abs(outs[0] - outs[1]), axis=0, keepdims=True)
            at = 2 * t + h
            out_ref[t, h : h + 1] = near_ref[at : at + 1] + far


def per_device(
    latent_feat, norm_gain, conv_weight, rgb_weight, real_frames, disc_first, disc_second
):
    frames, height, width, chans = latent_feat.shape
    depth1, depth2 = disc_first.shape[1], disc_second.shape[1]
    cells = frames * width

    to_a, to_b, tail = local(
        act_kernel,
        (kept(frames, width, chans), kept(frames, width, chans), kept(2, 2, width, chans)),
        (latent_feat, norm_gain),
        hbm=(0, 1),
        scratch=[
            pltpu.VMEM(latent_feat.shape, BF16),
            pltpu.VMEM(norm_gain.shape, F32),
            pltpu.SemaphoreType.DMA((frames + 1,)),
        ],
    )
    past = onward(tail, "tm")
    from_b = swap(to_b, "rows", 1)
    from_a = swap(to_a, "rows", 0)

    line = 2 * width * chans * chans
    lines, w2, w1 = local(
        prep_kernel,
        (
            kept(height, frames, width, chans),
            kept(3 * depth2, 12 * depth1),
            kept(2 * depth1, 27 * 8),
        ),
        (to_a, to_b, jnp.transpose(disc_second, (0, 2, 1)), jnp.transpose(disc_first, (2, 0, 1))),
        flops=40 * 3 * line,
    )
    sums = local(
        own_kernel,
        kept(height, cells, 3 * chans, dtype=F32),
        (lines, past, conv_weight),
        flops=48 * 3 * line,
    )
    corner_a = onward(from_a[frames - 2 :], "tm")
    corner_b = onward(from_b[frames - 2 :], "tm")
    rest = (latent_feat, rgb_weight.T, real_frames)
    early = kept(2 * width, 3 * chans, dtype=F32)
    shown = (kept(frames, height, width, chans), kept(frames, height, 8, width))
    ends = []
    outs = ()
    for side, row in enumerate((from_a, from_b)):
        y, *outs = local(
            functools.partial(near_kernel, side),
            (early,) + shown,
            (row, conv_weight, sums) + rest + tuple(outs),
            scratch=[pltpu.VMEM((cells, 3 * chans), F32)],
            aliases={6: 1, 7: 2} if side else {},
            flops=12 * 3 * line,
        )
        ends.append(y)
    for side, row in enumerate((corner_a, corner_b)):
        outs = local(
            functools.partial(corner_kernel, side),
            shown,
            (row, conv_weight, ends[side]) + rest + tuple(outs),
            scratch=[pltpu.VMEM((2 * width, 3 * chans), F32)],
            aliases={6: 0, 7: 1},
            flops=4 * 3 * line,
        )
    decoded, colour = outs
    stored, = local(
        store_kernel,
        (jax.ShapeDtypeStruct(decoded.shape, BF16),),
        (decoded,),
        stored=(0,),
        scratch=[pltpu.SemaphoreType.DMA],
    )

    side_b = swap(colour, "rows", 1)
    side_a = swap(colour, "rows", 0)
    ends = kept(2, height + 4, 8, width)
    for_a, for_b = local(pack_kernel, (ends, ends), (side_a, colour, side_b))
    time_b = swap(for_b, "tm", 1)
    time_a = swap(for_a, "tm", 0)

    inner = local(
        inner_kernel,
        (
            kept(frames + 4, height + 4, 24, width, dtype=F32),
            kept(frames + 2, height + 2, 2 * depth1, width),
            kept(frames * height, width, dtype=F32),
            kept(frames * height, 3 * depth2, 2 * width, dtype=F32),
        ),
        (side_a, colour, side_b, w1, w2),
    )
    match_map, *_ = local(
        disc_kernel,
        (jax.ShapeDtypeStruct((frames, height, width), F32),)
        + tuple(kept(*x.shape, dtype=x.dtype) for x in inner[:3]),
        (time_a, time_b, w1, w2, inner[3]) + tuple(inner[:3]),
        aliases={5: 1, 6: 2, 7: 3},
    )
    return (stored, match_map)


def solution(mesh):
    placed = (P("tm", "rows", None, None), P(), P(), P(), P(None, "tm", "rows", None), P(), P())
    return jax.shard_map(
        per_device,
        mesh=mesh,
        in_specs=placed,
        out_specs=(P("tm", "rows", None, None), P("tm", "rows", None)),
        check_vma=False,
    )
```

```python
import functools

import jax
import jax.numpy as jnp
from jax import lax
from jax.experimental import pallas as pl
from jax.experimental.pallas import tpu as pltpu
from jax.sharding import PartitionSpec as P


F32 = jnp.float32
BF16 = jnp.bfloat16
VMEM = pl.BlockSpec(memory_space=pltpu.VMEM)
HBM = pl.BlockSpec(memory_space=pltpu.HBM)
NT = (((1,), (1,)), ((), ()))


def pairs(count, first):
    route = []
    for i in range(first, count - 1, 2):
        route += [(i, i + 1), (i + 1, i)]
    return route


def swap(block, axis, first):
    return lax.ppermute(block, axis, pairs(lax.axis_size(axis), first))


def onward(block, axis):
    return lax.ppermute(block, axis, [(i, i + 1) for i in range(lax.axis_size(axis) - 1)])


def local(kernel, outs, args, scratch=(), aliases=None, flops=0, hbm=(), stored=(), limit=24):
    args = [
        pltpu.with_memory_space_constraint(a, pltpu.HBM if i in hbm else pltpu.VMEM)
        for i, a in enumerate(args)
    ]
    return pl.pallas_call(
        kernel,
        out_shape=outs,
        in_specs=[HBM if i in hbm else VMEM for i in range(len(args))],
        out_specs=tuple(HBM if i in stored else VMEM for i in range(len(outs)))
        if isinstance(outs, tuple)
        else VMEM,
        scratch_shapes=scratch,
        input_output_aliases=aliases or {},
        compiler_params=pltpu.CompilerParams(vmem_limit_bytes=limit << 20),
        cost_estimate=pl.CostEstimate(flops=flops, bytes_accessed=10**6, transcendentals=0),
    )(*args)


def kept(*dims, dtype=BF16):
    return pltpu.VMEM(dims, dtype)


def leaky(value):
    return jnp.maximum(value, 0.2 * value)


def act_kernel(feat_ref, gain_ref, to_a_ref, to_b_ref, tail_ref, feats_ref, scale_ref, sems):
    odd = lax.rem(lax.axis_index("rows"), 2)
    frames = feat_ref.shape[0]
    order = [frames - 2, frames - 1] + list(range(frames - 2))
    fetch_gain = pltpu.make_async_copy(gain_ref, scale_ref, sems.at[frames])
    fetch = [pltpu.make_async_copy(feat_ref.at[t], feats_ref.at[t], sems.at[t]) for t in range(frames)]
    fetch_gain.start()
    for t in order:
        fetch[t].start()
    fetch_gain.wait()
    gain = scale_ref[...]
    for t in order:
        fetch[t].wait()
        for k, (row, out_ref) in enumerate(((1 - odd, to_a_ref), (odd, to_b_ref))):
            feats = feats_ref[t, row].astype(F32)
            mean = jnp.mean(feats * feats, axis=-1, keepdims=True)
            normed = feats * lax.rsqrt(mean + 1e-06) * gain
            act = (normed * jax.nn.sigmoid(normed)).astype(BF16)
            out_ref[t] = act
            if t >= frames - 2:
                tail_ref[k, t - frames + 2] = act


def column_blocks(chans):
    return [(dw, off) for dw in range(3) for off in range(0, chans, 128)]


def rhs_block(w_ref, dw, off, taps):
    return jnp.concatenate([w_ref[9 * dt + 3 * dh + dw, :, off : off + 128] for dt, dh in taps], axis=0)


def own_kernel(lines_ref, past_ref, w_ref, y_ref):
    odd = lax.rem(lax.axis_index("rows"), 2)
    frames, _, chans = lines_ref.shape[1:]
    past = [past_ref[lax.rem(1 + i + odd, 2)] for i in range(2)]
    inputs = [(dt, i) for dt in range(3) for i in range(2)]
    parts = []
    for dt, i in inputs:
        part = [past[i][dt:].reshape(-1, chans)] if dt < 2 else []
        part.append(lines_ref[i, : frames - 2 + dt].reshape(-1, chans))
        parts.append(jnp.concatenate(part, axis=0))
    lhs = jnp.concatenate(parts, axis=1)
    blocks = [(o, off) for o in range(2) for off in range(0, chans, 128)]
    for dw in range(3):
        for j in range(0, len(blocks), 2):
            pair = blocks[j : j + 2]
            rhs = [rhs_block(w_ref, dw, off, [(dt, i - o + 1) for dt, i in inputs]) for o, off in pair]
            got = jnp.dot(lhs, jnp.concatenate(rhs, axis=1), preferred_element_type=F32)
            for k, (o, off) in enumerate(pair):
                at = dw * chans + off
                y_ref[o, :, at : at + 128] = got[:, k * 128 : (k + 1) * 128]


def store_kernel(decoded_ref, out_ref, sem):
    store = pltpu.make_async_copy(decoded_ref, out_ref, sem)
    store.start()
    store.wait()


def prep_kernel(
    a_ref, b_ref, second_ref, first_ref, lines_ref, w2_ref, w1_ref, d2_ref, d1_ref, sems
):
    loads = [
        pltpu.make_async_copy(second_ref, d2_ref, sems.at[0]),
        pltpu.make_async_copy(first_ref, d1_ref, sems.at[1]),
    ]
    for load in loads:
        load.start()
    odd = lax.rem(lax.axis_index("rows"), 2)
    lines_ref[1 - odd] = a_ref[...]
    lines_ref[odd] = b_ref[...]
    for load in loads:
        load.wait()
    depth1, depth2 = d2_ref.shape[1:]
    for dt in range(3):
        for dw in range(3):
            parts = [d2_ref[9 * dt + 3 * dh + dw].astype(F32) for dh in range(3)]
            parts.append(jnp.zeros((depth1, depth2), F32))
            for k in range(2):
                wide = jnp.concatenate(parts[2 * k : 2 * k + 2], axis=0)
                at = 4 * dt * depth1 + 2 * k * depth1
                w2_ref[dw * depth2 : (dw + 1) * depth2, at : at + 2 * depth1] = wide.T.astype(BF16)
    tap = lax.broadcasted_iota(jnp.int32, (27, 27 * 8), 0)
    place = lax.broadcasted_iota(jnp.int32, (27, 27 * 8), 1)
    for side in range(2):
        total = jnp.zeros((depth1, 27 * 8), F32)
        for c in range(3):
            pick = jnp.where(place == 8 * tap + 3 * side + c, 1.0, 0.0).astype(BF16)
            total = total + lax.dot_general(
                d1_ref[c], pick, (((0,), (0,)), ((), ())), preferred_element_type=F32
            )
        w1_ref[side * depth1 : (side + 1) * depth1] = total.astype(BF16)


def finish(ys, feats, rgb, reals):
    width, chans = ys[1].shape
    col = lax.broadcasted_iota(jnp.int32, (width, chans), 0)
    total = (
        ys[1]
        + jnp.where(col == 0, 0.0, pltpu.roll(ys[0], 1, 0))
        + jnp.where(col == width - 1, 0.0, pltpu.roll(ys[2], width - 1, 0))
    )
    decoded = (feats.astype(F32) + total).astype(BF16)
    colour = lax.dot_general(rgb, decoded, NT, preferred_element_type=F32)
    both = jnp.concatenate(
        [colour.astype(BF16).astype(F32)]
        + [real.astype(F32) for real in reals]
        + [jnp.zeros((2, width), F32)],
        axis=0,
    )
    return decoded, both.astype(BF16)


def finish_row(ts, row, sums, feat_ref, rgb_ref, real_ref, decoded_ref, colour_ref):
    width, chans = feat_ref.shape[2:]
    for k, t in enumerate(ts):
        ys = [sums[k * width : (k + 1) * width, dw * chans : (dw + 1) * chans] for dw in range(3)]
        reals = []
        for c in range(3):
            both = real_ref[c, t].astype(F32)
            reals.append(jnp.where(row == 0, both[0:1], both[1:2]))
        decoded_ref[t, row], colour_ref[t, row] = finish(ys, feat_ref[t, row], rgb_ref[...], reals)


def near_kernel(side, line_ref, past_ref, w_ref, sums_ref, feat_ref, rgb_ref, real_ref, *refs):
    decoded_ref, colour_ref, all_ref = refs[-3:]
    odd = lax.rem(lax.axis_index("rows"), 2)
    row = 1 - odd if side == 0 else odd
    frames, _, chans = line_ref.shape
    line = [past_ref[0], past_ref[1]] + [line_ref[t] for t in range(frames)]
    lhs = jnp.concatenate(
        [jnp.concatenate(line[dt : dt + frames], axis=0) for dt in range(3)], axis=1
    )
    blocks = column_blocks(chans)
    for j in range(0, len(blocks), 2):
        some = blocks[j : j + 2]
        rhs = [rhs_block(w_ref, dw, off, [(dt, 2 * row) for dt in range(3)]) for dw, off in some]
        cols = slice(j * 128, (j + len(some)) * 128)
        all_ref[:, cols] = sums_ref[row, :, cols] + jnp.dot(
            lhs, rhs[0] if len(rhs) == 1 else jnp.concatenate(rhs, axis=1), preferred_element_type=F32
        )
    finish_row(
        range(frames), row, all_ref, feat_ref, rgb_ref, real_ref, decoded_ref, colour_ref
    )


def pack_kernel(a_ref, own_ref, b_ref, for_a_ref, for_b_ref):
    odd = lax.rem(lax.axis_index("tm"), 2)
    frames = own_ref.shape[0]
    for start, out_ref in (((frames - 2) * (1 - odd), for_a_ref), ((frames - 2) * odd, for_b_ref)):
        for k, ref in enumerate((a_ref, own_ref, b_ref)):
            out_ref[:, 2 * k : 2 * k + 2] = ref[pl.ds(start, 2)]


def put_line(x_ref, t, h, line):
    x = line.astype(F32)
    width = x.shape[1]
    col = lax.broadcasted_iota(jnp.int32, x.shape, 1)
    x_ref[t, h, 0:8] = jnp.where(col == 0, 0.0, pltpu.roll(x, 1, 1))
    x_ref[t, h, 8:16] = x
    x_ref[t, h, 16:24] = jnp.where(col == width - 1, 0.0, pltpu.roll(x, width - 1, 1))


def band_rows():
    odd = lax.rem(lax.axis_index("rows"), 2)
    return [4 * (1 - odd), 4 * (1 - odd) + 1, 2, 3, 4 * odd, 4 * odd + 1]


def first_layer(t, frames, x_ref, w1_ref, f_ref, near_ref):
    tm, band = lax.axis_index("tm"), lax.axis_index("rows")
    width = x_ref.shape[3]
    for h in range(0, 4, 2):
        cols = []
        for hh in (h, h + 1):
            cols.append(
                jnp.concatenate(
                    [x_ref[t + dt, hh + dh] for dt in range(3) for dh in range(3)], axis=0
                ).astype(BF16)
            )
        first = leaky(
            jnp.dot(w1_ref[...], jnp.concatenate(cols, axis=1), preferred_element_type=F32)
        )
        for i, hh in enumerate((h, h + 1)):
            part = first[:, i * width : (i + 1) * width]
            inside = []
            if t == 0:
                inside.append(tm > 0)
            if t == frames + 1:
                inside.append(tm < lax.axis_size("tm") - 1)
            if hh == 0:
                inside.append(band > 0)
            if hh == 3:
                inside.append(band < lax.axis_size("rows") - 1)
            if inside:
                keep = inside[0] if len(inside) == 1 else jnp.logical_and(*inside)
                part = jnp.where(keep, part, 0.0)
            part = part.astype(BF16)
            f_ref[t, hh] = part
            if 1 <= t <= frames and 1 <= hh <= 2:
                wide = part.astype(F32)
                half = wide.shape[0] // 2
                at = 2 * (t - 1) + hh - 1
                near_ref[at : at + 1] = jnp.mean(
                    jnp.abs(wide[:half] - wide[half:]), axis=0, keepdims=True
                )


def second_sums(t, h, dts, w2_ref, f_ref):
    half, width = f_ref.shape[2] // 2, f_ref.shape[3]
    zeros = jnp.zeros((half, width), BF16)
    sides = []
    for s in range(2):
        rows = []
        for dt in dts:
            rows += [f_ref[t + dt, h + dh, s * half : (s + 1) * half] for dh in range(3)] + [zeros]
        sides.append(jnp.concatenate(rows, axis=0))
    return jnp.dot(
        w2_ref[:, 4 * half * dts[0] : 4 * half * (dts[-1] + 1)],
        jnp.concatenate(sides, axis=1),
        preferred_element_type=F32,
    )


def inner_dts(t, frames):
    return [dt for dt in range(3) if 2 <= t + dt <= frames - 1]


def inner_kernel(a_ref, own_ref, b_ref, w1_ref, w2_ref, x_ref, f_ref, near_ref, part_ref):
    frames = own_ref.shape[0]
    rows = band_rows()
    for t in range(frames):
        for k in range(6):
            put_line(x_ref, t + 2, rows[k], (a_ref, own_ref, b_ref)[k // 2][t, k % 2])
    for t in range(2, frames):
        first_layer(t, frames, x_ref, w1_ref, f_ref, near_ref)
    for t in range(frames):
        for h in range(2):
            part_ref[2 * t + h] = second_sums(t, h, inner_dts(t, frames), w2_ref, f_ref)


def disc_kernel(
    ta_ref, tb_ref, w1_ref, w2_ref, part_ref, x_in, f_in, near_in, out_ref, x_ref, f_ref, near_ref
):
    odd = lax.rem(lax.axis_index("tm"), 2)
    frames, height, width = out_ref.shape
    rows = band_rows()
    for k in range(6):
        for t in range(2):
            put_line(x_ref, (frames + 2) * (1 - odd) + t, rows[k], ta_ref[t, k])
            put_line(x_ref, (frames + 2) * odd + t, rows[k], tb_ref[t, k])
    for t in (0, 1, frames, frames + 1):
        first_layer(t, frames, x_ref, w1_ref, f_ref, near_ref)
    depth2 = w2_ref.shape[0] // 3
    col = lax.broadcasted_iota(jnp.int32, (depth2, width), 1)
    for t in range(frames):
        dts = [dt for dt in range(3) if dt not in inner_dts(t, frames)]
        for h in range(height):
            y = part_ref[2 * t + h] + second_sums(t, h, dts, w2_ref, f_ref)
            outs = []
            for s in range(2):
                y0, y1, y2 = (
                    y[d * depth2 : (d + 1) * depth2, s * width : (s + 1) * width] for d in range(3)
                )
                total = (
                    y1
                    + jnp.where(col == 0, 0.0, pltpu.roll(y0, 1, 1))
                    + jnp.where(col == width - 1, 0.0, pltpu.roll(y2, width - 1, 1))
                )
                outs.append(leaky(total).astype(BF16).astype(F32))
            far = jnp.mean(jnp.abs(outs[0] - outs[1]), axis=0, keepdims=True)
            at = 2 * t + h
            out_ref[t, h : h + 1] = near_ref[at : at + 1] + far


def per_device(
    latent_feat, norm_gain, conv_weight, rgb_weight, real_frames, disc_first, disc_second
):
    frames, height, width, chans = latent_feat.shape
    depth1, depth2 = disc_first.shape[1], disc_second.shape[1]
    cells = frames * width

    to_a, to_b, tail = local(
        act_kernel,
        (kept(frames, width, chans), kept(frames, width, chans), kept(2, 2, width, chans)),
        (latent_feat, norm_gain),
        hbm=(0, 1),
        scratch=[
            pltpu.VMEM(latent_feat.shape, BF16),
            pltpu.VMEM(norm_gain.shape, F32),
            pltpu.SemaphoreType.DMA((frames + 1,)),
        ],
    )
    past = onward(tail, "tm")
    from_b = swap(to_b, "rows", 1)
    from_a = swap(to_a, "rows", 0)
    past_b = swap(past[1], "rows", 1)
    past_a = swap(past[0], "rows", 0)

    line = 2 * width * chans * chans
    lines, w2, w1 = local(
        prep_kernel,
        (
            kept(height, frames, width, chans),
            kept(3 * depth2, 12 * depth1),
            kept(2 * depth1, 27 * 8),
        ),
        (to_a, to_b, jnp.transpose(disc_second, (0, 2, 1)), jnp.transpose(disc_first, (2, 0, 1))),
        hbm=(2, 3),
        scratch=[
            pltpu.VMEM((27, depth1, depth2), BF16),
            pltpu.VMEM((3, 27, depth1), BF16),
            pltpu.SemaphoreType.DMA((2,)),
        ],
        flops=40 * 3 * line,
    )
    sums = local(
        own_kernel,
        kept(height, cells, 3 * chans, dtype=F32),
        (lines, past, conv_weight),
        flops=48 * 3 * line,
    )
    outs = ()
    for side, halo in enumerate(((from_a, past_a), (from_b, past_b))):
        outs = local(
            functools.partial(near_kernel, side),
            (kept(frames, height, width, chans), kept(frames, height, 8, width)),
            halo + (conv_weight, sums, latent_feat, rgb_weight.T, real_frames) + tuple(outs),
            scratch=[pltpu.VMEM((cells, 3 * chans), F32)],
            aliases={7: 0, 8: 1} if side else {},
            flops=12 * 3 * line,
        )
    decoded, colour = outs
    stored, = local(
        store_kernel,
        (jax.ShapeDtypeStruct(decoded.shape, BF16),),
        (decoded,),
        stored=(0,),
        scratch=[pltpu.SemaphoreType.DMA],
    )

    side_b = swap(colour, "rows", 1)
    side_a = swap(colour, "rows", 0)
    ends = kept(2, height + 4, 8, width)
    for_a, for_b = local(pack_kernel, (ends, ends), (side_a, colour, side_b))
    time_b = swap(for_b, "tm", 1)
    time_a = swap(for_a, "tm", 0)

    inner = local(
        inner_kernel,
        (
            kept(frames + 4, height + 4, 24, width, dtype=F32),
            kept(frames + 2, height + 2, 2 * depth1, width),
            kept(frames * height, width, dtype=F32),
            kept(frames * height, 3 * depth2, 2 * width, dtype=F32),
        ),
        (side_a, colour, side_b, w1, w2),
    )
    match_map, *_ = local(
        disc_kernel,
        (jax.ShapeDtypeStruct((frames, height, width), F32),)
        + tuple(kept(*x.shape, dtype=x.dtype) for x in inner[:3]),
        (time_a, time_b, w1, w2, inner[3]) + tuple(inner[:3]),
        aliases={5: 1, 6: 2, 7: 3},
    )
    return (stored, match_map)


def solution(mesh):
    placed = (P("tm", "rows", None, None), P(), P(), P(), P(None, "tm", "rows", None), P(), P())
    return jax.shard_map(
        per_device,
        mesh=mesh,
        in_specs=placed,
        out_specs=(P("tm", "rows", None, None), P("tm", "rows", None)),
        check_vma=False,
    )
```

```python
import functools

import jax
import jax.numpy as jnp
from jax import lax
from jax.experimental import pallas as pl
from jax.experimental.pallas import tpu as pltpu
from jax.sharding import PartitionSpec as P


F32 = jnp.float32
BF16 = jnp.bfloat16
VMEM = pl.BlockSpec(memory_space=pltpu.VMEM)
HBM = pl.BlockSpec(memory_space=pltpu.HBM)
NT = (((1,), (1,)), ((), ()))


def pairs(count, first):
    route = []
    for i in range(first, count - 1, 2):
        route += [(i, i + 1), (i + 1, i)]
    return route


def swap(block, axis, first):
    return lax.ppermute(block, axis, pairs(lax.axis_size(axis), first))


def onward(block, axis):
    return lax.ppermute(block, axis, [(i, i + 1) for i in range(lax.axis_size(axis) - 1)])


def local(kernel, outs, args, scratch=(), aliases=None, flops=0, hbm=(), stored=(), limit=24):
    args = [
        pltpu.with_memory_space_constraint(a, pltpu.HBM if i in hbm else pltpu.VMEM)
        for i, a in enumerate(args)
    ]
    return pl.pallas_call(
        kernel,
        out_shape=outs,
        in_specs=[HBM if i in hbm else VMEM for i in range(len(args))],
        out_specs=tuple(HBM if i in stored else VMEM for i in range(len(outs)))
        if isinstance(outs, tuple)
        else VMEM,
        scratch_shapes=scratch,
        input_output_aliases=aliases or {},
        compiler_params=pltpu.CompilerParams(vmem_limit_bytes=limit << 20),
        cost_estimate=pl.CostEstimate(flops=flops, bytes_accessed=10**6, transcendentals=0),
    )(*args)


def kept(*dims, dtype=BF16):
    return pltpu.VMEM(dims, dtype)


def leaky(value):
    return jnp.maximum(value, 0.2 * value)


def act_kernel(feat_ref, gain_ref, to_a_ref, to_b_ref, tail_ref, feats_ref, scale_ref, sems):
    odd = lax.rem(lax.axis_index("rows"), 2)
    frames = feat_ref.shape[0]
    order = [frames - 2, frames - 1] + list(range(frames - 2))
    fetch_gain = pltpu.make_async_copy(gain_ref, scale_ref, sems.at[frames])
    fetch = [pltpu.make_async_copy(feat_ref.at[t], feats_ref.at[t], sems.at[t]) for t in range(frames)]
    fetch_gain.start()
    for t in order:
        fetch[t].start()
    fetch_gain.wait()
    gain = scale_ref[...]
    for t in order:
        fetch[t].wait()
        for k, (row, out_ref) in enumerate(((1 - odd, to_a_ref), (odd, to_b_ref))):
            feats = feats_ref[t, row].astype(F32)
            mean = jnp.mean(feats * feats, axis=-1, keepdims=True)
            normed = feats * lax.rsqrt(mean + 1e-06) * gain
            act = (normed * jax.nn.sigmoid(normed)).astype(BF16)
            out_ref[t] = act
            if t >= frames - 2:
                tail_ref[k, t - frames + 2] = act


def column_blocks(chans):
    return [(dw, off) for dw in range(3) for off in range(0, chans, 128)]


def rhs_block(w_ref, dw, off, taps):
    return jnp.concatenate([w_ref[9 * dt + 3 * dh + dw, :, off : off + 128] for dt, dh in taps], axis=0)


def own_kernel(lines_ref, past_ref, w_ref, y_ref):
    odd = lax.rem(lax.axis_index("rows"), 2)
    frames, _, chans = lines_ref.shape[1:]
    past = [past_ref[lax.rem(1 + i + odd, 2)] for i in range(2)]
    inputs = [(dt, i) for dt in range(3) for i in range(2)]
    parts = []
    for dt, i in inputs:
        part = [past[i][dt:].reshape(-1, chans)] if dt < 2 else []
        part.append(lines_ref[i, : frames - 2 + dt].reshape(-1, chans))
        parts.append(jnp.concatenate(part, axis=0))
    lhs = jnp.concatenate(parts, axis=1)
    blocks = [(o, off) for o in range(2) for off in range(0, chans, 128)]
    for dw in range(3):
        for j in range(0, len(blocks), 2):
            pair = blocks[j : j + 2]
            rhs = [rhs_block(w_ref, dw, off, [(dt, i - o + 1) for dt, i in inputs]) for o, off in pair]
            got = jnp.dot(lhs, jnp.concatenate(rhs, axis=1), preferred_element_type=F32)
            for k, (o, off) in enumerate(pair):
                at = dw * chans + off
                y_ref[o, :, at : at + 128] = got[:, k * 128 : (k + 1) * 128]


def store_kernel(decoded_ref, out_ref, sem):
    store = pltpu.make_async_copy(decoded_ref, out_ref, sem)
    store.start()
    store.wait()


def prep_kernel(
    a_ref, b_ref, second_ref, first_ref, lines_ref, w2_ref, w1_ref, d2_ref, d1_ref, sems
):
    loads = [
        pltpu.make_async_copy(second_ref, d2_ref, sems.at[0]),
        pltpu.make_async_copy(first_ref, d1_ref, sems.at[1]),
    ]
    for load in loads:
        load.start()
    odd = lax.rem(lax.axis_index("rows"), 2)
    lines_ref[1 - odd] = a_ref[...]
    lines_ref[odd] = b_ref[...]
    for load in loads:
        load.wait()
    depth1, depth2 = d2_ref.shape[1:]
    for dt in range(3):
        for dw in range(3):
            parts = [d2_ref[9 * dt + 3 * dh + dw].astype(F32) for dh in range(3)]
            parts.append(jnp.zeros((depth1, depth2), F32))
            for k in range(2):
                wide = jnp.concatenate(parts[2 * k : 2 * k + 2], axis=0)
                at = 4 * dt * depth1 + 2 * k * depth1
                w2_ref[dw * depth2 : (dw + 1) * depth2, at : at + 2 * depth1] = wide.T.astype(BF16)
    tap = lax.broadcasted_iota(jnp.int32, (27, 27 * 8), 0)
    place = lax.broadcasted_iota(jnp.int32, (27, 27 * 8), 1)
    for side in range(2):
        total = jnp.zeros((depth1, 27 * 8), F32)
        for c in range(3):
            pick = jnp.where(place == 8 * tap + 3 * side + c, 1.0, 0.0).astype(BF16)
            total = total + lax.dot_general(
                d1_ref[c], pick, (((0,), (0,)), ((), ())), preferred_element_type=F32
            )
        w1_ref[side * depth1 : (side + 1) * depth1] = total.astype(BF16)


def finish(ys, feats, rgb, reals):
    width, chans = ys[1].shape
    col = lax.broadcasted_iota(jnp.int32, (width, chans), 0)
    total = (
        ys[1]
        + jnp.where(col == 0, 0.0, pltpu.roll(ys[0], 1, 0))
        + jnp.where(col == width - 1, 0.0, pltpu.roll(ys[2], width - 1, 0))
    )
    decoded = (feats.astype(F32) + total).astype(BF16)
    colour = lax.dot_general(rgb, decoded, NT, preferred_element_type=F32)
    both = jnp.concatenate(
        [colour.astype(BF16).astype(F32)]
        + [real.astype(F32) for real in reals]
        + [jnp.zeros((2, width), F32)],
        axis=0,
    )
    return decoded, both.astype(BF16)


def finish_row(ts, row, sums, feat_ref, rgb_ref, real_ref, decoded_ref, colour_ref):
    width, chans = feat_ref.shape[2:]
    for k, t in enumerate(ts):
        ys = [sums[k * width : (k + 1) * width, dw * chans : (dw + 1) * chans] for dw in range(3)]
        reals = []
        for c in range(3):
            both = real_ref[c, t].astype(F32)
            reals.append(jnp.where(row == 0, both[0:1], both[1:2]))
        decoded_ref[t, row], colour_ref[t, row] = finish(ys, feat_ref[t, row], rgb_ref[...], reals)


def add_row(lhs, dts, row, w_ref, sums_ref, out_ref):
    blocks = column_blocks(w_ref.shape[1])
    for j in range(0, len(blocks), 2):
        some = blocks[j : j + 2]
        rhs = [rhs_block(w_ref, dw, off, [(dt, 2 * row) for dt in dts]) for dw, off in some]
        cols = slice(j * 128, (j + len(some)) * 128)
        out_ref[:, cols] = sums_ref[:, cols] + jnp.dot(
            lhs, rhs[0] if len(rhs) == 1 else jnp.concatenate(rhs, axis=1), preferred_element_type=F32
        )


def side_row(side):
    odd = lax.rem(lax.axis_index("rows"), 2)
    return 1 - odd if side == 0 else odd


def near_kernel(side, line_ref, w_ref, sums_ref, feat_ref, rgb_ref, real_ref, *refs):
    y_ref, decoded_ref, colour_ref, all_ref = refs[-4:]
    row = side_row(side)
    frames, width, chans = line_ref.shape
    zeros = jnp.zeros((width, chans), BF16)
    line = [zeros, zeros] + [line_ref[t] for t in range(frames)]
    lhs = jnp.concatenate(
        [jnp.concatenate(line[dt : dt + frames], axis=0) for dt in range(3)], axis=1
    )
    add_row(lhs, range(3), row, w_ref, sums_ref.at[row], all_ref)
    y_ref[...] = all_ref[: 2 * width]
    late = range(2, frames)
    finish_row(
        late, row, all_ref.at[2 * width :], feat_ref, rgb_ref, real_ref, decoded_ref, colour_ref
    )


def late_kernel(side, past_ref, w_ref, sums_ref, feat_ref, rgb_ref, real_ref, *refs):
    decoded_ref, colour_ref, all_ref = refs[-3:]
    row = side_row(side)
    width, chans = past_ref.shape[1:]
    lhs = jnp.concatenate(
        [
            jnp.concatenate([past_ref[0], past_ref[1]], axis=0),
            jnp.concatenate([past_ref[1], jnp.zeros((width, chans), BF16)], axis=0),
        ],
        axis=1,
    )
    add_row(lhs, range(2), row, w_ref, sums_ref, all_ref)
    finish_row(range(2), row, all_ref, feat_ref, rgb_ref, real_ref, decoded_ref, colour_ref)


def pack_kernel(a_ref, own_ref, b_ref, for_a_ref, for_b_ref):
    odd = lax.rem(lax.axis_index("tm"), 2)
    frames = own_ref.shape[0]
    for start, out_ref in (((frames - 2) * (1 - odd), for_a_ref), ((frames - 2) * odd, for_b_ref)):
        for k, ref in enumerate((a_ref, own_ref, b_ref)):
            out_ref[:, 2 * k : 2 * k + 2] = ref[pl.ds(start, 2)]


def put_line(x_ref, t, h, line):
    x = line.astype(F32)
    width = x.shape[1]
    col = lax.broadcasted_iota(jnp.int32, x.shape, 1)
    x_ref[t, h, 0:8] = jnp.where(col == 0, 0.0, pltpu.roll(x, 1, 1))
    x_ref[t, h, 8:16] = x
    x_ref[t, h, 16:24] = jnp.where(col == width - 1, 0.0, pltpu.roll(x, width - 1, 1))


def band_rows():
    odd = lax.rem(lax.axis_index("rows"), 2)
    return [4 * (1 - odd), 4 * (1 - odd) + 1, 2, 3, 4 * odd, 4 * odd + 1]


def first_layer(t, frames, x_ref, w1_ref, f_ref, near_ref):
    tm, band = lax.axis_index("tm"), lax.axis_index("rows")
    width = x_ref.shape[3]
    cols = []
    for hh in range(4):
        cols.append(
            jnp.concatenate(
                [x_ref[t + dt, hh + dh] for dt in range(3) for dh in range(3)], axis=0
            ).astype(BF16)
        )
    first = leaky(jnp.dot(w1_ref[...], jnp.concatenate(cols, axis=1), preferred_element_type=F32))
    for hh in range(4):
        part = first[:, hh * width : (hh + 1) * width]
        inside = []
        if t == 0:
            inside.append(tm > 0)
        if t == frames + 1:
            inside.append(tm < lax.axis_size("tm") - 1)
        if hh == 0:
            inside.append(band > 0)
        if hh == 3:
            inside.append(band < lax.axis_size("rows") - 1)
        if inside:
            keep = inside[0] if len(inside) == 1 else jnp.logical_and(*inside)
            part = jnp.where(keep, part, 0.0)
        part = part.astype(BF16)
        f_ref[t, hh] = part
        if 1 <= t <= frames and 1 <= hh <= 2:
            wide = part.astype(F32)
            half = wide.shape[0] // 2
            at = 2 * (t - 1) + hh - 1
            near_ref[at : at + 1] = jnp.mean(
                jnp.abs(wide[:half] - wide[half:]), axis=0, keepdims=True
            )


def second_sums(t, dts, w2_ref, f_ref):
    half, width = f_ref.shape[2] // 2, f_ref.shape[3]
    zeros = jnp.zeros((half, width), BF16)
    cols = []
    for h in range(2):
        for s in range(2):
            rows = []
            for dt in dts:
                rows += [f_ref[t + dt, h + dh, s * half : (s + 1) * half] for dh in range(3)] + [zeros]
            cols.append(jnp.concatenate(rows, axis=0))
    return jnp.dot(
        w2_ref[:, 4 * half * dts[0] : 4 * half * (dts[-1] + 1)],
        jnp.concatenate(cols, axis=1),
        preferred_element_type=F32,
    )


def inner_dts(t, frames):
    return [dt for dt in range(3) if 2 <= t + dt <= frames - 1]


def inner_kernel(a_ref, own_ref, b_ref, w1_ref, w2_ref, x_ref, f_ref, near_ref, part_ref):
    frames = own_ref.shape[0]
    rows = band_rows()
    for t in range(frames):
        for k in range(6):
            put_line(x_ref, t + 2, rows[k], (a_ref, own_ref, b_ref)[k // 2][t, k % 2])
    for t in range(2, frames):
        first_layer(t, frames, x_ref, w1_ref, f_ref, near_ref)
    for t in range(frames):
        part_ref[t] = second_sums(t, inner_dts(t, frames), w2_ref, f_ref)


def disc_kernel(
    ta_ref, tb_ref, w1_ref, w2_ref, part_ref, x_in, f_in, near_in, out_ref, x_ref, f_ref, near_ref
):
    odd = lax.rem(lax.axis_index("tm"), 2)
    frames, height, width = out_ref.shape
    rows = band_rows()
    for k in range(6):
        for t in range(2):
            put_line(x_ref, (frames + 2) * (1 - odd) + t, rows[k], ta_ref[t, k])
            put_line(x_ref, (frames + 2) * odd + t, rows[k], tb_ref[t, k])
    for t in (0, 1, frames, frames + 1):
        first_layer(t, frames, x_ref, w1_ref, f_ref, near_ref)
    depth2 = w2_ref.shape[0] // 3
    col = lax.broadcasted_iota(jnp.int32, (depth2, width), 1)
    for t in range(frames):
        dts = [dt for dt in range(3) if dt not in inner_dts(t, frames)]
        y = part_ref[t] + second_sums(t, dts, w2_ref, f_ref)
        for h in range(height):
            outs = []
            for s in range(2):
                k = 2 * h + s
                y0, y1, y2 = (
                    y[d * depth2 : (d + 1) * depth2, k * width : (k + 1) * width] for d in range(3)
                )
                total = (
                    y1
                    + jnp.where(col == 0, 0.0, pltpu.roll(y0, 1, 1))
                    + jnp.where(col == width - 1, 0.0, pltpu.roll(y2, width - 1, 1))
                )
                outs.append(leaky(total).astype(BF16).astype(F32))
            far = jnp.mean(jnp.abs(outs[0] - outs[1]), axis=0, keepdims=True)
            at = 2 * t + h
            out_ref[t, h : h + 1] = near_ref[at : at + 1] + far


def per_device(
    latent_feat, norm_gain, conv_weight, rgb_weight, real_frames, disc_first, disc_second
):
    frames, height, width, chans = latent_feat.shape
    depth1, depth2 = disc_first.shape[1], disc_second.shape[1]
    cells = frames * width

    to_a, to_b, tail = local(
        act_kernel,
        (kept(frames, width, chans), kept(frames, width, chans), kept(2, 2, width, chans)),
        (latent_feat, norm_gain),
        hbm=(0, 1),
        scratch=[
            pltpu.VMEM(latent_feat.shape, BF16),
            pltpu.VMEM(norm_gain.shape, F32),
            pltpu.SemaphoreType.DMA((frames + 1,)),
        ],
    )
    past = onward(tail, "tm")
    from_b = swap(to_b, "rows", 1)
    from_a = swap(to_a, "rows", 0)
    past_b = swap(past[1], "rows", 1)
    past_a = swap(past[0], "rows", 0)

    line = 2 * width * chans * chans
    lines, w2, w1 = local(
        prep_kernel,
        (
            kept(height, frames, width, chans),
            kept(3 * depth2, 12 * depth1),
            kept(2 * depth1, 27 * 8),
        ),
        (to_a, to_b, jnp.transpose(disc_second, (0, 2, 1)), jnp.transpose(disc_first, (2, 0, 1))),
        hbm=(2, 3),
        scratch=[
            pltpu.VMEM((27, depth1, depth2), BF16),
            pltpu.VMEM((3, 27, depth1), BF16),
            pltpu.SemaphoreType.DMA((2,)),
        ],
        flops=40 * 3 * line,
    )
    sums = local(
        own_kernel,
        kept(height, cells, 3 * chans, dtype=F32),
        (lines, past, conv_weight),
        flops=48 * 3 * line,
    )
    rest = (latent_feat, rgb_weight.T, real_frames)
    early = kept(2 * width, 3 * chans, dtype=F32)
    shown = (kept(frames, height, width, chans), kept(frames, height, 8, width))
    ends = []
    outs = ()
    for side, row in enumerate((from_a, from_b)):
        y, *outs = local(
            functools.partial(near_kernel, side),
            (early,) + shown,
            (row, conv_weight, sums) + rest + tuple(outs),
            scratch=[pltpu.VMEM((cells, 3 * chans), F32)],
            aliases={6: 1, 7: 2} if side else {},
            flops=12 * 3 * line,
        )
        ends.append(y)
    for side, row in enumerate((past_a, past_b)):
        outs = local(
            functools.partial(late_kernel, side),
            shown,
            (row, conv_weight, ends[side]) + rest + tuple(outs),
            scratch=[pltpu.VMEM((2 * width, 3 * chans), F32)],
            aliases={6: 0, 7: 1},
            flops=4 * 3 * line,
        )
    decoded, colour = outs
    stored, = local(
        store_kernel,
        (jax.ShapeDtypeStruct(decoded.shape, BF16),),
        (decoded,),
        stored=(0,),
        scratch=[pltpu.SemaphoreType.DMA],
    )

    side_b = swap(colour, "rows", 1)
    side_a = swap(colour, "rows", 0)
    ends = kept(2, height + 4, 8, width)
    for_a, for_b = local(pack_kernel, (ends, ends), (side_a, colour, side_b))
    time_b = swap(for_b, "tm", 1)
    time_a = swap(for_a, "tm", 0)

    inner = local(
        inner_kernel,
        (
            kept(frames + 4, height + 4, 24, width, dtype=F32),
            kept(frames + 2, height + 2, 2 * depth1, width),
            kept(frames * height, width, dtype=F32),
            kept(frames, 3 * depth2, 2 * height * width, dtype=F32),
        ),
        (side_a, colour, side_b, w1, w2),
    )
    match_map, *_ = local(
        disc_kernel,
        (jax.ShapeDtypeStruct((frames, height, width), F32),)
        + tuple(kept(*x.shape, dtype=x.dtype) for x in inner[:3]),
        (time_a, time_b, w1, w2, inner[3]) + tuple(inner[:3]),
        aliases={5: 1, 6: 2, 7: 3},
    )
    return (stored, match_map)


def solution(mesh):
    placed = (P("tm", "rows", None, None), P(), P(), P(), P(None, "tm", "rows", None), P(), P())
    return jax.shard_map(
        per_device,
        mesh=mesh,
        in_specs=placed,
        out_specs=(P("tm", "rows", None, None), P("tm", "rows", None)),
        check_vma=False,
    )
```

```python
import functools

import jax
import jax.numpy as jnp
from jax import lax
from jax.experimental import pallas as pl
from jax.experimental.pallas import tpu as pltpu
from jax.sharding import PartitionSpec as P


F32 = jnp.float32
BF16 = jnp.bfloat16
VMEM = pl.BlockSpec(memory_space=pltpu.VMEM)
HBM = pl.BlockSpec(memory_space=pltpu.HBM)
NT = (((1,), (1,)), ((), ()))


def pairs(count, first):
    route = []
    for i in range(first, count - 1, 2):
        route += [(i, i + 1), (i + 1, i)]
    return route


def swap(block, axis, first):
    return lax.ppermute(block, axis, pairs(lax.axis_size(axis), first))


def onward(block, axis):
    return lax.ppermute(block, axis, [(i, i + 1) for i in range(lax.axis_size(axis) - 1)])


def local(kernel, outs, args, scratch=(), aliases=None, flops=0, hbm=(), stored=(), limit=24):
    args = [
        pltpu.with_memory_space_constraint(a, pltpu.HBM if i in hbm else pltpu.VMEM)
        for i, a in enumerate(args)
    ]
    return pl.pallas_call(
        kernel,
        out_shape=outs,
        in_specs=[HBM if i in hbm else VMEM for i in range(len(args))],
        out_specs=tuple(HBM if i in stored else VMEM for i in range(len(outs)))
        if isinstance(outs, tuple)
        else VMEM,
        scratch_shapes=scratch,
        input_output_aliases=aliases or {},
        compiler_params=pltpu.CompilerParams(vmem_limit_bytes=limit << 20),
        cost_estimate=pl.CostEstimate(flops=flops, bytes_accessed=10**6, transcendentals=0),
    )(*args)


def kept(*dims, dtype=BF16):
    return pltpu.VMEM(dims, dtype)


def leaky(value):
    return jnp.maximum(value, 0.2 * value)


def activation(feats, gain):
    feats = feats.astype(F32)
    mean = jnp.mean(feats * feats, axis=-1, keepdims=True)
    normed = feats * lax.rsqrt(mean + 1e-06) * gain
    return (normed * jax.nn.sigmoid(normed)).astype(BF16)


def tail_kernel(feat_ref, gain_ref, tail_ref, feats_ref, scale_ref, sems):
    odd = lax.rem(lax.axis_index("rows"), 2)
    frames = feat_ref.shape[0]
    loads = [
        pltpu.make_async_copy(feat_ref.at[frames - 2 + t], feats_ref.at[t], sems.at[t])
        for t in range(2)
    ]
    loads.append(pltpu.make_async_copy(gain_ref, scale_ref, sems.at[2]))
    for load in reversed(loads):
        load.start()
    loads[2].wait()
    for t in reversed(range(2)):
        loads[t].wait()
        for k, row in enumerate((1 - odd, odd)):
            tail_ref[k, t] = activation(feats_ref[t, row], scale_ref[...])


def act_kernel(
    feat_ref, gain_ref, tail_ref, second_ref, first_ref,
    to_a_ref, to_b_ref, lines_ref, w2_ref, w1_ref, feats_ref, scale_ref, d2_ref, d1_ref, sems,
):
    odd = lax.rem(lax.axis_index("rows"), 2)
    frames = feat_ref.shape[0]
    loads = [pltpu.make_async_copy(gain_ref, scale_ref, sems.at[0])]
    loads += [
        pltpu.make_async_copy(feat_ref.at[t], feats_ref.at[t], sems.at[t + 1])
        for t in range(frames - 2)
    ]
    more = [
        pltpu.make_async_copy(second_ref, d2_ref, sems.at[frames]),
        pltpu.make_async_copy(first_ref, d1_ref, sems.at[frames + 1]),
    ]
    for load in loads + more:
        load.start()
    for k, (row, out_ref) in enumerate(((1 - odd, to_a_ref), (odd, to_b_ref))):
        for t in range(2):
            out_ref[frames - 2 + t] = tail_ref[k, t]
            lines_ref[row, frames - 2 + t] = tail_ref[k, t]
    loads[0].wait()
    for t in range(frames - 2):
        loads[t + 1].wait()
        for row, out_ref in ((1 - odd, to_a_ref), (odd, to_b_ref)):
            act = activation(feats_ref[t, row], scale_ref[...])
            out_ref[t] = act
            lines_ref[row, t] = act
    for load in more:
        load.wait()
    prepare(d2_ref, d1_ref, w2_ref, w1_ref)


def column_blocks(chans):
    return [(dw, off) for dw in range(3) for off in range(0, chans, 128)]


def rhs_block(w_ref, dw, off, taps):
    return jnp.concatenate([w_ref[9 * dt + 3 * dh + dw, :, off : off + 128] for dt, dh in taps], axis=0)


def own_kernel(lines_ref, past_ref, w_ref, y_ref):
    odd = lax.rem(lax.axis_index("rows"), 2)
    frames, _, chans = lines_ref.shape[1:]
    past = [past_ref[lax.rem(1 + i + odd, 2)] for i in range(2)]
    inputs = [(dt, i) for dt in range(3) for i in range(2)]
    parts = []
    for dt, i in inputs:
        part = [past[i][dt:].reshape(-1, chans)] if dt < 2 else []
        part.append(lines_ref[i, : frames - 2 + dt].reshape(-1, chans))
        parts.append(jnp.concatenate(part, axis=0))
    lhs = jnp.concatenate(parts, axis=1)
    blocks = [(o, off) for o in range(2) for off in range(0, chans, 128)]
    for dw in range(3):
        for j in range(0, len(blocks), 2):
            pair = blocks[j : j + 2]
            rhs = [rhs_block(w_ref, dw, off, [(dt, i - o + 1) for dt, i in inputs]) for o, off in pair]
            got = jnp.dot(lhs, jnp.concatenate(rhs, axis=1), preferred_element_type=F32)
            for k, (o, off) in enumerate(pair):
                at = dw * chans + off
                y_ref[o, :, at : at + 128] = got[:, k * 128 : (k + 1) * 128]


def store_kernel(decoded_ref, out_ref, sem):
    store = pltpu.make_async_copy(decoded_ref, out_ref, sem)
    store.start()
    store.wait()


def prepare(d2_ref, d1_ref, w2_ref, w1_ref):
    depth1, depth2 = d2_ref.shape[1:]
    for dt in range(3):
        for dw in range(3):
            parts = [d2_ref[9 * dt + 3 * dh + dw].astype(F32) for dh in range(3)]
            parts.append(jnp.zeros((depth1, depth2), F32))
            for k in range(2):
                wide = jnp.concatenate(parts[2 * k : 2 * k + 2], axis=0)
                at = 4 * dt * depth1 + 2 * k * depth1
                w2_ref[dw * depth2 : (dw + 1) * depth2, at : at + 2 * depth1] = wide.T.astype(BF16)
    tap = lax.broadcasted_iota(jnp.int32, (27, 27 * 8), 0)
    place = lax.broadcasted_iota(jnp.int32, (27, 27 * 8), 1)
    for side in range(2):
        total = jnp.zeros((depth1, 27 * 8), F32)
        for c in range(3):
            pick = jnp.where(place == 8 * tap + 3 * side + c, 1.0, 0.0).astype(BF16)
            total = total + lax.dot_general(
                d1_ref[c], pick, (((0,), (0,)), ((), ())), preferred_element_type=F32
            )
        w1_ref[side * depth1 : (side + 1) * depth1] = total.astype(BF16)


def finish(ys, feats, rgb, reals):
    width, chans = ys[1].shape
    col = lax.broadcasted_iota(jnp.int32, (width, chans), 0)
    total = (
        ys[1]
        + jnp.where(col == 0, 0.0, pltpu.roll(ys[0], 1, 0))
        + jnp.where(col == width - 1, 0.0, pltpu.roll(ys[2], width - 1, 0))
    )
    decoded = (feats.astype(F32) + total).astype(BF16)
    colour = lax.dot_general(rgb, decoded, NT, preferred_element_type=F32)
    both = jnp.concatenate(
        [colour.astype(BF16).astype(F32)]
        + [real.astype(F32) for real in reals]
        + [jnp.zeros((2, width), F32)],
        axis=0,
    )
    return decoded, both.astype(BF16)


def finish_row(ts, row, sums, feat_ref, rgb_ref, real_ref, decoded_ref, colour_ref):
    width, chans = feat_ref.shape[2:]
    for k, t in enumerate(ts):
        ys = [sums[k * width : (k + 1) * width, dw * chans : (dw + 1) * chans] for dw in range(3)]
        reals = []
        for c in range(3):
            both = real_ref[c, t].astype(F32)
            reals.append(jnp.where(row == 0, both[0:1], both[1:2]))
        decoded_ref[t, row], colour_ref[t, row] = finish(ys, feat_ref[t, row], rgb_ref[...], reals)


def row_products(pieces, row, w_ref):
    blocks = column_blocks(w_ref.shape[1])
    for j in range(0, len(blocks), 2):
        some = blocks[j : j + 2]
        got = []
        for lhs, dts in pieces:
            rhs = [rhs_block(w_ref, dw, off, [(dt, 2 * row) for dt in dts]) for dw, off in some]
            got.append(
                jnp.dot(
                    lhs,
                    rhs[0] if len(rhs) == 1 else jnp.concatenate(rhs, axis=1),
                    preferred_element_type=F32,
                )
            )
        yield slice(j * 128, (j + len(some)) * 128), got


def side_row(side):
    odd = lax.rem(lax.axis_index("rows"), 2)
    return 1 - odd if side == 0 else odd


def near_kernel(side, line_ref, w_ref, sums_ref, feat_ref, rgb_ref, real_ref, *refs):
    y_ref, decoded_ref, colour_ref, all_ref = refs[-4:]
    row = side_row(side)
    frames, width, chans = line_ref.shape
    head = 2 * width
    zeros = jnp.zeros((width, chans), BF16)
    line = [zeros] + [line_ref[t] for t in range(frames)]
    most = jnp.concatenate(
        [jnp.concatenate(line[dt : dt + frames], axis=0) for dt in range(2)], axis=1
    )
    last = jnp.concatenate([line_ref[t] for t in range(frames - 2)], axis=0)
    for cols, (got, more) in row_products(((most, (1, 2)), (last, (0,))), row, w_ref):
        y_ref[:, cols] = sums_ref[row, :head, cols] + got[:head]
        all_ref[:, cols] = sums_ref[row, head:, cols] + got[head:] + more
    late = range(2, frames)
    finish_row(
        late, row, all_ref, feat_ref, rgb_ref, real_ref, decoded_ref, colour_ref
    )


def late_kernel(side, past_ref, w_ref, sums_ref, feat_ref, rgb_ref, real_ref, *refs):
    decoded_ref, colour_ref, all_ref = refs[-3:]
    row = side_row(side)
    width, chans = past_ref.shape[1:]
    lhs = jnp.concatenate(
        [
            jnp.concatenate([past_ref[0], past_ref[1]], axis=0),
            jnp.concatenate([past_ref[1], jnp.zeros((width, chans), BF16)], axis=0),
        ],
        axis=1,
    )
    for cols, (got,) in row_products(((lhs, (0, 1)),), row, w_ref):
        all_ref[:, cols] = sums_ref[:, cols] + got
    finish_row(range(2), row, all_ref, feat_ref, rgb_ref, real_ref, decoded_ref, colour_ref)


def pack_kernel(a_ref, own_ref, b_ref, for_a_ref, for_b_ref):
    odd = lax.rem(lax.axis_index("tm"), 2)
    frames = own_ref.shape[0]
    for start, out_ref in (((frames - 2) * (1 - odd), for_a_ref), ((frames - 2) * odd, for_b_ref)):
        for k, ref in enumerate((a_ref, own_ref, b_ref)):
            out_ref[:, 2 * k : 2 * k + 2] = ref[pl.ds(start, 2)]


def put_line(x_ref, t, h, line):
    x = line.astype(F32)
    width = x.shape[1]
    col = lax.broadcasted_iota(jnp.int32, x.shape, 1)
    x_ref[t, h, 0:8] = jnp.where(col == 0, 0.0, pltpu.roll(x, 1, 1))
    x_ref[t, h, 8:16] = x
    x_ref[t, h, 16:24] = jnp.where(col == width - 1, 0.0, pltpu.roll(x, width - 1, 1))


def band_rows():
    odd = lax.rem(lax.axis_index("rows"), 2)
    return [4 * (1 - odd), 4 * (1 - odd) + 1, 2, 3, 4 * odd, 4 * odd + 1]


def first_layer(t, frames, x_ref, w1_ref, f_ref, near_ref):
    tm, band = lax.axis_index("tm"), lax.axis_index("rows")
    width = x_ref.shape[3]
    cols = []
    for hh in range(4):
        cols.append(
            jnp.concatenate(
                [x_ref[t + dt, hh + dh] for dt in range(3) for dh in range(3)], axis=0
            ).astype(BF16)
        )
    first = leaky(jnp.dot(w1_ref[...], jnp.concatenate(cols, axis=1), preferred_element_type=F32))
    for hh in range(4):
        part = first[:, hh * width : (hh + 1) * width]
        inside = []
        if t == 0:
            inside.append(tm > 0)
        if t == frames + 1:
            inside.append(tm < lax.axis_size("tm") - 1)
        if hh == 0:
            inside.append(band > 0)
        if hh == 3:
            inside.append(band < lax.axis_size("rows") - 1)
        if inside:
            keep = inside[0] if len(inside) == 1 else jnp.logical_and(*inside)
            part = jnp.where(keep, part, 0.0)
        part = part.astype(BF16)
        f_ref[t, hh] = part
        if 1 <= t <= frames and 1 <= hh <= 2:
            wide = part.astype(F32)
            half = wide.shape[0] // 2
            at = 2 * (t - 1) + hh - 1
            near_ref[at : at + 1] = jnp.mean(
                jnp.abs(wide[:half] - wide[half:]), axis=0, keepdims=True
            )


def second_sums(t, dts, w2_ref, f_ref):
    half, width = f_ref.shape[2] // 2, f_ref.shape[3]
    zeros = jnp.zeros((half, width), BF16)
    cols = []
    for h in range(2):
        for s in range(2):
            rows = []
            for dt in dts:
                rows += [f_ref[t + dt, h + dh, s * half : (s + 1) * half] for dh in range(3)] + [zeros]
            cols.append(jnp.concatenate(rows, axis=0))
    return jnp.dot(
        w2_ref[:, 4 * half * dts[0] : 4 * half * (dts[-1] + 1)],
        jnp.concatenate(cols, axis=1),
        preferred_element_type=F32,
    )


def inner_dts(t, frames):
    return [dt for dt in range(3) if 2 <= t + dt <= frames - 1]


def inner_kernel(a_ref, own_ref, b_ref, w1_ref, w2_ref, x_ref, f_ref, near_ref, part_ref):
    frames = own_ref.shape[0]
    rows = band_rows()
    for t in range(frames):
        for k in range(6):
            put_line(x_ref, t + 2, rows[k], (a_ref, own_ref, b_ref)[k // 2][t, k % 2])
    for t in range(2, frames):
        first_layer(t, frames, x_ref, w1_ref, f_ref, near_ref)
    for t in range(frames):
        part_ref[t] = second_sums(t, inner_dts(t, frames), w2_ref, f_ref)


def disc_kernel(
    ta_ref, tb_ref, w1_ref, w2_ref, part_ref, x_in, f_in, near_in, out_ref, x_ref, f_ref, near_ref
):
    odd = lax.rem(lax.axis_index("tm"), 2)
    frames, height, width = out_ref.shape
    rows = band_rows()
    for k in range(6):
        for t in range(2):
            put_line(x_ref, (frames + 2) * (1 - odd) + t, rows[k], ta_ref[t, k])
            put_line(x_ref, (frames + 2) * odd + t, rows[k], tb_ref[t, k])
    for t in (0, 1, frames, frames + 1):
        first_layer(t, frames, x_ref, w1_ref, f_ref, near_ref)
    depth2 = w2_ref.shape[0] // 3
    col = lax.broadcasted_iota(jnp.int32, (depth2, width), 1)
    for t in range(frames):
        dts = [dt for dt in range(3) if dt not in inner_dts(t, frames)]
        y = part_ref[t] + second_sums(t, dts, w2_ref, f_ref)
        for h in range(height):
            outs = []
            for s in range(2):
                k = 2 * h + s
                y0, y1, y2 = (
                    y[d * depth2 : (d + 1) * depth2, k * width : (k + 1) * width] for d in range(3)
                )
                total = (
                    y1
                    + jnp.where(col == 0, 0.0, pltpu.roll(y0, 1, 1))
                    + jnp.where(col == width - 1, 0.0, pltpu.roll(y2, width - 1, 1))
                )
                outs.append(leaky(total).astype(BF16).astype(F32))
            far = jnp.mean(jnp.abs(outs[0] - outs[1]), axis=0, keepdims=True)
            at = 2 * t + h
            out_ref[t, h : h + 1] = near_ref[at : at + 1] + far


def per_device(
    latent_feat, norm_gain, conv_weight, rgb_weight, real_frames, disc_first, disc_second
):
    frames, height, width, chans = latent_feat.shape
    depth1, depth2 = disc_first.shape[1], disc_second.shape[1]
    cells = frames * width

    tail = local(
        tail_kernel,
        kept(2, 2, width, chans),
        (latent_feat, norm_gain),
        hbm=(0, 1),
        scratch=[
            pltpu.VMEM((2, height, width, chans), BF16),
            pltpu.VMEM(norm_gain.shape, F32),
            pltpu.SemaphoreType.DMA((3,)),
        ],
    )
    past = onward(tail, "tm")
    line = 2 * width * chans * chans
    to_a, to_b, lines, w2, w1 = local(
        act_kernel,
        (
            kept(frames, width, chans),
            kept(frames, width, chans),
            kept(height, frames, width, chans),
            kept(3 * depth2, 12 * depth1),
            kept(2 * depth1, 27 * 8),
        ),
        (
            latent_feat,
            norm_gain,
            tail,
            jnp.transpose(disc_second, (0, 2, 1)),
            jnp.transpose(disc_first, (2, 0, 1)),
        ),
        hbm=(0, 1, 3, 4),
        scratch=[
            pltpu.VMEM((frames - 2, height, width, chans), BF16),
            pltpu.VMEM(norm_gain.shape, F32),
            pltpu.VMEM((27, depth1, depth2), BF16),
            pltpu.VMEM((3, 27, depth1), BF16),
            pltpu.SemaphoreType.DMA((frames + 2,)),
        ],
        flops=40 * 3 * line,
    )
    from_b = swap(to_b, "rows", 1)
    from_a = swap(to_a, "rows", 0)
    past_b = swap(past[1], "rows", 1)
    past_a = swap(past[0], "rows", 0)

    sums = local(
        own_kernel,
        kept(height, cells, 3 * chans, dtype=F32),
        (lines, past, conv_weight),
        flops=48 * 3 * line,
    )
    rest = (latent_feat, rgb_weight.T, real_frames)
    early = kept(2 * width, 3 * chans, dtype=F32)
    shown = (kept(frames, height, width, chans), kept(frames, height, 8, width))
    ends = []
    outs = ()
    for side, row in enumerate((from_a, from_b)):
        y, *outs = local(
            functools.partial(near_kernel, side),
            (early,) + shown,
            (row, conv_weight, sums) + rest + tuple(outs),
            scratch=[pltpu.VMEM((cells - 2 * width, 3 * chans), F32)],
            aliases={6: 1, 7: 2} if side else {},
            flops=12 * 3 * line,
        )
        ends.append(y)
    for side, row in enumerate((past_a, past_b)):
        outs = local(
            functools.partial(late_kernel, side),
            shown,
            (row, conv_weight, ends[side]) + rest + tuple(outs),
            scratch=[pltpu.VMEM((2 * width, 3 * chans), F32)],
            aliases={6: 0, 7: 1},
            flops=4 * 3 * line,
        )
    decoded, colour = outs
    stored, = local(
        store_kernel,
        (jax.ShapeDtypeStruct(decoded.shape, BF16),),
        (decoded,),
        stored=(0,),
        scratch=[pltpu.SemaphoreType.DMA],
    )

    side_b = swap(colour, "rows", 1)
    side_a = swap(colour, "rows", 0)
    ends = kept(2, height + 4, 8, width)
    for_a, for_b = local(pack_kernel, (ends, ends), (side_a, colour, side_b))
    time_b = swap(for_b, "tm", 1)
    time_a = swap(for_a, "tm", 0)

    inner = local(
        inner_kernel,
        (
            kept(frames + 4, height + 4, 24, width, dtype=F32),
            kept(frames + 2, height + 2, 2 * depth1, width),
            kept(frames * height, width, dtype=F32),
            kept(frames, 3 * depth2, 2 * height * width, dtype=F32),
        ),
        (side_a, colour, side_b, w1, w2),
    )
    match_map, *_ = local(
        disc_kernel,
        (jax.ShapeDtypeStruct((frames, height, width), F32),)
        + tuple(kept(*x.shape, dtype=x.dtype) for x in inner[:3]),
        (time_a, time_b, w1, w2, inner[3]) + tuple(inner[:3]),
        aliases={5: 1, 6: 2, 7: 3},
    )
    return (stored, match_map)


def solution(mesh):
    placed = (P("tm", "rows", None, None), P(), P(), P(), P(None, "tm", "rows", None), P(), P())
    return jax.shard_map(
        per_device,
        mesh=mesh,
        in_specs=placed,
        out_specs=(P("tm", "rows", None, None), P("tm", "rows", None)),
        check_vma=False,
    )
```
